128 devices in a mesh: depth: 4 (over x), panel: 32 (over y, z, core).
Axes of the slice: x: 4, y: 4, z: 4, core: 2. Of those that a mesh axis runs over, the one named last changes fastest.
Arguments:
- diag_blocks: float32 [4, 1024, 1024], P('depth', 'panel'), as said below
- coupling: float32 [4, 1024, 1024], P('depth', 'panel'), may hold values from -0.078125 to 0.078125
- sources: float32 [4, 1024, 256], P('depth', 'panel'), may hold values from -6 to 6
- requests: int32 [4, 128], P('depth', 'panel'), may hold values from 0 to 1023, as said below
Outputs:
- panels: float32 [4, 1024, 256], P('depth', 'panel')
- picked: float32 [4, 128, 256], P('depth', 'panel')
The draws below stay inside these ranges and needn't reach their ends.
Inputs may be any that keep to these rules, and one draw needn't show every extreme that they name: `requests`: row numbers within their block; both 0 and 1023 occur. `diag_blocks`: every diagonal block is exactly symmetric with a positive diagonal.
All inputs are finite; a program needn't handle non-finite values.
Results may differ from the reference program's by a relative error of at most 0.0001.
Values sent between devices are 32-bit elements; how exact they have to be, the bound alone decides.
No kernel may reach another device: no remote copies, remote signals or barrier semaphores. Data moves between devices by JAX's collectives and lax.ppermute only.
A program may use at most 64 MiB of HBM per device.

```python
import math
import jax
import jax.numpy as jnp
from jax import lax

B = 1024
Q = 256
R = 128
ITERS = 2
NB = 4


def draw_diag_blocks(key, part):
    key_off, key_diag = jax.random.split(key)
    raw_values = jax.random.normal(key_off, (NB, B, B), jnp.float32)
    symmetric = (raw_values + jnp.swapaxes(raw_values, 1, 2)) * (0.5 / math.sqrt(2.0 * B))
    diag_values = jax.random.uniform(key_diag, (NB, B), jnp.float32, 3.0, 5.0)
    identity = jnp.eye(B, dtype=jnp.float32)
    return symmetric * (1.0 - identity) + diag_values[:, :, None] * identity


def draw_requests(key, part):
    row_numbers = jax.random.randint(key, (NB, R), 0, B, jnp.int32)
    return row_numbers.at[0, 0].set(B - 1).at[NB - 1, R - 1].set(0)


def level_of(own_key, shape, pieces, least, largest):
    factor_of = 1.0
    for dim, blocks in pieces:
        draws = jax.random.uniform(jax.random.fold_in(jax.random.fold_in(own_key, 6), dim), (blocks,), jnp.float32, least / len(pieces), largest / len(pieces))
        factor_of = factor_of * jnp.repeat(jnp.exp(draws), shape[dim] // blocks).reshape((-1,) + (1,) * (len(shape) - 1 - dim))
    return factor_of


def centred(key, shape, deviation, most, shards=(), kind=jnp.bfloat16):
    drawn = deviation * jax.random.normal(key, shape, jnp.float32)
    if shards:
        drawn = drawn * level_of(key, shape, shards, -0.22, 0.18)
    return jnp.clip(drawn, -most, most).astype(kind)


def setup_inputs(seed: int = 0) -> dict:
    streams_of = jax.random.split(jax.random.key(seed), 5)
    diag_blocks = draw_diag_blocks(jax.random.fold_in(streams_of[4], 71), 0)
    coupling = centred(streams_of[1], (NB, B, B), (5 * B) ** -0.5, 0.078125, ((0, 4), (1, 32)), jnp.float32)
    sources = centred(streams_of[2], (NB, B, Q), 1.0, 6.0, ((0, 4), (1, 32)), jnp.float32)
    requests = draw_requests(jax.random.fold_in(streams_of[4], 71), 0)
    return dict(diag_blocks=diag_blocks, coupling=coupling, sources=sources, requests=requests)


def jacobi(matrix, right_hand):
    diag_part = jnp.diagonal(matrix)[:, None]
    iterate = right_hand / diag_part
    for sweep_no in range(ITERS):
        image = jnp.dot(matrix, iterate, precision=lax.Precision.HIGHEST, preferred_element_type=jnp.float32)
        iterate = iterate + (right_hand - image) / diag_part
    return iterate


def reference(diag_blocks, coupling, sources, requests):
    block_total = diag_blocks.shape[0]
    left_terms = []
    carried = jnp.zeros(sources.shape[1:], jnp.float32)
    for block_no in range(block_total):
        left_terms.append(carried)
        forward = jacobi(diag_blocks[block_no], sources[block_no] - carried)
        carried = jnp.dot(coupling[block_no].T, forward, precision=lax.Precision.HIGHEST, preferred_element_type=jnp.float32)
    results = [None] * block_total
    ahead = jnp.zeros(sources.shape[1:], jnp.float32)
    for block_no in reversed(range(block_total)):
        right_term = jnp.dot(coupling[block_no], ahead, precision=lax.Precision.HIGHEST, preferred_element_type=jnp.float32)
        ahead = jacobi(diag_blocks[block_no], sources[block_no] - left_terms[block_no] - right_term)
        results[block_no] = ahead
    panels = jnp.stack(results)
    where_rows = jnp.broadcast_to(requests[:, :, None], (requests.shape[0], requests.shape[1], panels.shape[2]))
    picked = jnp.take_along_axis(panels, where_rows, axis=1)
    return (panels, picked)
```

```python
import functools

import jax
import jax.numpy as jnp
from jax import lax
from jax.experimental import pallas as pl
from jax.experimental.pallas import tpu as pltpu
from jax.sharding import PartitionSpec as P

ITERS = 2
F32, BF16 = jnp.float32, jnp.bfloat16
LANES = 128

ORDERS = {
    (0, 0): (1, 3, 4, 12),
    (0, 1): (3, 1, 12, 4),
    (1, 0): (4, 12, 1, 3),
    (1, 1): (12, 4, 3, 1),
}


def exchange_pairs(half, step):
    return [
        (yz * 2 + core, (yz ^ ORDERS[core, half][step]) * 2 + core)
        for yz in range(16)
        for core in range(2)
    ]


SIBLINGS = [(p, p ^ 1) for p in range(32)]


def offset_of(core, half, unit):
    offset = 0
    for step in range(4):
        if unit >> step & 1:
            offset ^= ORDERS[core, half][step]
    return offset


def gathered(shard):
    half_rows = shard.shape[0] // 2
    held = [shard[:half_rows], shard[half_rows:]]
    for step in range(3):
        got = [lax.ppermute(held[h], "panel", exchange_pairs(h, step)) for h in range(2)]
        held = [jnp.concatenate([held[h], got[h]], 0) for h in range(2)]
    last = [lax.ppermute(held[h], "panel", exchange_pairs(h, 3)) for h in range(2)]
    other = [lax.ppermute(held[h], "panel", SIBLINGS) for h in range(2)]
    other_last = [lax.ppermute(last[h], "panel", SIBLINGS) for h in range(2)]
    return [*held, *last, *other, *other_last]


def split(x):
    high = x.astype(BF16)
    return high, (x - high.astype(F32)).astype(BF16)


def product(x, high_ref, low_ref, transposed=False):
    rows = x.shape[0]
    both = jnp.concatenate(split(x), 0)
    dims = (((1,), (1 if transposed else 0,)), ((), ()))
    first = lax.dot_general(both, high_ref[...], dims, preferred_element_type=F32)
    second = lax.dot_general(both, low_ref[...], dims, preferred_element_type=F32)
    total = first + second
    return total[:rows] + total[rows:]


def jacobi(right_hand, diag, d_high, d_low):
    iterate = right_hand / diag
    for _ in range(ITERS):
        image = product(iterate, d_high, d_low)
        iterate = iterate + (right_hand - image) / diag
    return iterate


def first_kernel(me_ref, *refs, size, cols, width):
    pieces = refs[:8]
    d_high, d_low, c_high, c_low, source, diag, wanted, carried = refs[8:16]
    whole, sems = refs[16:]
    me = me_ref[0]
    core = lax.rem(me, 2)
    place = lax.div(me, 2)
    unit_rows = size // 64
    copies = []
    for number in range(8):
        half = number % 2
        last = number // 2 % 2
        sibling = number // 4
        for unit in range(8):
            offset = jnp.where(
                core == sibling,
                offset_of(0, half, unit + 8 * last),
                offset_of(1, half, unit + 8 * last),
            )
            owner = lax.bitwise_xor(place, offset) * 2 + lax.bitwise_xor(core, sibling)
            row = pl.multiple_of((owner * 2 + half) * unit_rows, unit_rows)
            copy = pltpu.make_async_copy(
                pieces[number].at[pl.ds(unit * unit_rows, unit_rows)],
                whole.at[pl.ds(row, unit_rows)],
                sems.at[number * 8 + unit],
            )
            copy.start()
            copies.append(copy)
    for copy in copies:
        copy.wait()

    step_rows = 64

    def cut(i, _):
        rows = pl.ds(pl.multiple_of(i * step_rows, step_rows), step_rows)
        d_high[rows, :], d_low[rows, :] = split(whole[rows, 0:size])
        c_high[rows, :], c_low[rows, :] = split(whole[rows, size : 2 * size])
        return 0

    lax.fori_loop(0, size // step_rows, cut, 0)

    at = 2 * size
    pick = lax.broadcasted_iota(jnp.int32, (8, cols), 1) == (
        lax.broadcasted_iota(jnp.int32, (8, cols), 0) + me * 8
    )
    own = lax.dot_general(
        pick.astype(F32),
        whole[:, at : at + cols],
        (((1,), (1,)), ((), ())),
        precision=lax.Precision.HIGHEST,
        preferred_element_type=F32,
    )
    source[...] = own
    eye = lax.broadcasted_iota(jnp.int32, (LANES, LANES), 0) == lax.broadcasted_iota(
        jnp.int32, (LANES, LANES), 1
    )
    for start in range(0, size, LANES):
        tile = whole[start : start + LANES, start : start + LANES]
        line = jnp.sum(jnp.where(eye, tile, 0.0), axis=0, keepdims=True)
        diag[:, start : start + LANES] = jnp.broadcast_to(line, (8, LANES))
    line = jnp.sum(whole[:, at + cols : at + cols + LANES], axis=0, keepdims=True)
    wanted[...] = jnp.broadcast_to(line, (8, LANES))
    forward = jacobi(own, diag[...], d_high, d_low)
    carried[...] = product(forward, c_high, c_low)


def forward_kernel(count, d_high, d_low, c_high, c_low, source, diag, *refs):
    right_hand = source[...]
    for ref in refs[:count]:
        right_hand = right_hand - ref[...]
    forward = jacobi(right_hand, diag[...], d_high, d_low)
    refs[count][...] = product(forward, c_high, c_low)


def turn_kernel(count, d_high, d_low, source, diag, *refs):
    right_hand = source[...]
    for ref in refs[:count]:
        right_hand = right_hand - ref[...]
    refs[count][...] = right_hand
    refs[count + 1][...] = jacobi(right_hand, diag[...], d_high, d_low)


def ahead_of(refs):
    ahead = refs[0][...]
    for ref in refs[1:]:
        ahead = ahead + ref[...]
    return ahead


def backward_kernel(count, d_high, d_low, c_high, c_low, right_hand, diag, *refs):
    ahead = ahead_of(refs[:count])
    rest = right_hand[...] - product(ahead, c_high, c_low, True)
    refs[count][...] = jacobi(rest, diag[...], d_high, d_low)


def last_kernel(count, d_high, d_low, c_high, c_low, right_hand, diag, wanted, *refs):
    ahead = ahead_of(refs[:count])
    rest = right_hand[...] - product(ahead, c_high, c_low, True)
    panel = jacobi(rest, diag[...], d_high, d_low)
    size = panel.shape[1]
    high = panel.astype(BF16)
    rest = panel - high.astype(F32)
    middle = rest.astype(BF16)
    low = (rest - middle.astype(F32)).astype(BF16)
    line = wanted[0:1, :].astype(jnp.int32)
    chosen = (lax.broadcasted_iota(jnp.int32, (size, LANES), 0) == line).astype(BF16)
    parts = [jnp.dot(part, chosen, preferred_element_type=F32) for part in (high, middle, low)]
    picked = parts[0] + parts[1] + parts[2]
    send = refs[count]
    blocks = send.shape[0]
    own, few = size // blocks, LANES // blocks
    filler = jnp.zeros((8, LANES - own - few), F32)
    for block in range(blocks):
        send[block] = jnp.concatenate(
            [
                panel[:, block * own : (block + 1) * own],
                picked[:, block * few : (block + 1) * few],
                filler,
            ],
            1,
        )


def unpack_kernel(got, panels, picked):
    turned = got[...].T
    own = panels.shape[0]
    panels[...] = turned[:own]
    picked[...] = turned[own : own + picked.shape[0]]


def call(kernel, out_shape, *args):
    return pl.pallas_call(kernel, out_shape=out_shape)(*args)


def per_device(diag_blocks, coupling, sources, requests):
    rows, size, cols = diag_blocks.shape[1], diag_blocks.shape[2], sources.shape[2]
    few = requests.shape[1]
    me = lax.axis_index("panel").astype(jnp.int32)
    lane = lax.broadcasted_iota(jnp.int32, (rows, LANES), 1)
    row = lax.broadcasted_iota(jnp.int32, (rows, LANES), 0)
    slots = jnp.zeros((rows, LANES), F32)
    for k in range(few):
        slots = slots + jnp.where((lane == me * few + k) & (row == 0), requests[0, k].astype(F32), 0.0)
    shard = jnp.concatenate([diag_blocks[0], coupling[0], sources[0], slots], 1)
    width = shard.shape[1]
    pieces = gathered(shard)

    vec = jax.ShapeDtypeStruct((8, size), F32)
    mat = jax.ShapeDtypeStruct((size, size), BF16)
    anywhere = pl.BlockSpec(memory_space=pl.ANY)
    d_high, d_low, c_high, c_low, source, diag, wanted, carried = pl.pallas_call(
        functools.partial(first_kernel, size=size, cols=cols, width=width),
        out_shape=(mat, mat, mat, mat, vec, vec, jax.ShapeDtypeStruct((8, LANES), F32), vec),
        in_specs=[pl.BlockSpec(memory_space=pltpu.SMEM)] + [anywhere] * 8,
        scratch_shapes=[pltpu.VMEM((size, width), F32), pltpu.SemaphoreType.DMA((64,))],
    )(me[None], *pieces)
    mats = (d_high, d_low, c_high, c_low)

    lefts = []
    for k in range(3):
        lefts.append(lax.ppermute(carried, "depth", [(k, k + 1)]))
        if k < 2:
            carried = call(
                functools.partial(forward_kernel, k + 1), vec, *mats, source, diag, *lefts
            )
    right_hand, panel = call(
        functools.partial(turn_kernel, 3), (vec, vec), d_high, d_low, source, diag, *lefts
    )
    aheads = []
    for k in range(3):
        aheads.append(lax.ppermute(panel, "depth", [(3 - k, 2 - k)]))
        if k < 2:
            panel = call(
                functools.partial(backward_kernel, k + 1), vec, *mats, right_hand, diag, *aheads
            )
    send = call(
        functools.partial(last_kernel, 3),
        jax.ShapeDtypeStruct((size // rows, 8, LANES), F32),
        *mats, right_hand, diag, wanted, *aheads,
    )
    got = lax.all_to_all(send, "panel", 0, 0, tiled=True).reshape(cols, LANES)
    panels, picked = call(
        unpack_kernel,
        (jax.ShapeDtypeStruct((rows, cols), F32), jax.ShapeDtypeStruct((few, cols), F32)),
        got,
    )
    return panels[None], picked[None]


def solution(mesh):
    placed = (
        P("depth", "panel", None),
        P("depth", "panel", None),
        P("depth", "panel", None),
        P("depth", "panel"),
    )
    return jax.shard_map(
        per_device,
        mesh=mesh,
        in_specs=placed,
        out_specs=(P("depth", "panel", None), P("depth", "panel", None)),
        check_vma=False,
    )
```

```python
import functools

import jax
import jax.numpy as jnp
from jax import lax
from jax.experimental import pallas as pl
from jax.experimental.pallas import tpu as pltpu
from jax.sharding import PartitionSpec as P

ITERS = 2
F32, BF16 = jnp.float32, jnp.bfloat16
LANES = 128

ORDERS = {
    (0, 0): (1, 3, 4, 12),
    (0, 1): (3, 1, 12, 4),
    (1, 0): (4, 12, 1, 3),
    (1, 1): (12, 4, 3, 1),
}


def exchange_pairs(half, step):
    return [
        (yz * 2 + core, (yz ^ ORDERS[core, half][step]) * 2 + core)
        for yz in range(16)
        for core in range(2)
    ]


SIBLINGS = [(p, p ^ 1) for p in range(32)]


def offset_of(core, half, unit):
    offset = 0
    for step in range(4):
        if unit >> step & 1:
            offset ^= ORDERS[core, half][step]
    return offset


def gathered(held):
    for step in range(3):
        got = [lax.ppermute(held[h], "panel", exchange_pairs(h, step)) for h in range(2)]
        held = [jnp.concatenate([held[h], got[h]], 0) for h in range(2)]
    last = [lax.ppermute(held[h], "panel", exchange_pairs(h, 3)) for h in range(2)]
    other = [lax.ppermute(held[h], "panel", SIBLINGS) for h in range(2)]
    other_last = [lax.ppermute(last[h], "panel", SIBLINGS) for h in range(2)]
    return [*held, *last, *other, *other_last]


def split(x):
    high = x.astype(BF16)
    return high, (x - high.astype(F32)).astype(BF16)


def product(x, high_ref, low_ref, transposed=False):
    rows = x.shape[0]
    both = jnp.concatenate(split(x), 0)
    dims = (((1,), (1 if transposed else 0,)), ((), ()))
    first = lax.dot_general(both, high_ref[...], dims, preferred_element_type=F32)
    second = lax.dot_general(both, low_ref[...], dims, preferred_element_type=F32)
    total = first + second
    return total[:rows] + total[rows:]


def jacobi(right_hand, diag, d_high, d_low):
    iterate = right_hand / diag
    for _ in range(ITERS):
        image = product(iterate, d_high, d_low)
        iterate = iterate + (right_hand - image) / diag
    return iterate


def pack_kernel(me_ref, requests, diag_rows, coupling_rows, source_rows, *halves):
    few = requests.shape[0]
    count = halves[0].shape[0]
    size, cols = diag_rows.shape[1], source_rows.shape[1]
    row = lax.broadcasted_iota(jnp.int32, (count, LANES), 0)
    lane = lax.broadcasted_iota(jnp.int32, (count, LANES), 1)
    slots = jnp.zeros((count, LANES), F32)
    for k in range(few):
        here = (row == 0) & (lane == me_ref[0] * few + k)
        slots = jnp.where(here, requests[k].astype(F32), slots)
    for number, half in enumerate(halves):
        rows = slice(number * count, (number + 1) * count)
        half[:, 0:size] = diag_rows[rows]
        half[:, size : 2 * size] = coupling_rows[rows]
        half[:, 2 * size : 2 * size + cols] = source_rows[rows]
        half[:, 2 * size + cols :] = slots if number == 0 else jnp.zeros_like(slots)


def first_kernel(me_ref, *refs, size, cols):
    pieces = refs[:8]
    d_high, d_low, c_high, c_low, source, diag, wanted, carried, side = refs[8:]
    me = me_ref[0]
    core = lax.rem(me, 2)
    place = lax.div(me, 2)
    unit_rows = size // 64
    for number in range(8):
        half = number % 2
        last = number // 2 % 2
        sibling = number // 4
        for unit in range(8):
            offset = jnp.where(
                core == sibling,
                offset_of(0, half, unit + 8 * last),
                offset_of(1, half, unit + 8 * last),
            )
            owner = lax.bitwise_xor(place, offset) * 2 + lax.bitwise_xor(core, sibling)
            row = pl.multiple_of((owner * 2 + half) * unit_rows, unit_rows)
            held = pieces[number].at[unit * unit_rows : (unit + 1) * unit_rows]
            rows = pl.ds(row, unit_rows)
            d_high[rows, :], d_low[rows, :] = split(held[:, 0:size])
            c_high[rows, :], c_low[rows, :] = split(held[:, size : 2 * size])
            side[rows, :] = held[:, 2 * size :]

    pick = lax.broadcasted_iota(jnp.int32, (8, cols), 1) == (
        lax.broadcasted_iota(jnp.int32, (8, cols), 0) + me * 8
    )
    own = lax.dot_general(
        pick.astype(F32),
        side[:, 0:cols],
        (((1,), (1,)), ((), ())),
        precision=lax.Precision.HIGHEST,
        preferred_element_type=F32,
    )
    source[...] = own
    eye = lax.broadcasted_iota(jnp.int32, (LANES, LANES), 0) == lax.broadcasted_iota(
        jnp.int32, (LANES, LANES), 1
    )
    for start in range(0, size, LANES):
        tiles = slice(start, start + LANES)
        tile = d_high[tiles, tiles].astype(F32) + d_low[tiles, tiles].astype(F32)
        line = jnp.sum(jnp.where(eye, tile, 0.0), axis=0, keepdims=True)
        diag[:, start : start + LANES] = jnp.broadcast_to(line, (8, LANES))
    line = jnp.sum(side[:, cols : cols + LANES], axis=0, keepdims=True)
    wanted[...] = jnp.broadcast_to(line, (8, LANES))
    forward = jacobi(own, diag[...], d_high, d_low)
    carried[...] = product(forward, c_high, c_low)


def forward_kernel(count, d_high, d_low, c_high, c_low, source, diag, *refs):
    right_hand = source[...]
    for ref in refs[:count]:
        right_hand = right_hand - ref[...]
    forward = jacobi(right_hand, diag[...], d_high, d_low)
    refs[count][...] = product(forward, c_high, c_low)


def turn_kernel(count, d_high, d_low, source, diag, *refs):
    right_hand = source[...]
    for ref in refs[:count]:
        right_hand = right_hand - ref[...]
    refs[count][...] = right_hand
    refs[count + 1][...] = jacobi(right_hand, diag[...], d_high, d_low)


def ahead_of(refs):
    ahead = refs[0][...]
    for ref in refs[1:]:
        ahead = ahead + ref[...]
    return ahead


def backward_kernel(count, d_high, d_low, c_high, c_low, right_hand, diag, *refs):
    ahead = ahead_of(refs[:count])
    rest = right_hand[...] - product(ahead, c_high, c_low, True)
    refs[count][...] = jacobi(rest, diag[...], d_high, d_low)


def last_kernel(count, d_high, d_low, c_high, c_low, right_hand, diag, wanted, *refs):
    ahead = ahead_of(refs[:count])
    rest = right_hand[...] - product(ahead, c_high, c_low, True)
    panel = jacobi(rest, diag[...], d_high, d_low)
    size = panel.shape[1]
    high = panel.astype(BF16)
    rest = panel - high.astype(F32)
    middle = rest.astype(BF16)
    low = (rest - middle.astype(F32)).astype(BF16)
    line = wanted[0:1, :].astype(jnp.int32)
    chosen = (lax.broadcasted_iota(jnp.int32, (size, LANES), 0) == line).astype(BF16)
    parts = [jnp.dot(part, chosen, preferred_element_type=F32) for part in (high, middle, low)]
    picked = parts[0] + parts[1] + parts[2]
    send = refs[count]
    blocks = send.shape[0]
    own, few = size // blocks, LANES // blocks
    filler = jnp.zeros((8, LANES - own - few), F32)
    for block in range(blocks):
        send[block] = jnp.concatenate(
            [
                panel[:, block * own : (block + 1) * own],
                picked[:, block * few : (block + 1) * few],
                filler,
            ],
            1,
        )


def unpack_kernel(got, panels, picked):
    turned = got[...].T
    own = panels.shape[0]
    panels[...] = turned[:own]
    picked[...] = turned[own : own + picked.shape[0]]


def vmem(shape, dtype=F32):
    return pltpu.VMEM(shape, dtype)


def call(kernel, out_shape, *args, scalars=(), scratch=(), limit=8, near=True):
    if near:
        args = [pltpu.with_memory_space_constraint(arg, pltpu.VMEM) for arg in args]
    space = pl.BlockSpec(memory_space=pltpu.VMEM)
    scalar = pl.BlockSpec(memory_space=pltpu.SMEM)
    return pl.pallas_call(
        kernel,
        out_shape=out_shape,
        in_specs=[scalar] * len(scalars) + [space] * len(args),
        out_specs=jax.tree.map(lambda _: space, out_shape),
        scratch_shapes=scratch,
        compiler_params=pltpu.CompilerParams(vmem_limit_bytes=limit * 1024 * 1024),
    )(*scalars, *args)


def per_device(diag_blocks, coupling, sources, requests):
    rows, size, cols = diag_blocks.shape[1], diag_blocks.shape[2], sources.shape[2]
    few = requests.shape[1]
    me = lax.axis_index("panel").astype(jnp.int32)
    width = 2 * size + cols + LANES
    half = vmem((rows // 2, width))
    pieces = gathered(
        call(
            pack_kernel,
            (half, half),
            diag_blocks[0], coupling[0], sources[0],
            scalars=(me[None], requests[0]),
            near=False,
        )
    )

    vec = vmem((8, size))
    mat = vmem((size, size), BF16)
    d_high, d_low, c_high, c_low, source, diag, wanted, carried = call(
        functools.partial(first_kernel, size=size, cols=cols),
        (mat, mat, mat, mat, vec, vec, vmem((8, LANES)), vec),
        *pieces,
        scalars=(me[None],),
        scratch=[pltpu.VMEM((size, width - 2 * size), F32)],
    )
    mats = (d_high, d_low, c_high, c_low)

    lefts = []
    for k in range(3):
        lefts.append(lax.ppermute(carried, "depth", [(k, k + 1)]))
        if k < 2:
            carried = call(
                functools.partial(forward_kernel, k + 1), vec, *mats, source, diag, *lefts
            )
    right_hand, panel = call(
        functools.partial(turn_kernel, 3), (vec, vec), d_high, d_low, source, diag, *lefts
    )
    aheads = []
    for k in range(3):
        aheads.append(lax.ppermute(panel, "depth", [(3 - k, 2 - k)]))
        if k < 2:
            panel = call(
                functools.partial(backward_kernel, k + 1), vec, *mats, right_hand, diag, *aheads
            )
    send = call(
        functools.partial(last_kernel, 3),
        vmem((size // rows, 8, LANES)),
        *mats, right_hand, diag, wanted, *aheads,
    )
    got = lax.all_to_all(send, "panel", 0, 0, tiled=True).reshape(cols, LANES)
    panels, picked = call(
        unpack_kernel,
        (jax.ShapeDtypeStruct((rows, cols), F32), jax.ShapeDtypeStruct((few, cols), F32)),
        got,
    )
    return panels[None], picked[None]


def solution(mesh):
    placed = (
        P("depth", "panel", None),
        P("depth", "panel", None),
        P("depth", "panel", None),
        P("depth", "panel"),
    )
    return jax.shard_map(
        per_device,
        mesh=mesh,
        in_specs=placed,
        out_specs=(P("depth", "panel", None), P("depth", "panel", None)),
        check_vma=False,
    )
```

```python
import functools

import jax
import jax.numpy as jnp
from jax import lax
from jax.experimental import pallas as pl
from jax.experimental.pallas import tpu as pltpu
from jax.sharding import PartitionSpec as P

ITERS = 2
F32, BF16 = jnp.float32, jnp.bfloat16
LANES = 128

AXES = ((1, 3, 2), (4, 12, 8))
SIBLINGS = [(p, p ^ 1) for p in range(32)]


def from_partner(block, phase, number):
    pairs = [
        (yz * 2 + core, (yz ^ AXES[core ^ phase][number]) * 2 + core)
        for yz in range(16)
        for core in range(2)
    ]
    return lax.ppermute(block, "panel", pairs)


PIECES = (("A", None), ("B", None), ("A", 0), ("A", 1), ("B", 0), ("B", 1), ("A", 2), ("B", 2))


def offset_of(core, piece, unit):
    half, line = piece
    near = AXES[core]
    offset = ((0, near[0]) if half == "A" else (near[1], near[2]))[unit]
    return offset ^ (0 if line is None else AXES[1 - core][line])


def gathered(own):
    near, other, far = [from_partner(own, 0, number) for number in range(3)]
    own, near, other, far = lax.optimization_barrier((own, near, other, far))
    a = jnp.concatenate([own, near], 0)
    b = jnp.concatenate([other, far], 0)
    a0, a1 = from_partner(a, 1, 0), from_partner(a, 1, 1)
    b0, b1 = from_partner(b, 1, 0), from_partner(b, 1, 1)
    a2, b2 = from_partner(a1, 1, 0), from_partner(b0, 1, 1)
    pieces = [a, b, a0, a1, b0, b1, a2, b2]
    return pieces + [lax.ppermute(piece, "panel", SIBLINGS) for piece in pieces]


def split(x):
    high = x.astype(BF16)
    return high, (x - high.astype(F32)).astype(BF16)


def product(x, high_ref, low_ref, transposed=False):
    rows = x.shape[0]
    both = jnp.concatenate(split(x), 0)
    dims = (((1,), (1 if transposed else 0,)), ((), ()))
    first = lax.dot_general(both, high_ref[...], dims, preferred_element_type=F32)
    second = lax.dot_general(both, low_ref[...], dims, preferred_element_type=F32)
    total = first + second
    return total[:rows] + total[rows:]


def jacobi(right_hand, diag, d_high, d_low):
    iterate = right_hand / diag
    for _ in range(ITERS):
        image = product(iterate, d_high, d_low)
        iterate = iterate + (right_hand - image) / diag
    return iterate


def pack_kernel(me_ref, asked, diag_rows, coupling_rows, source_rows, packed, requests, sems):
    few = requests.shape[1]
    fetch = pltpu.make_async_copy(asked, requests, sems.at[3])
    fetch.start()
    count, size = diag_rows.shape
    cols = source_rows.shape[1]
    copies = []
    at = 0
    for number, rows in enumerate((diag_rows, coupling_rows, source_rows)):
        width = rows.shape[1]
        copies.append(
            pltpu.make_async_copy(rows, packed.at[:, at : at + width], sems.at[number])
        )
        copies[-1].start()
        at += width
    fetch.wait()
    row = lax.broadcasted_iota(jnp.int32, (count, LANES), 0)
    lane = lax.broadcasted_iota(jnp.int32, (count, LANES), 1)
    slots = jnp.zeros((count, LANES), F32)
    for k in range(few):
        here = (row == 0) & (lane == me_ref[0] * few + k)
        slots = jnp.where(here, requests[0, k].astype(F32), slots)
    packed[:, at:] = slots
    for copy in copies:
        copy.wait()


def first_kernel(me_ref, *refs, size, cols):
    pieces = refs[:16]
    d_high, d_low, c_high, c_low, source, diag, wanted, carried, side = refs[16:]
    me = me_ref[0]
    core = lax.rem(me, 2)
    place = lax.div(me, 2)
    unit_rows = size // 32
    for number in range(16):
        sibling = number // 8
        for unit in range(2):
            piece = PIECES[number % 8]
            offset = jnp.where(
                core == sibling, offset_of(0, piece, unit), offset_of(1, piece, unit)
            )
            owner = lax.bitwise_xor(place, offset) * 2 + lax.bitwise_xor(core, sibling)
            rows = pl.ds(pl.multiple_of(owner * unit_rows, unit_rows), unit_rows)
            held = pieces[number].at[unit * unit_rows : (unit + 1) * unit_rows]
            d_high[rows, :], d_low[rows, :] = split(held[:, 0:size])
            c_high[rows, :], c_low[rows, :] = split(held[:, size : 2 * size])
            side[rows, :] = held[:, 2 * size :]

    pick = lax.broadcasted_iota(jnp.int32, (8, cols), 1) == (
        lax.broadcasted_iota(jnp.int32, (8, cols), 0) + me * 8
    )
    own = lax.dot_general(
        pick.astype(F32),
        side[:, 0:cols],
        (((1,), (1,)), ((), ())),
        precision=lax.Precision.HIGHEST,
        preferred_element_type=F32,
    )
    source[...] = own
    eye = lax.broadcasted_iota(jnp.int32, (LANES, LANES), 0) == lax.broadcasted_iota(
        jnp.int32, (LANES, LANES), 1
    )
    for start in range(0, size, LANES):
        tiles = slice(start, start + LANES)
        tile = d_high[tiles, tiles].astype(F32) + d_low[tiles, tiles].astype(F32)
        line = jnp.sum(jnp.where(eye, tile, 0.0), axis=0, keepdims=True)
        diag[:, start : start + LANES] = jnp.broadcast_to(line, (8, LANES))
    line = jnp.sum(side[:, cols : cols + LANES], axis=0, keepdims=True)
    wanted[...] = jnp.broadcast_to(line, (8, LANES))
    forward = jacobi(own, diag[...], d_high, d_low)
    carried[...] = product(forward, c_high, c_low)


def forward_kernel(count, d_high, d_low, c_high, c_low, source, diag, *refs):
    right_hand = source[...]
    for ref in refs[:count]:
        right_hand = right_hand - ref[...]
    forward = jacobi(right_hand, diag[...], d_high, d_low)
    refs[count][...] = product(forward, c_high, c_low)


def turn_kernel(count, d_high, d_low, source, diag, *refs):
    right_hand = source[...]
    for ref in refs[:count]:
        right_hand = right_hand - ref[...]
    refs[count][...] = right_hand
    refs[count + 1][...] = jacobi(right_hand, diag[...], d_high, d_low)


def ahead_of(refs):
    ahead = refs[0][...]
    for ref in refs[1:]:
        ahead = ahead + ref[...]
    return ahead


def backward_kernel(count, d_high, d_low, c_high, c_low, right_hand, diag, *refs):
    ahead = ahead_of(refs[:count])
    rest = right_hand[...] - product(ahead, c_high, c_low, True)
    refs[count][...] = jacobi(rest, diag[...], d_high, d_low)


def last_kernel(count, d_high, d_low, c_high, c_low, right_hand, diag, wanted, *refs):
    ahead = ahead_of(refs[:count])
    rest = right_hand[...] - product(ahead, c_high, c_low, True)
    panel = jacobi(rest, diag[...], d_high, d_low)
    size = panel.shape[1]
    high = panel.astype(BF16)
    rest = panel - high.astype(F32)
    middle = rest.astype(BF16)
    low = (rest - middle.astype(F32)).astype(BF16)
    line = wanted[0:1, :].astype(jnp.int32)
    chosen = (lax.broadcasted_iota(jnp.int32, (size, LANES), 0) == line).astype(BF16)
    parts = [jnp.dot(part, chosen, preferred_element_type=F32) for part in (high, middle, low)]
    picked = parts[0] + parts[1] + parts[2]
    send = refs[count]
    blocks = send.shape[0]
    own, few = size // blocks, LANES // blocks
    filler = jnp.zeros((8, LANES - own - few), F32)
    for block in range(blocks):
        send[block] = jnp.concatenate(
            [
                panel[:, block * own : (block + 1) * own],
                picked[:, block * few : (block + 1) * few],
                filler,
            ],
            1,
        )


def unpack_kernel(got, panels, picked):
    turned = got[...].T
    own = panels.shape[0]
    panels[...] = turned[:own]
    picked[...] = turned[own : own + picked.shape[0]]


def vmem(shape, dtype=F32):
    return pltpu.VMEM(shape, dtype)


def call(kernel, out_shape, *args, scalars=(), scratch=(), limit=8):
    args = [pltpu.with_memory_space_constraint(arg, pltpu.VMEM) for arg in args]
    space = pl.BlockSpec(memory_space=pltpu.VMEM)
    scalar = pl.BlockSpec(memory_space=pltpu.SMEM)
    return pl.pallas_call(
        kernel,
        out_shape=out_shape,
        in_specs=[scalar] * len(scalars) + [space] * len(args),
        out_specs=jax.tree.map(lambda _: space, out_shape),
        scratch_shapes=scratch,
        compiler_params=pltpu.CompilerParams(vmem_limit_bytes=limit * 1024 * 1024),
    )(*scalars, *args)


def per_device(diag_blocks, coupling, sources, requests):
    rows, size, cols = diag_blocks.shape[1], diag_blocks.shape[2], sources.shape[2]
    few = requests.shape[1]
    me = lax.axis_index("panel").astype(jnp.int32)
    width = 2 * size + cols + LANES
    far = pl.BlockSpec(memory_space=pltpu.HBM)
    operands = (requests, diag_blocks[0], coupling[0], sources[0])
    scalar = pl.BlockSpec(memory_space=pltpu.SMEM)
    packed = pl.pallas_call(
        pack_kernel,
        out_shape=vmem((rows, width)),
        in_specs=[scalar, far, far, far, far],
        out_specs=pl.BlockSpec(memory_space=pltpu.VMEM),
        scratch_shapes=[pltpu.SMEM(requests.shape, jnp.int32), pltpu.SemaphoreType.DMA((4,))],
        compiler_params=pltpu.CompilerParams(vmem_limit_bytes=8 * 1024 * 1024),
    )(me[None], *[pltpu.with_memory_space_constraint(x, pltpu.HBM) for x in operands])
    pieces = gathered(packed)

    vec = vmem((8, size))
    mat = vmem((size, size), BF16)
    d_high, d_low, c_high, c_low, source, diag, wanted, carried = call(
        functools.partial(first_kernel, size=size, cols=cols),
        (mat, mat, mat, mat, vec, vec, vmem((8, LANES)), vec),
        *pieces,
        scalars=(me[None],),
        scratch=[pltpu.VMEM((size, width - 2 * size), F32)],
    )
    mats = (d_high, d_low, c_high, c_low)

    lefts = []
    for k in range(3):
        lefts.append(lax.ppermute(carried, "depth", [(k, k + 1)]))
        if k < 2:
            carried = call(
                functools.partial(forward_kernel, k + 1), vec, *mats, source, diag, *lefts
            )
    right_hand, panel = call(
        functools.partial(turn_kernel, 3), (vec, vec), d_high, d_low, source, diag, *lefts
    )
    aheads = []
    for k in range(3):
        aheads.append(lax.ppermute(panel, "depth", [(3 - k, 2 - k)]))
        if k < 2:
            panel = call(
                functools.partial(backward_kernel, k + 1), vec, *mats, right_hand, diag, *aheads
            )
    send = call(
        functools.partial(last_kernel, 3),
        vmem((size // rows, 8, LANES)),
        *mats, right_hand, diag, wanted, *aheads,
    )
    got = lax.all_to_all(send, "panel", 0, 0, tiled=True).reshape(cols, LANES)
    panels, picked = call(
        unpack_kernel,
        (jax.ShapeDtypeStruct((rows, cols), F32), jax.ShapeDtypeStruct((few, cols), F32)),
        got,
    )
    return panels[None], picked[None]


def solution(mesh):
    placed = (
        P("depth", "panel", None),
        P("depth", "panel", None),
        P("depth", "panel", None),
        P("depth", "panel"),
    )
    return jax.shard_map(
        per_device,
        mesh=mesh,
        in_specs=placed,
        out_specs=(P("depth", "panel", None), P("depth", "panel", None)),
        check_vma=False,
    )
```

```python
import functools

import jax
import jax.numpy as jnp
from jax import lax
from jax.experimental import pallas as pl
from jax.experimental.pallas import tpu as pltpu
from jax.sharding import PartitionSpec as P

ITERS = 2
F32, BF16 = jnp.float32, jnp.bfloat16
LANES = 128

AXES = ((1, 3, 2), (4, 12, 8))
SIBLINGS = [(p, p ^ 1) for p in range(32)]


def from_partner(block, phase, number):
    pairs = [
        (yz * 2 + core, (yz ^ AXES[core ^ phase][number]) * 2 + core)
        for yz in range(16)
        for core in range(2)
    ]
    return lax.ppermute(block, "panel", pairs)


PIECES = (("A", None), ("B", None), ("A", 0), ("A", 1), ("B", 0), ("B", 1), ("A", 2), ("B", 2))


def offset_of(core, piece, unit):
    half, line = piece
    near = AXES[core]
    offset = ((0, near[0]) if half == "A" else (near[1], near[2]))[unit]
    return offset ^ (0 if line is None else AXES[1 - core][line])


def gathered(own):
    near, other, far = [from_partner(own, 0, number) for number in range(3)]
    own, near, other, far = lax.optimization_barrier((own, near, other, far))
    a = jnp.concatenate([own, near], 0)
    b = jnp.concatenate([other, far], 0)
    a0, a1 = from_partner(a, 1, 0), from_partner(a, 1, 1)
    b0, b1 = from_partner(b, 1, 0), from_partner(b, 1, 1)
    a2, b2 = from_partner(a1, 1, 0), from_partner(b0, 1, 1)
    pieces = [a, b, a0, a1, b0, b1, a2, b2]
    return pieces + [lax.ppermute(piece, "panel", SIBLINGS) for piece in pieces]


def split(x):
    high = x.astype(BF16)
    return high, (x - high.astype(F32)).astype(BF16)


def product(x, high_ref, low_ref, transposed=False):
    rows = x.shape[0]
    both = jnp.concatenate(split(x), 0)
    dims = (((1,), (1 if transposed else 0,)), ((), ()))
    first = lax.dot_general(both, high_ref[...], dims, preferred_element_type=F32)
    second = lax.dot_general(both, low_ref[...], dims, preferred_element_type=F32)
    total = first + second
    return total[:rows] + total[rows:]


def jacobi(right_hand, diag, d_high, d_low):
    iterate = right_hand / diag
    for _ in range(ITERS):
        image = product(iterate, d_high, d_low)
        iterate = iterate + (right_hand - image) / diag
    return iterate


def pack_kernel(me_ref, asked, diag_rows, coupling_rows, source_rows, packed, requests, sems):
    few = requests.shape[1]
    fetch = pltpu.make_async_copy(asked, requests, sems.at[3])
    fetch.start()
    count, size = diag_rows.shape
    cols = source_rows.shape[1]
    copies = []
    at = 0
    for number, rows in enumerate((diag_rows, coupling_rows, source_rows)):
        width = rows.shape[1]
        copies.append(
            pltpu.make_async_copy(rows, packed.at[:, at : at + width], sems.at[number])
        )
        copies[-1].start()
        at += width
    fetch.wait()
    row = lax.broadcasted_iota(jnp.int32, (count, LANES), 0)
    lane = lax.broadcasted_iota(jnp.int32, (count, LANES), 1)
    slots = jnp.zeros((count, LANES), F32)
    for k in range(few):
        here = (row == 0) & (lane == me_ref[0] * few + k)
        slots = jnp.where(here, requests[0, k].astype(F32), slots)
    packed[:, at:] = slots
    for copy in copies:
        copy.wait()


def first_kernel(me_ref, *refs, size, cols):
    pieces = refs[:16]
    d_high, d_low, c_high, c_low, source, diag, wanted, side = refs[16:]
    me = me_ref[0]
    core = lax.rem(me, 2)
    place = lax.div(me, 2)
    unit_rows = size // 32
    step = 16

    def move(piece, start, to):
        def body(i, _):
            rows = pl.ds(pl.multiple_of(to + i * step, step), step)
            held = piece.at[pl.ds(pl.multiple_of(start + i * step, step), step)]
            d_high[rows, :], d_low[rows, :] = split(held[:, 0:size])
            c_high[rows, :], c_low[rows, :] = split(held[:, size : 2 * size])
            side[rows, :] = held[:, 2 * size :]
            return 0

        lax.fori_loop(0, unit_rows // step, body, 0)

    for number in range(16):
        sibling = number // 8
        for unit in range(2):
            piece = PIECES[number % 8]
            offset = jnp.where(
                core == sibling, offset_of(0, piece, unit), offset_of(1, piece, unit)
            )
            owner = lax.bitwise_xor(place, offset) * 2 + lax.bitwise_xor(core, sibling)
            move(pieces[number], unit * unit_rows, owner * unit_rows)

    pick = lax.broadcasted_iota(jnp.int32, (8, cols), 1) == (
        lax.broadcasted_iota(jnp.int32, (8, cols), 0) + me * 8
    )
    own = lax.dot_general(
        pick.astype(F32),
        side[:, 0:cols],
        (((1,), (1,)), ((), ())),
        precision=lax.Precision.HIGHEST,
        preferred_element_type=F32,
    )
    source[...] = own
    eye = lax.broadcasted_iota(jnp.int32, (LANES, LANES), 0) == lax.broadcasted_iota(
        jnp.int32, (LANES, LANES), 1
    )
    for start in range(0, size, LANES):
        tiles = slice(start, start + LANES)
        tile = d_high[tiles, tiles].astype(F32) + d_low[tiles, tiles].astype(F32)
        line = jnp.sum(jnp.where(eye, tile, 0.0), axis=0, keepdims=True)
        diag[:, start : start + LANES] = jnp.broadcast_to(line, (8, LANES))
    line = jnp.sum(side[:, cols : cols + LANES], axis=0, keepdims=True)
    wanted[...] = jnp.broadcast_to(line, (8, LANES))


def hop(block, here, there):
    other = [k for k in range(4) if k not in (here, there)]
    route = [(here, there), (there, here), tuple(other), tuple(other[::-1])]
    return lax.ppermute(block, "depth", route)


def taken(plane, planes, refs):
    total = jnp.zeros_like(refs[0])
    for meant, ref in zip(planes, refs):
        total = jnp.where(plane == meant, ref[...], total)
    return total


def forward_kernel(stage, plane_ref, d_high, d_low, c_high, c_low, source, diag, *refs):
    @pl.when(plane_ref[0] == stage)
    def _():
        right_hand = source[...] - refs[0][...] if stage else source[...]
        forward = jacobi(right_hand, diag[...], d_high, d_low)
        refs[-1][...] = product(forward, c_high, c_low)


def turn_kernel(count, plane_ref, d_high, d_low, source, diag, *refs):
    right_hand = source[...] - taken(plane_ref[0], range(1, count + 1), refs[:count])
    refs[count][...] = right_hand

    @pl.when(plane_ref[0] == count)
    def _():
        refs[count + 1][...] = jacobi(right_hand, diag[...], d_high, d_low)


def backward_kernel(plane, plane_ref, d_high, d_low, c_high, c_low, right_hand, diag, ahead, panel):
    @pl.when(plane_ref[0] == plane)
    def _():
        rest = right_hand[...] - product(ahead[...], c_high, c_low, True)
        panel[...] = jacobi(rest, diag[...], d_high, d_low)


def last_kernel(count, plane_ref, d_high, d_low, c_high, c_low, right_hand, diag, wanted, *refs):
    ahead = taken(plane_ref[0], range(count - 1, -1, -1), refs[:count])
    rest = right_hand[...] - product(ahead, c_high, c_low, True)
    panel = jacobi(rest, diag[...], d_high, d_low)
    size = panel.shape[1]
    high = panel.astype(BF16)
    rest = panel - high.astype(F32)
    middle = rest.astype(BF16)
    low = (rest - middle.astype(F32)).astype(BF16)
    line = wanted[0:1, :].astype(jnp.int32)
    chosen = (lax.broadcasted_iota(jnp.int32, (size, LANES), 0) == line).astype(BF16)
    parts = [jnp.dot(part, chosen, preferred_element_type=F32) for part in (high, middle, low)]
    picked = parts[0] + parts[1] + parts[2]
    send = refs[count]
    blocks = send.shape[0]
    own, few = size // blocks, LANES // blocks
    filler = jnp.zeros((8, LANES - own - few), F32)
    for block in range(blocks):
        send[block] = jnp.concatenate(
            [
                panel[:, block * own : (block + 1) * own],
                picked[:, block * few : (block + 1) * few],
                filler,
            ],
            1,
        )


def unpack_kernel(got, panels, picked):
    turned = got[...].T
    own = panels.shape[0]
    panels[...] = turned[:own]
    picked[...] = turned[own : own + picked.shape[0]]


def vmem(shape, dtype=F32):
    return pltpu.VMEM(shape, dtype)


def call(kernel, out_shape, *args, scalars=(), scratch=(), limit=8):
    args = [pltpu.with_memory_space_constraint(arg, pltpu.VMEM) for arg in args]
    space = pl.BlockSpec(memory_space=pltpu.VMEM)
    scalar = pl.BlockSpec(memory_space=pltpu.SMEM)
    return pl.pallas_call(
        kernel,
        out_shape=out_shape,
        in_specs=[scalar] * len(scalars) + [space] * len(args),
        out_specs=jax.tree.map(lambda _: space, out_shape),
        scratch_shapes=scratch,
        compiler_params=pltpu.CompilerParams(vmem_limit_bytes=limit * 1024 * 1024),
    )(*scalars, *args)


def per_device(diag_blocks, coupling, sources, requests):
    rows, size, cols = diag_blocks.shape[1], diag_blocks.shape[2], sources.shape[2]
    few = requests.shape[1]
    me = lax.axis_index("panel").astype(jnp.int32)
    plane = lax.axis_index("depth").astype(jnp.int32)[None]
    width = 2 * size + cols + LANES
    far = pl.BlockSpec(memory_space=pltpu.HBM)
    operands = (requests, diag_blocks[0], coupling[0], sources[0])
    scalar = pl.BlockSpec(memory_space=pltpu.SMEM)
    packed = pl.pallas_call(
        pack_kernel,
        out_shape=vmem((rows, width)),
        in_specs=[scalar, far, far, far, far],
        out_specs=pl.BlockSpec(memory_space=pltpu.VMEM),
        scratch_shapes=[pltpu.SMEM(requests.shape, jnp.int32), pltpu.SemaphoreType.DMA((4,))],
        compiler_params=pltpu.CompilerParams(vmem_limit_bytes=8 * 1024 * 1024),
    )(me[None], *[pltpu.with_memory_space_constraint(x, pltpu.HBM) for x in operands])
    pieces = gathered(packed)

    vec = vmem((8, size))
    mat = vmem((size, size), BF16)
    d_high, d_low, c_high, c_low, source, diag, wanted = call(
        functools.partial(first_kernel, size=size, cols=cols),
        (mat, mat, mat, mat, vec, vec, vmem((8, LANES))),
        *pieces,
        scalars=(me[None],), limit=12,
        scratch=[pltpu.VMEM((size, width - 2 * size), F32)],
    )
    mats = (d_high, d_low, c_high, c_low)

    last = 3
    lefts = []
    for k in range(last):
        carried = call(
            functools.partial(forward_kernel, k),
            vec, *mats, source, diag, *lefts[-1:], scalars=(plane,),
        )
        lefts.append(hop(carried, k, k + 1))
    right_hand, panel = call(
        functools.partial(turn_kernel, last),
        (vec, vec), d_high, d_low, source, diag, *lefts, scalars=(plane,),
    )
    aheads = []
    for k in range(last - 1, -1, -1):
        aheads.append(hop(panel, k + 1, k))
        if k > 0:
            panel = call(
                functools.partial(backward_kernel, k),
                vec, *mats, right_hand, diag, aheads[-1], scalars=(plane,),
            )
    send = call(
        functools.partial(last_kernel, last),
        vmem((size // rows, 8, LANES)),
        *mats, right_hand, diag, wanted, *aheads, scalars=(plane,),
    )
    got = lax.all_to_all(send, "panel", 0, 0, tiled=True).reshape(cols, LANES)
    panels, picked = call(
        unpack_kernel,
        (jax.ShapeDtypeStruct((rows, cols), F32), jax.ShapeDtypeStruct((few, cols), F32)),
        got,
    )
    return panels[None], picked[None]


def solution(mesh):
    placed = (
        P("depth", "panel", None),
        P("depth", "panel", None),
        P("depth", "panel", None),
        P("depth", "panel"),
    )
    return jax.shard_map(
        per_device,
        mesh=mesh,
        in_specs=placed,
        out_specs=(P("depth", "panel", None), P("depth", "panel", None)),
        check_vma=False,
    )
```

```python
import functools

import jax
import jax.numpy as jnp
from jax import lax
from jax.experimental import pallas as pl
from jax.experimental.pallas import tpu as pltpu
from jax.sharding import PartitionSpec as P

ITERS = 2
F32, BF16 = jnp.float32, jnp.bfloat16
LANES = 128

AXES = ((1, 3, 2), (4, 12, 8))
SIBLINGS = [(p, p ^ 1) for p in range(32)]


def from_partner(block, phase, number):
    pairs = [
        (yz * 2 + core, (yz ^ AXES[core ^ phase][number]) * 2 + core)
        for yz in range(16)
        for core in range(2)
    ]
    return lax.ppermute(block, "panel", pairs)


PIECES = (("A", None), ("B", None), ("A", 0), ("A", 1), ("B", 0), ("B", 1), ("A", 2), ("B", 2))


def offset_of(core, piece, unit):
    half, line = piece
    near = AXES[core]
    offset = ((0, near[0]) if half == "A" else (near[1], near[2]))[unit]
    return offset ^ (0 if line is None else AXES[1 - core][line])


def gathered(own):
    near, other, far = [from_partner(own, 0, number) for number in range(3)]
    own, near, other, far = lax.optimization_barrier((own, near, other, far))
    a = jnp.concatenate([own, near], 0)
    b = jnp.concatenate([other, far], 0)
    a0, a1 = from_partner(a, 1, 0), from_partner(a, 1, 1)
    b0, b1 = from_partner(b, 1, 0), from_partner(b, 1, 1)
    a2, b2 = from_partner(a1, 1, 0), from_partner(b0, 1, 1)
    pieces = [a, b, a0, a1, b0, b1, a2, b2]
    return pieces + [lax.ppermute(piece, "panel", SIBLINGS) for piece in pieces]


def split(x):
    high = x.astype(BF16)
    return high, (x - high.astype(F32)).astype(BF16)


def product(x, high_ref, low_ref, transposed=False):
    rows = x.shape[0]
    both = jnp.concatenate(split(x), 0)
    dims = (((1,), (1 if transposed else 0,)), ((), ()))
    first = lax.dot_general(both, high_ref[...], dims, preferred_element_type=F32)
    second = lax.dot_general(both, low_ref[...], dims, preferred_element_type=F32)
    total = first + second
    return total[:rows] + total[rows:]


def jacobi(right_hand, diag, d_high, d_low):
    iterate = right_hand / diag
    for _ in range(ITERS):
        image = product(iterate, d_high, d_low)
        iterate = iterate + (right_hand - image) / diag
    return iterate


def pack_kernel(where_ref, asked, diag_rows, coupling_rows, source_rows, packed, requests, sems):
    few = requests.shape[1]
    fetch = pltpu.make_async_copy(asked, requests, sems.at[3])
    fetch.start()
    count, size = diag_rows.shape
    cols = source_rows.shape[1]
    copies = []
    at = 0
    for number, rows in enumerate((diag_rows, coupling_rows, source_rows)):
        width = rows.shape[1]
        copies.append(
            pltpu.make_async_copy(rows, packed.at[:, at : at + width], sems.at[number])
        )
        copies[-1].start()
        at += width
    fetch.wait()
    row = lax.broadcasted_iota(jnp.int32, (count, LANES), 0)
    lane = lax.broadcasted_iota(jnp.int32, (count, LANES), 1)
    slots = jnp.zeros((count, LANES), F32)
    for k in range(few):
        here = (row == 0) & (lane == where_ref[0] * few + k)
        slots = jnp.where(here, requests[0, k].astype(F32), slots)
    packed[:, at:] = slots
    for copy in copies:
        copy.wait()


def first_kernel(where_ref, *refs, size, cols):
    pieces = refs[:16]
    d_high, d_low, c_high, c_low, source, diag, wanted, side = refs[16:]
    me = where_ref[0]
    core = lax.rem(me, 2)
    place = lax.div(me, 2)
    unit_rows = size // 32
    step = 16

    def move(piece, start, to):
        def body(i, _):
            rows = pl.ds(pl.multiple_of(to + i * step, step), step)
            held = piece.at[pl.ds(pl.multiple_of(start + i * step, step), step)]
            d_high[rows, :], d_low[rows, :] = split(held[:, 0:size])
            c_high[rows, :], c_low[rows, :] = split(held[:, size : 2 * size])
            side[rows, :] = held[:, 2 * size :]
            return 0

        lax.fori_loop(0, unit_rows // step, body, 0)

    for number in range(16):
        sibling = number // 8
        for unit in range(2):
            piece = PIECES[number % 8]
            offset = jnp.where(
                core == sibling, offset_of(0, piece, unit), offset_of(1, piece, unit)
            )
            owner = lax.bitwise_xor(place, offset) * 2 + lax.bitwise_xor(core, sibling)
            move(pieces[number], unit * unit_rows, owner * unit_rows)

    pick = lax.broadcasted_iota(jnp.int32, (8, cols), 1) == (
        lax.broadcasted_iota(jnp.int32, (8, cols), 0) + me * 8
    )
    own = lax.dot_general(
        pick.astype(F32),
        side[:, 0:cols],
        (((1,), (1,)), ((), ())),
        precision=lax.Precision.HIGHEST,
        preferred_element_type=F32,
    )
    source[...] = own
    eye = lax.broadcasted_iota(jnp.int32, (LANES, LANES), 0) == lax.broadcasted_iota(
        jnp.int32, (LANES, LANES), 1
    )
    for start in range(0, size, LANES):
        tiles = slice(start, start + LANES)
        tile = d_high[tiles, tiles].astype(F32) + d_low[tiles, tiles].astype(F32)
        line = jnp.sum(jnp.where(eye, tile, 0.0), axis=0, keepdims=True)
        diag[:, start : start + LANES] = jnp.broadcast_to(line, (8, LANES))
    line = jnp.sum(side[:, cols : cols + LANES], axis=0, keepdims=True)
    wanted[...] = jnp.broadcast_to(line, (8, LANES))


def hop(block, here, there):
    other = [k for k in range(4) if k not in (here, there)]
    route = [(here, there), (there, here), tuple(other), tuple(other[::-1])]
    return lax.ppermute(block, "depth", route)


def taken(plane, planes, refs):
    total = jnp.zeros_like(refs[0])
    for meant, ref in zip(planes, refs):
        total = jnp.where(plane == meant, ref[...], total)
    return total


def forward_kernel(stage, where_ref, d_high, d_low, c_high, c_low, source, diag, *refs):
    @pl.when(where_ref[1] == stage)
    def _():
        right_hand = source[...] - refs[0][...] if stage else source[...]
        forward = jacobi(right_hand, diag[...], d_high, d_low)
        refs[-1][...] = product(forward, c_high, c_low)


def turn_kernel(count, where_ref, d_high, d_low, source, diag, *refs):
    right_hand = source[...] - taken(where_ref[1], range(1, count + 1), refs[:count])
    refs[count][...] = right_hand

    @pl.when(where_ref[1] == count)
    def _():
        refs[count + 1][...] = jacobi(right_hand, diag[...], d_high, d_low)


def backward_kernel(plane, where_ref, d_high, d_low, c_high, c_low, right_hand, diag, ahead, panel):
    @pl.when(where_ref[1] == plane)
    def _():
        rest = right_hand[...] - product(ahead[...], c_high, c_low, True)
        panel[...] = jacobi(rest, diag[...], d_high, d_low)


def last_kernel(count, where_ref, d_high, d_low, c_high, c_low, right_hand, diag, wanted, *refs):
    ahead = taken(where_ref[1], range(count - 1, -1, -1), refs[:count])
    rest = right_hand[...] - product(ahead, c_high, c_low, True)
    panel = jacobi(rest, diag[...], d_high, d_low)
    size = panel.shape[1]
    high = panel.astype(BF16)
    rest = panel - high.astype(F32)
    middle = rest.astype(BF16)
    low = (rest - middle.astype(F32)).astype(BF16)
    line = wanted[0:1, :].astype(jnp.int32)
    chosen = (lax.broadcasted_iota(jnp.int32, (size, LANES), 0) == line).astype(BF16)
    parts = [jnp.dot(part, chosen, preferred_element_type=F32) for part in (high, middle, low)]
    picked = parts[0] + parts[1] + parts[2]
    send = refs[count]
    blocks = send.shape[0]
    own, few = size // blocks, LANES // blocks
    filler = jnp.zeros((8, LANES - own - few), F32)
    for block in range(blocks):
        send[block] = jnp.concatenate(
            [
                panel[:, block * own : (block + 1) * own],
                picked[:, block * few : (block + 1) * few],
                filler,
            ],
            1,
        )


def unpack_kernel(got, panels, picked):
    turned = got[...].T
    own = panels.shape[0]
    panels[...] = turned[:own]
    picked[...] = turned[own : own + picked.shape[0]]


def vmem(shape, dtype=F32):
    return pltpu.VMEM(shape, dtype)


def call(kernel, out_shape, *args, scalars=(), scratch=(), limit=8):
    args = [pltpu.with_memory_space_constraint(arg, pltpu.VMEM) for arg in args]
    space = pl.BlockSpec(memory_space=pltpu.VMEM)
    scalar = pl.BlockSpec(memory_space=pltpu.SMEM)
    return pl.pallas_call(
        kernel,
        out_shape=out_shape,
        in_specs=[scalar] * len(scalars) + [space] * len(args),
        out_specs=jax.tree.map(lambda _: space, out_shape),
        scratch_shapes=scratch,
        compiler_params=pltpu.CompilerParams(vmem_limit_bytes=limit * 1024 * 1024),
    )(*scalars, *args)


def per_device(diag_blocks, coupling, sources, requests):
    rows, size, cols = diag_blocks.shape[1], diag_blocks.shape[2], sources.shape[2]
    few = requests.shape[1]
    where = jnp.stack([lax.axis_index("panel"), lax.axis_index("depth")]).astype(jnp.int32)
    width = 2 * size + cols + LANES
    far = pl.BlockSpec(memory_space=pltpu.HBM)
    operands = (requests, diag_blocks[0], coupling[0], sources[0])
    scalar = pl.BlockSpec(memory_space=pltpu.SMEM)
    packed = pl.pallas_call(
        pack_kernel,
        out_shape=vmem((rows, width)),
        in_specs=[scalar, far, far, far, far],
        out_specs=pl.BlockSpec(memory_space=pltpu.VMEM),
        scratch_shapes=[pltpu.SMEM(requests.shape, jnp.int32), pltpu.SemaphoreType.DMA((4,))],
        compiler_params=pltpu.CompilerParams(vmem_limit_bytes=8 * 1024 * 1024),
    )(where, *[pltpu.with_memory_space_constraint(x, pltpu.HBM) for x in operands])
    pieces = gathered(packed)

    vec = vmem((8, size))
    mat = vmem((size, size), BF16)
    d_high, d_low, c_high, c_low, source, diag, wanted = call(
        functools.partial(first_kernel, size=size, cols=cols),
        (mat, mat, mat, mat, vec, vec, vmem((8, LANES))),
        *pieces,
        scalars=(where,),
        scratch=[pltpu.VMEM((size, width - 2 * size), F32)],
    )
    mats = (d_high, d_low, c_high, c_low)

    last = 3
    lefts = []
    for k in range(last):
        carried = call(
            functools.partial(forward_kernel, k),
            vec, *mats, source, diag, *lefts[-1:], scalars=(where,),
        )
        lefts.append(hop(carried, k, k + 1))
    right_hand, panel = call(
        functools.partial(turn_kernel, last),
        (vec, vec), d_high, d_low, source, diag, *lefts, scalars=(where,),
    )
    aheads = []
    for k in range(last - 1, -1, -1):
        aheads.append(hop(panel, k + 1, k))
        if k > 0:
            panel = call(
                functools.partial(backward_kernel, k),
                vec, *mats, right_hand, diag, aheads[-1], scalars=(where,),
            )
    send = call(
        functools.partial(last_kernel, last),
        vmem((size // rows, 8, LANES)),
        *mats, right_hand, diag, wanted, *aheads, scalars=(where,),
    )
    got = lax.all_to_all(send, "panel", 0, 0, tiled=True).reshape(cols, LANES)
    panels, picked = call(
        unpack_kernel,
        (jax.ShapeDtypeStruct((rows, cols), F32), jax.ShapeDtypeStruct((few, cols), F32)),
        got,
    )
    return panels[None], picked[None]


def solution(mesh):
    placed = (
        P("depth", "panel", None),
        P("depth", "panel", None),
        P("depth", "panel", None),
        P("depth", "panel"),
    )
    return jax.shard_map(
        per_device,
        mesh=mesh,
        in_specs=placed,
        out_specs=(P("depth", "panel", None), P("depth", "panel", None)),
        check_vma=False,
    )
```

```python
import functools

import jax
import jax.numpy as jnp
from jax import lax
from jax.experimental import pallas as pl
from jax.experimental.pallas import tpu as pltpu
from jax.sharding import PartitionSpec as P

ITERS = 2
F32, BF16 = jnp.float32, jnp.bfloat16
LANES = 128

AXES = ((1, 3, 2), (4, 12, 8))
SIBLINGS = [(p, p ^ 1) for p in range(32)]


def from_partner(block, phase, number):
    pairs = [
        (yz * 2 + core, (yz ^ AXES[core ^ phase][number]) * 2 + core)
        for yz in range(16)
        for core in range(2)
    ]
    return lax.ppermute(block, "panel", pairs)


PIECES = (("A", None), ("B", None), ("A", 0), ("A", 1), ("B", 0), ("B", 1), ("A", 2), ("B", 2))


def offset_of(core, piece, unit):
    half, line = piece
    near = AXES[core]
    offset = ((0, near[0]) if half == "A" else (near[1], near[2]))[unit]
    return offset ^ (0 if line is None else AXES[1 - core][line])


def gathered(own):
    near, other, far = [from_partner(own, 0, number) for number in range(3)]
    own, near, other, far = lax.optimization_barrier((own, near, other, far))
    a = jnp.concatenate([own, near], 0)
    b = jnp.concatenate([other, far], 0)
    a0, a1 = from_partner(a, 1, 0), from_partner(a, 1, 1)
    b0, b1 = from_partner(b, 1, 0), from_partner(b, 1, 1)
    a2, b2 = from_partner(a1, 1, 0), from_partner(b0, 1, 1)
    pieces = [a, b, a0, a1, b0, b1, a2, b2]
    return pieces + [lax.ppermute(piece, "panel", SIBLINGS) for piece in pieces]


def split(x):
    high = x.astype(BF16)
    return high, (x - high.astype(F32)).astype(BF16)


def product(x, high_ref, low_ref, transposed=False):
    rows = x.shape[0]
    both = jnp.concatenate(split(x), 0)
    dims = (((1,), (1 if transposed else 0,)), ((), ()))
    first = lax.dot_general(both, high_ref[...], dims, preferred_element_type=F32)
    second = lax.dot_general(both, low_ref[...], dims, preferred_element_type=F32)
    total = first + second
    return total[:rows] + total[rows:]


def jacobi(right_hand, diag, d_high, d_low):
    iterate = right_hand / diag
    for _ in range(ITERS):
        image = product(iterate, d_high, d_low)
        iterate = iterate + (right_hand - image) / diag
    return iterate


def pack_kernel(asked, diag_rows, coupling_rows, source_rows, packed, requests, sems):
    few = requests.shape[1]
    fetch = pltpu.make_async_copy(asked, requests, sems.at[3])
    fetch.start()
    count, size = diag_rows.shape
    cols = source_rows.shape[1]
    copies = []
    at = 0
    for number, rows in enumerate((diag_rows, coupling_rows, source_rows)):
        width = rows.shape[1]
        copies.append(
            pltpu.make_async_copy(rows, packed.at[:, at : at + width], sems.at[number])
        )
        copies[-1].start()
        at += width
    fetch.wait()
    row = lax.broadcasted_iota(jnp.int32, (count, LANES), 0)
    lane = lax.broadcasted_iota(jnp.int32, (count, LANES), 1)
    slots = jnp.zeros((count, LANES), F32)
    for k in range(few):
        here = (row == 0) & (lane == lax.axis_index("panel") * few + k)
        slots = jnp.where(here, requests[0, k].astype(F32), slots)
    packed[:, at:] = slots
    for copy in copies:
        copy.wait()


def first_kernel(*refs, size, cols):
    pieces = refs[:16]
    d_high, d_low, c_high, c_low, source, diag, wanted, side = refs[16:]
    me = lax.axis_index("panel")
    core = lax.rem(me, 2)
    place = lax.div(me, 2)
    unit_rows = size // 32
    step = 16

    def move(piece, start, to):
        def body(i, _):
            rows = pl.ds(pl.multiple_of(to + i * step, step), step)
            held = piece.at[pl.ds(pl.multiple_of(start + i * step, step), step)]
            d_high[rows, :], d_low[rows, :] = split(held[:, 0:size])
            c_high[rows, :], c_low[rows, :] = split(held[:, size : 2 * size])
            side[rows, :] = held[:, 2 * size :]
            return 0

        lax.fori_loop(0, unit_rows // step, body, 0)

    for number in range(16):
        sibling = number // 8
        for unit in range(2):
            piece = PIECES[number % 8]
            offset = jnp.where(
                core == sibling, offset_of(0, piece, unit), offset_of(1, piece, unit)
            )
            owner = lax.bitwise_xor(place, offset) * 2 + lax.bitwise_xor(core, sibling)
            move(pieces[number], unit * unit_rows, owner * unit_rows)

    pick = lax.broadcasted_iota(jnp.int32, (8, cols), 1) == (
        lax.broadcasted_iota(jnp.int32, (8, cols), 0) + me * 8
    )
    own = lax.dot_general(
        pick.astype(F32),
        side[:, 0:cols],
        (((1,), (1,)), ((), ())),
        precision=lax.Precision.HIGHEST,
        preferred_element_type=F32,
    )
    source[...] = own
    eye = lax.broadcasted_iota(jnp.int32, (LANES, LANES), 0) == lax.broadcasted_iota(
        jnp.int32, (LANES, LANES), 1
    )
    for start in range(0, size, LANES):
        tiles = slice(start, start + LANES)
        tile = d_high[tiles, tiles].astype(F32) + d_low[tiles, tiles].astype(F32)
        line = jnp.sum(jnp.where(eye, tile, 0.0), axis=0, keepdims=True)
        diag[:, start : start + LANES] = jnp.broadcast_to(line, (8, LANES))
    line = jnp.sum(side[:, cols : cols + LANES], axis=0, keepdims=True)
    wanted[...] = jnp.broadcast_to(line, (8, LANES))


def hop(block, here, there):
    other = [k for k in range(4) if k not in (here, there)]
    route = [(here, there), (there, here), tuple(other), tuple(other[::-1])]
    return lax.ppermute(block, "depth", route)


def taken(plane, planes, refs):
    total = jnp.zeros_like(refs[0])
    for meant, ref in zip(planes, refs):
        total = jnp.where(plane == meant, ref[...], total)
    return total


def forward_kernel(stage, d_high, d_low, c_high, c_low, source, diag, *refs):
    @pl.when(lax.axis_index("depth") == stage)
    def _():
        right_hand = source[...] - refs[0][...] if stage else source[...]
        forward = jacobi(right_hand, diag[...], d_high, d_low)
        refs[-1][...] = product(forward, c_high, c_low)


def turn_kernel(count, d_high, d_low, source, diag, *refs):
    right_hand = source[...] - taken(lax.axis_index("depth"), range(1, count + 1), refs[:count])
    refs[count][...] = right_hand

    @pl.when(lax.axis_index("depth") == count)
    def _():
        refs[count + 1][...] = jacobi(right_hand, diag[...], d_high, d_low)


def backward_kernel(plane, d_high, d_low, c_high, c_low, right_hand, diag, ahead, panel):
    @pl.when(lax.axis_index("depth") == plane)
    def _():
        rest = right_hand[...] - product(ahead[...], c_high, c_low, True)
        panel[...] = jacobi(rest, diag[...], d_high, d_low)


def last_kernel(count, d_high, d_low, c_high, c_low, right_hand, diag, wanted, *refs):
    ahead = taken(lax.axis_index("depth"), range(count - 1, -1, -1), refs[:count])
    rest = right_hand[...] - product(ahead, c_high, c_low, True)
    panel = jacobi(rest, diag[...], d_high, d_low)
    size = panel.shape[1]
    high = panel.astype(BF16)
    rest = panel - high.astype(F32)
    middle = rest.astype(BF16)
    low = (rest - middle.astype(F32)).astype(BF16)
    line = wanted[0:1, :].astype(jnp.int32)
    chosen = (lax.broadcasted_iota(jnp.int32, (size, LANES), 0) == line).astype(BF16)
    parts = [jnp.dot(part, chosen, preferred_element_type=F32) for part in (high, middle, low)]
    picked = parts[0] + parts[1] + parts[2]
    send = refs[count]
    blocks = send.shape[0]
    own, few = size // blocks, LANES // blocks
    filler = jnp.zeros((8, LANES - own - few), F32)
    for block in range(blocks):
        send[block] = jnp.concatenate(
            [
                panel[:, block * own : (block + 1) * own],
                picked[:, block * few : (block + 1) * few],
                filler,
            ],
            1,
        )


def unpack_kernel(got, panels, picked):
    turned = got[...].T
    own = panels.shape[0]
    panels[...] = turned[:own]
    picked[...] = turned[own : own + picked.shape[0]]


def vmem(shape, dtype=F32):
    return pltpu.VMEM(shape, dtype)


def call(kernel, out_shape, *args, scratch=(), limit=8):
    args = [pltpu.with_memory_space_constraint(arg, pltpu.VMEM) for arg in args]
    space = pl.BlockSpec(memory_space=pltpu.VMEM)
    return pl.pallas_call(
        kernel,
        out_shape=out_shape,
        in_specs=[space] * len(args),
        out_specs=jax.tree.map(lambda _: space, out_shape),
        scratch_shapes=scratch,
        compiler_params=pltpu.CompilerParams(vmem_limit_bytes=limit * 1024 * 1024),
    )(*args)


def per_device(diag_blocks, coupling, sources, requests):
    rows, size, cols = diag_blocks.shape[1], diag_blocks.shape[2], sources.shape[2]
    few = requests.shape[1]
    width = 2 * size + cols + LANES
    far = pl.BlockSpec(memory_space=pltpu.HBM)
    operands = (requests, diag_blocks[0], coupling[0], sources[0])
    packed = pl.pallas_call(
        pack_kernel,
        out_shape=vmem((rows, width)),
        in_specs=[far] * 4,
        out_specs=pl.BlockSpec(memory_space=pltpu.VMEM),
        scratch_shapes=[pltpu.SMEM(requests.shape, jnp.int32), pltpu.SemaphoreType.DMA((4,))],
        compiler_params=pltpu.CompilerParams(vmem_limit_bytes=8 * 1024 * 1024),
    )(*[pltpu.with_memory_space_constraint(x, pltpu.HBM) for x in operands])
    pieces = gathered(packed)

    vec = vmem((8, size))
    mat = vmem((size, size), BF16)
    d_high, d_low, c_high, c_low, source, diag, wanted = call(
        functools.partial(first_kernel, size=size, cols=cols),
        (mat, mat, mat, mat, vec, vec, vmem((8, LANES))),
        *pieces,

        scratch=[pltpu.VMEM((size, width - 2 * size), F32)],
    )
    mats = (d_high, d_low, c_high, c_low)

    last = 3
    lefts = []
    for k in range(last):
        carried = call(
            functools.partial(forward_kernel, k),
            vec, *mats, source, diag, *lefts[-1:],
        )
        lefts.append(hop(carried, k, k + 1))
    right_hand, panel = call(
        functools.partial(turn_kernel, last),
        (vec, vec), d_high, d_low, source, diag, *lefts,
    )
    aheads = []
    for k in range(last - 1, -1, -1):
        aheads.append(hop(panel, k + 1, k))
        if k > 0:
            panel = call(
                functools.partial(backward_kernel, k),
                vec, *mats, right_hand, diag, aheads[-1],
            )
    send = call(
        functools.partial(last_kernel, last),
        vmem((size // rows, 8, LANES)),
        *mats, right_hand, diag, wanted, *aheads,
    )
    got = lax.all_to_all(send, "panel", 0, 0, tiled=True).reshape(cols, LANES)
    panels, picked = call(
        unpack_kernel,
        (jax.ShapeDtypeStruct((rows, cols), F32), jax.ShapeDtypeStruct((few, cols), F32)),
        got,
    )
    return panels[None], picked[None]


def solution(mesh):
    placed = (
        P("depth", "panel", None),
        P("depth", "panel", None),
        P("depth", "panel", None),
        P("depth", "panel"),
    )
    return jax.shard_map(
        per_device,
        mesh=mesh,
        in_specs=placed,
        out_specs=(P("depth", "panel", None), P("depth", "panel", None)),
        check_vma=False,
    )
```

```python
import functools

import jax
import jax.numpy as jnp
from jax import lax
from jax.experimental import pallas as pl
from jax.experimental.pallas import tpu as pltpu
from jax.sharding import PartitionSpec as P

ITERS = 2
F32, BF16 = jnp.float32, jnp.bfloat16
LANES = 128
SENT_GROUPS = 5

AXES = ((1, 3, 2), (4, 12, 8))
SIBLINGS = [(p, p ^ 1) for p in range(32)]


def from_partner(block, phase, number):
    pairs = [
        (yz * 2 + core, (yz ^ AXES[core ^ phase][number]) * 2 + core)
        for yz in range(16)
        for core in range(2)
    ]
    return lax.ppermute(block, "panel", pairs)


PIECES = (("A", None), ("B", None), ("A", 0), ("A", 1), ("B", 0), ("B", 1), ("A", 2), ("B", 2))


def offset_of(core, piece, unit):
    half, line = piece
    near = AXES[core]
    offset = ((0, near[0]) if half == "A" else (near[1], near[2]))[unit]
    return offset ^ (0 if line is None else AXES[1 - core][line])


def gathered(own):
    near, other, far = [from_partner(own, 0, number) for number in range(3)]
    a = jnp.concatenate([own, near], 0)
    b = jnp.concatenate([other, far], 0)
    a0, a1 = from_partner(a, 1, 0), from_partner(a, 1, 1)
    b0, b1 = from_partner(b, 1, 0), from_partner(b, 1, 1)
    a2, b2 = from_partner(a1, 1, 0), from_partner(b0, 1, 1)
    pieces = [a, b, a0, a1, b0, b1, a2, b2]
    return pieces + [lax.ppermute(piece, "panel", SIBLINGS) for piece in pieces]


def split(x):
    high = x.astype(BF16)
    return high, (x - high.astype(F32)).astype(BF16)


def product(x, high_ref, low_ref, transposed=False):
    rows = x.shape[0]
    both = jnp.concatenate(split(x), 0)
    dims = (((1,), (1 if transposed else 0,)), ((), ()))
    first = lax.dot_general(both, high_ref[...], dims, preferred_element_type=F32)
    second = lax.dot_general(both, low_ref[...], dims, preferred_element_type=F32)
    total = first + second
    return total[:rows] + total[rows:]


def jacobi(right_hand, diag, d_high, d_low):
    iterate = right_hand / diag
    for _ in range(ITERS):
        image = product(iterate, d_high, d_low)
        iterate = iterate + (right_hand - image) / diag
    return iterate


def pack_kernel(asked, diag_rows, coupling_rows, source_rows, packed, requests, sems):
    few = requests.shape[1]
    fetch = pltpu.make_async_copy(asked, requests, sems.at[2 + SENT_GROUPS])
    fetch.start()
    count, size = diag_rows.shape
    cols = source_rows.shape[1]
    sent = [(coupling_rows, size), (source_rows, cols)]
    group = lax.div(lax.axis_index("panel") * count, LANES)
    for k in range(SENT_GROUPS):
        start = lax.rem(group + k, size // LANES) * LANES
        sent.append((diag_rows.at[:, pl.ds(pl.multiple_of(start, LANES), LANES)], LANES))
    copies = []
    at = 0
    for number, (rows, width) in enumerate(sent):
        copies.append(
            pltpu.make_async_copy(rows, packed.at[:, at : at + width], sems.at[number])
        )
        copies[-1].start()
        at += width
    fetch.wait()
    row = lax.broadcasted_iota(jnp.int32, (count, LANES), 0)
    lane = lax.broadcasted_iota(jnp.int32, (count, LANES), 1)
    slots = jnp.zeros((count, LANES), F32)
    for k in range(few):
        here = (row == 0) & (lane == lax.axis_index("panel") * few + k)
        slots = jnp.where(here, requests[0, k].astype(F32), slots)
    packed[:, at:] = slots
    for copy in copies:
        copy.wait()


def first_kernel(*refs, size, cols):
    pieces = refs[:16]
    d_high, d_low, c_high, c_low, source, diag, wanted, side = refs[16:]
    me = lax.axis_index("panel")
    core = lax.rem(me, 2)
    place = lax.div(me, 2)
    unit_rows = size // 32
    step = 16
    groups = size // LANES

    def move(piece, start, to):
        def body(i, _):
            rows = pl.ds(pl.multiple_of(to + i * step, step), step)
            held = piece.at[pl.ds(pl.multiple_of(start + i * step, step), step)]
            c_high[rows, :], c_low[rows, :] = split(held[:, 0:size])
            side[rows, 0:cols] = held[:, size : size + cols]
            for k in range(SENT_GROUPS):
                at = lax.rem(lax.div(to, LANES) + k, groups) * LANES
                where = pl.ds(pl.multiple_of(at, LANES), LANES)
                own = size + cols + k * LANES
                d_high[rows, where], d_low[rows, where] = split(held[:, own : own + LANES])
            side[rows, cols:] = held[:, size + cols + SENT_GROUPS * LANES :]
            return 0

        lax.fori_loop(0, unit_rows // step, body, 0)

    for number in range(16):
        sibling = number // 8
        for unit in range(2):
            piece = PIECES[number % 8]
            offset = jnp.where(
                core == sibling, offset_of(0, piece, unit), offset_of(1, piece, unit)
            )
            owner = lax.bitwise_xor(place, offset) * 2 + lax.bitwise_xor(core, sibling)
            move(pieces[number], unit * unit_rows, owner * unit_rows)

    for group in range(groups):
        for k in range(1, groups - SENT_GROUPS + 1):
            rows = slice(group * LANES, (group + 1) * LANES)
            where = (group + k) % groups * LANES
            where = slice(where, where + LANES)
            block = d_high[rows, where].astype(F32) + d_low[rows, where].astype(F32)
            d_high[where, rows], d_low[where, rows] = split(block.T)

    pick = lax.broadcasted_iota(jnp.int32, (8, cols), 1) == (
        lax.broadcasted_iota(jnp.int32, (8, cols), 0) + me * 8
    )
    own = lax.dot_general(
        pick.astype(F32),
        side[:, 0:cols],
        (((1,), (1,)), ((), ())),
        precision=lax.Precision.HIGHEST,
        preferred_element_type=F32,
    )
    source[...] = own
    eye = lax.broadcasted_iota(jnp.int32, (LANES, LANES), 0) == lax.broadcasted_iota(
        jnp.int32, (LANES, LANES), 1
    )
    for start in range(0, size, LANES):
        tiles = slice(start, start + LANES)
        tile = d_high[tiles, tiles].astype(F32) + d_low[tiles, tiles].astype(F32)
        line = jnp.sum(jnp.where(eye, tile, 0.0), axis=0, keepdims=True)
        diag[:, start : start + LANES] = jnp.broadcast_to(line, (8, LANES))
    line = jnp.sum(side[:, cols : cols + LANES], axis=0, keepdims=True)
    wanted[...] = jnp.broadcast_to(line, (8, LANES))


def hop(block, here, there):
    other = [k for k in range(4) if k not in (here, there)]
    route = [(here, there), (there, here), tuple(other), tuple(other[::-1])]
    return lax.ppermute(block, "depth", route)


def taken(plane, planes, refs):
    total = jnp.zeros_like(refs[0])
    for meant, ref in zip(planes, refs):
        total = jnp.where(plane == meant, ref[...], total)
    return total


def forward_kernel(stage, d_high, d_low, c_high, c_low, source, diag, *refs):
    @pl.when(lax.axis_index("depth") == stage)
    def _():
        right_hand = source[...] - refs[0][...] if stage else source[...]
        forward = jacobi(right_hand, diag[...], d_high, d_low)
        refs[-1][...] = product(forward, c_high, c_low)


def turn_kernel(count, d_high, d_low, source, diag, *refs):
    right_hand = source[...] - taken(lax.axis_index("depth"), range(1, count + 1), refs[:count])
    refs[count][...] = right_hand

    @pl.when(lax.axis_index("depth") == count)
    def _():
        refs[count + 1][...] = jacobi(right_hand, diag[...], d_high, d_low)


def backward_kernel(plane, d_high, d_low, c_high, c_low, right_hand, diag, ahead, panel):
    @pl.when(lax.axis_index("depth") == plane)
    def _():
        rest = right_hand[...] - product(ahead[...], c_high, c_low, True)
        panel[...] = jacobi(rest, diag[...], d_high, d_low)


def last_kernel(count, d_high, d_low, c_high, c_low, right_hand, diag, wanted, *refs):
    ahead = taken(lax.axis_index("depth"), range(count - 1, -1, -1), refs[:count])
    rest = right_hand[...] - product(ahead, c_high, c_low, True)
    panel = jacobi(rest, diag[...], d_high, d_low)
    size = panel.shape[1]
    high = panel.astype(BF16)
    rest = panel - high.astype(F32)
    middle = rest.astype(BF16)
    low = (rest - middle.astype(F32)).astype(BF16)
    line = wanted[0:1, :].astype(jnp.int32)
    chosen = (lax.broadcasted_iota(jnp.int32, (size, LANES), 0) == line).astype(BF16)
    parts = [jnp.dot(part, chosen, preferred_element_type=F32) for part in (high, middle, low)]
    picked = parts[0] + parts[1] + parts[2]
    send = refs[count]
    blocks = send.shape[0]
    own, few = size // blocks, LANES // blocks
    filler = jnp.zeros((8, LANES - own - few), F32)
    for block in range(blocks):
        send[block] = jnp.concatenate(
            [
                panel[:, block * own : (block + 1) * own],
                picked[:, block * few : (block + 1) * few],
                filler,
            ],
            1,
        )


def unpack_kernel(got, panels, picked):
    turned = got[...].T
    own = panels.shape[0]
    panels[...] = turned[:own]
    picked[...] = turned[own : own + picked.shape[0]]


def vmem(shape, dtype=F32):
    return pltpu.VMEM(shape, dtype)


def call(kernel, out_shape, *args, scratch=(), limit=8):
    args = [pltpu.with_memory_space_constraint(arg, pltpu.VMEM) for arg in args]
    space = pl.BlockSpec(memory_space=pltpu.VMEM)
    return pl.pallas_call(
        kernel,
        out_shape=out_shape,
        in_specs=[space] * len(args),
        out_specs=jax.tree.map(lambda _: space, out_shape),
        scratch_shapes=scratch,
        compiler_params=pltpu.CompilerParams(vmem_limit_bytes=limit * 1024 * 1024),
    )(*args)


def per_device(diag_blocks, coupling, sources, requests):
    rows, size, cols = diag_blocks.shape[1], diag_blocks.shape[2], sources.shape[2]
    few = requests.shape[1]
    width = size + cols + (SENT_GROUPS + 1) * LANES
    far = pl.BlockSpec(memory_space=pltpu.HBM)
    operands = (requests, diag_blocks[0], coupling[0], sources[0])
    packed = pl.pallas_call(
        pack_kernel,
        out_shape=vmem((rows, width)),
        in_specs=[far] * 4,
        out_specs=pl.BlockSpec(memory_space=pltpu.VMEM),
        scratch_shapes=[pltpu.SMEM(requests.shape, jnp.int32), pltpu.SemaphoreType.DMA((3 + SENT_GROUPS,))],
        compiler_params=pltpu.CompilerParams(vmem_limit_bytes=8 * 1024 * 1024),
    )(*[pltpu.with_memory_space_constraint(x, pltpu.HBM) for x in operands])
    pieces = gathered(packed)

    vec = vmem((8, size))
    mat = vmem((size, size), BF16)
    d_high, d_low, c_high, c_low, source, diag, wanted = call(
        functools.partial(first_kernel, size=size, cols=cols),
        (mat, mat, mat, mat, vec, vec, vmem((8, LANES))),
        *pieces,

        scratch=[pltpu.VMEM((size, cols + LANES), F32)],
    )
    mats = (d_high, d_low, c_high, c_low)

    last = 3
    lefts = []
    for k in range(last):
        carried = call(
            functools.partial(forward_kernel, k),
            vec, *mats, source, diag, *lefts[-1:],
        )
        lefts.append(hop(carried, k, k + 1))
    right_hand, panel = call(
        functools.partial(turn_kernel, last),
        (vec, vec), d_high, d_low, source, diag, *lefts,
    )
    aheads = []
    for k in range(last - 1, -1, -1):
        aheads.append(hop(panel, k + 1, k))
        if k > 0:
            panel = call(
                functools.partial(backward_kernel, k),
                vec, *mats, right_hand, diag, aheads[-1],
            )
    send = call(
        functools.partial(last_kernel, last),
        vmem((size // rows, 8, LANES)),
        *mats, right_hand, diag, wanted, *aheads,
    )
    got = lax.all_to_all(send, "panel", 0, 0, tiled=True).reshape(cols, LANES)
    panels, picked = call(
        unpack_kernel,
        (jax.ShapeDtypeStruct((rows, cols), F32), jax.ShapeDtypeStruct((few, cols), F32)),
        got,
    )
    return panels[None], picked[None]


def solution(mesh):
    placed = (
        P("depth", "panel", None),
        P("depth", "panel", None),
        P("depth", "panel", None),
        P("depth", "panel"),
    )
    return jax.shard_map(
        per_device,
        mesh=mesh,
        in_specs=placed,
        out_specs=(P("depth", "panel", None), P("depth", "panel", None)),
        check_vma=False,
    )
```

```python
import functools

import jax
import jax.numpy as jnp
from jax import lax
from jax.experimental import pallas as pl
from jax.experimental.pallas import tpu as pltpu
from jax.sharding import PartitionSpec as P


ITERS = 2
F32, BF16 = jnp.float32, jnp.bfloat16
LANES = 128
SENT_GROUPS = 5

AXES = ((1, 3, 2), (4, 12, 8))
SIBLINGS = [(p, p ^ 1) for p in range(32)]


def from_partner(block, phase, number):
    pairs = [
        (yz * 2 + core, (yz ^ AXES[core ^ phase][number]) * 2 + core)
        for yz in range(16)
        for core in range(2)
    ]
    return lax.ppermute(block, "panel", pairs)


def join_kernel(first, second, both):
    rows = first.shape[0]
    both[:rows] = first[...]
    both[rows:] = second[...]


def joined(first, second):
    return call(join_kernel, vmem((first.shape[0] * 2, first.shape[1])), first, second)


PIECES = (("A", None), ("B", None), ("A", 0), ("A", 1), ("B", 0), ("B", 1), ("A", 2), ("B", 2))


def offset_of(core, piece, unit):
    half, line = piece
    near = AXES[core]
    offset = ((0, near[0]) if half == "A" else (near[1], near[2]))[unit]
    return offset ^ (0 if line is None else AXES[1 - core][line])


def gathered(own):
    near = from_partner(own, 0, 0)
    other = from_partner(own, 0, 1)
    far = from_partner(own, 0, 2)
    a = joined(own, near)
    a1, a0 = from_partner(a, 1, 1), from_partner(a, 1, 0)
    b = joined(other, far)
    b0, b1 = from_partner(b, 1, 0), from_partner(b, 1, 1)
    a2, b2 = from_partner(a1, 1, 0), from_partner(b0, 1, 1)
    pieces = [a, b, a0, a1, b0, b1, a2, b2]
    return pieces + [lax.ppermute(piece, "panel", SIBLINGS) for piece in pieces]


def split(x):
    high = x.astype(BF16)
    return high, (x - high.astype(F32)).astype(BF16)


def product(x, high_ref, low_ref, transposed=False):
    rows = x.shape[0]
    both = jnp.concatenate(split(x), 0)
    dims = (((1,), (1 if transposed else 0,)), ((), ()))
    first = lax.dot_general(both, high_ref[...], dims, preferred_element_type=F32)
    second = lax.dot_general(both, low_ref[...], dims, preferred_element_type=F32)
    total = first + second
    return total[:rows] + total[rows:]


def jacobi(right_hand, diag, d_high, d_low):
    iterate = right_hand / diag
    for _ in range(ITERS):
        image = product(iterate, d_high, d_low)
        iterate = iterate + (right_hand - image) / diag
    return iterate


def pack_kernel(asked, diag_rows, coupling_rows, source_rows, packed, requests, sems):
    few = requests.shape[1]
    fetch = pltpu.make_async_copy(asked, requests, sems.at[2 + SENT_GROUPS])
    fetch.start()
    count, size = diag_rows.shape
    cols = source_rows.shape[1]
    sent = [(coupling_rows, size), (source_rows, cols)]
    group = lax.div(lax.axis_index("panel") * count, LANES)
    for k in range(SENT_GROUPS):
        start = lax.rem(group + k, size // LANES) * LANES
        sent.append((diag_rows.at[:, pl.ds(pl.multiple_of(start, LANES), LANES)], LANES))
    copies = []
    at = 0
    for number, (rows, width) in enumerate(sent):
        copies.append(
            pltpu.make_async_copy(rows, packed.at[:, at : at + width], sems.at[number])
        )
        copies[-1].start()
        at += width
    fetch.wait()
    row = lax.broadcasted_iota(jnp.int32, (count, LANES), 0)
    lane = lax.broadcasted_iota(jnp.int32, (count, LANES), 1)
    slots = jnp.zeros((count, LANES), F32)
    for k in range(few):
        here = (row == 0) & (lane == lax.axis_index("panel") * few + k)
        slots = jnp.where(here, requests[0, k].astype(F32), slots)
    packed[:, at:] = slots
    for copy in copies:
        copy.wait()


def first_kernel(*refs, size, cols):
    pieces = refs[:16]
    d_high, d_low, c_high, c_low, source, diag, wanted, side = refs[16:]
    me = lax.axis_index("panel")
    core = lax.rem(me, 2)
    place = lax.div(me, 2)
    unit_rows = size // 32
    step = 16
    groups = size // LANES

    def move(piece, start, to):
        def body(i, _):
            rows = pl.ds(pl.multiple_of(to + i * step, step), step)
            held = piece.at[pl.ds(pl.multiple_of(start + i * step, step), step)]
            c_high[rows, :], c_low[rows, :] = split(held[:, 0:size])
            side[rows, 0:cols] = held[:, size : size + cols]
            for k in range(SENT_GROUPS):
                at = lax.rem(lax.div(to, LANES) + k, groups) * LANES
                where = pl.ds(pl.multiple_of(at, LANES), LANES)
                own = size + cols + k * LANES
                d_high[rows, where], d_low[rows, where] = split(held[:, own : own + LANES])
            side[rows, cols:] = held[:, size + cols + SENT_GROUPS * LANES :]
            return 0

        lax.fori_loop(0, unit_rows // step, body, 0)

    for number in range(16):
        sibling = number // 8
        for unit in range(2):
            piece = PIECES[number % 8]
            offset = jnp.where(
                core == sibling, offset_of(0, piece, unit), offset_of(1, piece, unit)
            )
            owner = lax.bitwise_xor(place, offset) * 2 + lax.bitwise_xor(core, sibling)
            move(pieces[number], unit * unit_rows, owner * unit_rows)

    for group in range(groups):
        for k in range(1, groups - SENT_GROUPS + 1):
            rows = slice(group * LANES, (group + 1) * LANES)
            where = (group + k) % groups * LANES
            where = slice(where, where + LANES)
            block = d_high[rows, where].astype(F32) + d_low[rows, where].astype(F32)
            d_high[where, rows], d_low[where, rows] = split(block.T)

    pick = lax.broadcasted_iota(jnp.int32, (8, cols), 1) == (
        lax.broadcasted_iota(jnp.int32, (8, cols), 0) + me * 8
    )
    own = lax.dot_general(
        pick.astype(F32),
        side[:, 0:cols],
        (((1,), (1,)), ((), ())),
        precision=lax.Precision.HIGHEST,
        preferred_element_type=F32,
    )
    source[...] = own
    eye = lax.broadcasted_iota(jnp.int32, (LANES, LANES), 0) == lax.broadcasted_iota(
        jnp.int32, (LANES, LANES), 1
    )
    for start in range(0, size, LANES):
        tiles = slice(start, start + LANES)
        tile = d_high[tiles, tiles].astype(F32) + d_low[tiles, tiles].astype(F32)
        line = jnp.sum(jnp.where(eye, tile, 0.0), axis=0, keepdims=True)
        diag[:, start : start + LANES] = jnp.broadcast_to(line, (8, LANES))
    line = jnp.sum(side[:, cols : cols + LANES], axis=0, keepdims=True)
    wanted[...] = jnp.broadcast_to(line, (8, LANES))


def hop(block, here, there):
    other = [k for k in range(4) if k not in (here, there)]
    route = [(here, there), (there, here), tuple(other), tuple(other[::-1])]
    return lax.ppermute(block, "depth", route)


def taken(plane, planes, refs):
    total = jnp.zeros_like(refs[0])
    for meant, ref in zip(planes, refs):
        total = jnp.where(plane == meant, ref[...], total)
    return total


def forward_kernel(stage, d_high, d_low, c_high, c_low, source, diag, *refs):
    @pl.when(lax.axis_index("depth") == stage)
    def _():
        right_hand = source[...] - refs[0][...] if stage else source[...]
        forward = jacobi(right_hand, diag[...], d_high, d_low)
        refs[-1][...] = product(forward, c_high, c_low)


def turn_kernel(count, d_high, d_low, source, diag, *refs):
    right_hand = source[...] - taken(lax.axis_index("depth"), range(1, count + 1), refs[:count])
    refs[count][...] = right_hand

    @pl.when(lax.axis_index("depth") == count)
    def _():
        refs[count + 1][...] = jacobi(right_hand, diag[...], d_high, d_low)


def backward_kernel(plane, d_high, d_low, c_high, c_low, right_hand, diag, ahead, panel):
    @pl.when(lax.axis_index("depth") == plane)
    def _():
        rest = right_hand[...] - product(ahead[...], c_high, c_low, True)
        panel[...] = jacobi(rest, diag[...], d_high, d_low)


def last_kernel(count, d_high, d_low, c_high, c_low, right_hand, diag, wanted, *refs):
    ahead = taken(lax.axis_index("depth"), range(count - 1, -1, -1), refs[:count])
    rest = right_hand[...] - product(ahead, c_high, c_low, True)
    panel = jacobi(rest, diag[...], d_high, d_low)
    size = panel.shape[1]
    high = panel.astype(BF16)
    rest = panel - high.astype(F32)
    middle = rest.astype(BF16)
    low = (rest - middle.astype(F32)).astype(BF16)
    line = wanted[0:1, :].astype(jnp.int32)
    chosen = (lax.broadcasted_iota(jnp.int32, (size, LANES), 0) == line).astype(BF16)
    parts = [jnp.dot(part, chosen, preferred_element_type=F32) for part in (high, middle, low)]
    picked = parts[0] + parts[1] + parts[2]
    send = refs[count]
    blocks = send.shape[0]
    own, few = size // blocks, LANES // blocks
    filler = jnp.zeros((8, LANES - own - few), F32)
    for block in range(blocks):
        send[block] = jnp.concatenate(
            [
                panel[:, block * own : (block + 1) * own],
                picked[:, block * few : (block + 1) * few],
                filler,
            ],
            1,
        )


def unpack_kernel(got, panels, picked):
    turned = got[...].T
    own = panels.shape[0]
    panels[...] = turned[:own]
    picked[...] = turned[own : own + picked.shape[0]]


def vmem(shape, dtype=F32):
    return pltpu.VMEM(shape, dtype)


def call(kernel, out_shape, *args, scratch=(), limit=8):
    args = [pltpu.with_memory_space_constraint(arg, pltpu.VMEM) for arg in args]
    space = pl.BlockSpec(memory_space=pltpu.VMEM)
    return pl.pallas_call(
        kernel,
        out_shape=out_shape,
        in_specs=[space] * len(args),
        out_specs=jax.tree.map(lambda _: space, out_shape),
        scratch_shapes=scratch,
        compiler_params=pltpu.CompilerParams(vmem_limit_bytes=limit * 1024 * 1024),
    )(*args)


def per_device(diag_blocks, coupling, sources, requests):
    rows, size, cols = diag_blocks.shape[1], diag_blocks.shape[2], sources.shape[2]
    few = requests.shape[1]
    width = size + cols + (SENT_GROUPS + 1) * LANES
    far = pl.BlockSpec(memory_space=pltpu.HBM)
    operands = (requests, diag_blocks[0], coupling[0], sources[0])
    packed = pl.pallas_call(
        pack_kernel,
        out_shape=vmem((rows, width)),
        in_specs=[far] * 4,
        out_specs=pl.BlockSpec(memory_space=pltpu.VMEM),
        scratch_shapes=[pltpu.SMEM(requests.shape, jnp.int32), pltpu.SemaphoreType.DMA((3 + SENT_GROUPS,))],
        compiler_params=pltpu.CompilerParams(vmem_limit_bytes=8 * 1024 * 1024),
    )(*[pltpu.with_memory_space_constraint(x, pltpu.HBM) for x in operands])
    pieces = gathered(packed)

    vec = vmem((8, size))
    mat = vmem((size, size), BF16)
    d_high, d_low, c_high, c_low, source, diag, wanted = call(
        functools.partial(first_kernel, size=size, cols=cols),
        (mat, mat, mat, mat, vec, vec, vmem((8, LANES))),
        *pieces,
        scratch=[pltpu.VMEM((size, cols + LANES), F32)],
    )
    mats = (d_high, d_low, c_high, c_low)

    last = 3
    lefts = []
    for k in range(last):
        carried = call(
            functools.partial(forward_kernel, k),
            vec, *mats, source, diag, *lefts[-1:],
        )
        lefts.append(hop(carried, k, k + 1))
    right_hand, panel = call(
        functools.partial(turn_kernel, last),
        (vec, vec), d_high, d_low, source, diag, *lefts,
    )
    aheads = []
    for k in range(last - 1, -1, -1):
        aheads.append(hop(panel, k + 1, k))
        if k > 0:
            panel = call(
                functools.partial(backward_kernel, k),
                vec, *mats, right_hand, diag, aheads[-1],
            )
    send = call(
        functools.partial(last_kernel, last),
        vmem((size // rows, 8, LANES)),
        *mats, right_hand, diag, wanted, *aheads,
    )
    got = lax.all_to_all(send, "panel", 0, 0, tiled=True).reshape(cols, LANES)
    panels, picked = call(
        unpack_kernel,
        (jax.ShapeDtypeStruct((rows, cols), F32), jax.ShapeDtypeStruct((few, cols), F32)),
        got,
    )
    return panels[None], picked[None]


def solution(mesh):
    placed = (
        P("depth", "panel", None),
        P("depth", "panel", None),
        P("depth", "panel", None),
        P("depth", "panel"),
    )
    return jax.shard_map(
        per_device,
        mesh=mesh,
        in_specs=placed,
        out_specs=(P("depth", "panel", None), P("depth", "panel", None)),
        check_vma=False,
    )
```

```python
import functools

import jax
import jax.numpy as jnp
from jax import lax
from jax.experimental import pallas as pl
from jax.experimental.pallas import tpu as pltpu
from jax.sharding import PartitionSpec as P


ITERS = 2
F32, BF16 = jnp.float32, jnp.bfloat16
LANES = 128
SENT_GROUPS = 5

AXES = ((1, 3, 2), (4, 12, 8))
SIBLINGS = [(p, p ^ 1) for p in range(32)]


def from_partner(block, phase, number):
    pairs = [
        (yz * 2 + core, (yz ^ AXES[core ^ phase][number]) * 2 + core)
        for yz in range(16)
        for core in range(2)
    ]
    return lax.ppermute(block, "panel", pairs)


def join_kernel(first, second, both):
    rows = first.shape[0]
    both[:rows] = first[...]
    both[rows:] = second[...]


def joined(first, second):
    return call(join_kernel, vmem((first.shape[0] * 2, first.shape[1])), first, second)


PIECES = (("A", None), ("B", None), ("A", 0), ("A", 1), ("B", 0), ("B", 1), ("A", 2), ("B", 2))


def offset_of(core, piece, unit):
    half, line = piece
    near = AXES[core]
    offset = ((0, near[0]) if half == "A" else (near[1], near[2]))[unit]
    return offset ^ (0 if line is None else AXES[1 - core][line])


def gathered(own):
    near = from_partner(own, 0, 0)
    other = from_partner(own, 0, 1)
    far = from_partner(own, 0, 2)
    a = joined(own, near)
    a1, a0 = from_partner(a, 1, 1), from_partner(a, 1, 0)
    b = joined(other, far)
    b0, b1 = from_partner(b, 1, 0), from_partner(b, 1, 1)
    a2, b2 = from_partner(a1, 1, 0), from_partner(b0, 1, 1)
    pieces = [a, b, a0, a1, b0, b1, a2, b2]
    return pieces + [lax.ppermute(piece, "panel", SIBLINGS) for piece in pieces]


def split(x):
    high = x.astype(BF16)
    return high, (x - high.astype(F32)).astype(BF16)


def product(x, high_ref, low_ref):
    rows = x.shape[0]
    both = jnp.concatenate(split(x), 0)
    dims = (((1,), (0,)), ((), ()))
    first = lax.dot_general(both, high_ref[...], dims, preferred_element_type=F32)
    second = lax.dot_general(both, low_ref[...], dims, preferred_element_type=F32)
    total = first + second
    return total[:rows] + total[rows:]


def jacobi(right_hand, diag, d_high, d_low):
    iterate = right_hand / diag
    for _ in range(ITERS):
        image = product(iterate, d_high, d_low)
        iterate = iterate + (right_hand - image) / diag
    return iterate


def pack_kernel(asked, diag_rows, coupling_rows, source_rows, packed, requests, sems):
    few = requests.shape[1]
    fetch = pltpu.make_async_copy(asked, requests, sems.at[2 + SENT_GROUPS])
    fetch.start()
    count, size = diag_rows.shape
    cols = source_rows.shape[1]
    sent = [(coupling_rows, size), (source_rows, cols)]
    group = lax.div(lax.axis_index("panel") * count, LANES)
    for k in range(SENT_GROUPS):
        start = lax.rem(group + k, size // LANES) * LANES
        sent.append((diag_rows.at[:, pl.ds(pl.multiple_of(start, LANES), LANES)], LANES))
    copies = []
    at = 0
    for number, (rows, width) in enumerate(sent):
        copies.append(
            pltpu.make_async_copy(rows, packed.at[:, at : at + width], sems.at[number])
        )
        copies[-1].start()
        at += width
    fetch.wait()
    row = lax.broadcasted_iota(jnp.int32, (count, LANES), 0)
    lane = lax.broadcasted_iota(jnp.int32, (count, LANES), 1)
    slots = jnp.zeros((count, LANES), F32)
    for k in range(few):
        here = (row == 0) & (lane == lax.axis_index("panel") * few + k)
        slots = jnp.where(here, requests[0, k].astype(F32), slots)
    packed[:, at:] = slots
    for copy in copies:
        copy.wait()


def move_pieces(numbers, pieces, d_high, d_low, c_high, c_low, side):
    size = d_high.shape[0]
    cols = side.shape[1] - LANES
    core = lax.rem(lax.axis_index("panel"), 2)
    place = lax.div(lax.axis_index("panel"), 2)
    unit_rows = size // 32
    step = 16
    groups = size // LANES

    def move(piece, start, to):
        def body(i, _):
            rows = pl.ds(pl.multiple_of(to + i * step, step), step)
            held = piece.at[pl.ds(pl.multiple_of(start + i * step, step), step)]
            c_high[rows, :], c_low[rows, :] = split(held[:, 0:size])
            side[rows, 0:cols] = held[:, size : size + cols]
            for k in range(SENT_GROUPS):
                at = lax.rem(lax.div(to, LANES) + k, groups) * LANES
                where = pl.ds(pl.multiple_of(at, LANES), LANES)
                own = size + cols + k * LANES
                d_high[rows, where], d_low[rows, where] = split(held[:, own : own + LANES])
            side[rows, cols:] = held[:, size + cols + SENT_GROUPS * LANES :]
            return 0

        lax.fori_loop(0, unit_rows // step, body, 0)

    for number, held in zip(numbers, pieces):
        sibling = number // 8
        for unit in range(2):
            piece = PIECES[number % 8]
            offset = jnp.where(
                core == sibling, offset_of(0, piece, unit), offset_of(1, piece, unit)
            )
            owner = lax.bitwise_xor(place, offset) * 2 + lax.bitwise_xor(core, sibling)
            move(held, unit * unit_rows, owner * unit_rows)


EARLY = (0, 1, 2, 3, 4, 5, 8, 9, 10, 11)
LATE = tuple(number for number in range(16) if number not in EARLY)


def early_kernel(*refs):
    count = len(EARLY)
    move_pieces(EARLY, refs[:count], *refs[count:])


def late_kernel(*refs):
    count = len(LATE)
    side = refs[count + 4]
    d_high, d_low, c_high, c_low, source, diag, wanted = refs[count + 5 :]
    size = d_high.shape[0]
    groups = size // LANES
    cols = side.shape[1] - LANES
    move_pieces(LATE, refs[:count], d_high, d_low, c_high, c_low, side)

    for group in range(groups):
        for k in range(1, groups - SENT_GROUPS + 1):
            rows = slice(group * LANES, (group + 1) * LANES)
            where = (group + k) % groups * LANES
            where = slice(where, where + LANES)
            block = d_high[rows, where].astype(F32) + d_low[rows, where].astype(F32)
            d_high[where, rows], d_low[where, rows] = split(block.T)

    pick = lax.broadcasted_iota(jnp.int32, (8, cols), 1) == (
        lax.broadcasted_iota(jnp.int32, (8, cols), 0) + lax.axis_index("panel") * 8
    )
    own = lax.dot_general(
        pick.astype(F32),
        side[:, 0:cols],
        (((1,), (1,)), ((), ())),
        precision=lax.Precision.HIGHEST,
        preferred_element_type=F32,
    )
    source[...] = own
    eye = lax.broadcasted_iota(jnp.int32, (LANES, LANES), 0) == lax.broadcasted_iota(
        jnp.int32, (LANES, LANES), 1
    )
    for start in range(0, size, LANES):
        tiles = slice(start, start + LANES)
        tile = d_high[tiles, tiles].astype(F32) + d_low[tiles, tiles].astype(F32)
        line = jnp.sum(jnp.where(eye, tile, 0.0), axis=0, keepdims=True)
        diag[:, start : start + LANES] = jnp.broadcast_to(line, (8, LANES))
    line = jnp.sum(side[:, cols : cols + LANES], axis=0, keepdims=True)
    wanted[...] = jnp.broadcast_to(line, (8, LANES))


def hop(block, here, there):
    other = [k for k in range(4) if k not in (here, there)]
    route = [(here, there), (there, here), tuple(other), tuple(other[::-1])]
    return lax.ppermute(block, "depth", route)


def taken(plane, planes, refs):
    total = jnp.zeros_like(refs[0])
    for meant, ref in zip(planes, refs):
        total = jnp.where(plane == meant, ref[...], total)
    return total


def forward_kernel(stage, d_high, d_low, c_high, c_low, source, diag, *refs):
    @pl.when(lax.axis_index("depth") == stage)
    def _():
        right_hand = source[...] - refs[0][...] if stage else source[...]
        forward = jacobi(right_hand, diag[...], d_high, d_low)
        refs[-1][...] = product(forward, c_high, c_low)


def transpose_kernel(last, high, low, high_turned, low_turned):
    @pl.when(lax.axis_index("depth") != last)
    def _():
        for ref, turned in ((high, high_turned), (low, low_turned)):
            for row in range(0, ref.shape[0], LANES):
                for col in range(0, ref.shape[1], LANES):
                    block = ref[row : row + LANES, col : col + LANES].astype(F32)
                    turned[col : col + LANES, row : row + LANES] = block.T.astype(BF16)


def turn_kernel(count, d_high, d_low, source, diag, *refs):
    right_hand = source[...] - taken(lax.axis_index("depth"), range(1, count + 1), refs[:count])
    refs[count][...] = right_hand

    @pl.when(lax.axis_index("depth") == count)
    def _():
        refs[count + 1][...] = jacobi(right_hand, diag[...], d_high, d_low)


def backward_kernel(plane, d_high, d_low, c_high, c_low, right_hand, diag, ahead, panel):
    @pl.when(lax.axis_index("depth") == plane)
    def _():
        rest = right_hand[...] - product(ahead[...], c_high, c_low)
        panel[...] = jacobi(rest, diag[...], d_high, d_low)


def last_kernel(count, d_high, d_low, c_high, c_low, right_hand, diag, wanted, *refs):
    ahead = taken(lax.axis_index("depth"), range(count - 1, -1, -1), refs[:count])
    coupled = jnp.where(lax.axis_index("depth") == count, 0.0, product(ahead, c_high, c_low))
    panel = jacobi(right_hand[...] - coupled, diag[...], d_high, d_low)
    size = panel.shape[1]
    high = panel.astype(BF16)
    rest = panel - high.astype(F32)
    middle = rest.astype(BF16)
    low = (rest - middle.astype(F32)).astype(BF16)
    line = wanted[0:1, :].astype(jnp.int32)
    chosen = (lax.broadcasted_iota(jnp.int32, (size, LANES), 0) == line).astype(BF16)
    parts = [jnp.dot(part, chosen, preferred_element_type=F32) for part in (high, middle, low)]
    picked = parts[0] + parts[1] + parts[2]
    send = refs[count]
    blocks = send.shape[0]
    own, few = size // blocks, LANES // blocks
    filler = jnp.zeros((8, LANES - own - few), F32)
    for block in range(blocks):
        send[block] = jnp.concatenate(
            [
                panel[:, block * own : (block + 1) * own],
                picked[:, block * few : (block + 1) * few],
                filler,
            ],
            1,
        )


def unpack_kernel(got, panels, picked):
    turned = got[...].T
    own = panels.shape[0]
    panels[...] = turned[:own]
    picked[...] = turned[own : own + picked.shape[0]]


def vmem(shape, dtype=F32):
    return pltpu.VMEM(shape, dtype)


def call(kernel, out_shape, *args, aliases=None, limit=8):
    args = [pltpu.with_memory_space_constraint(arg, pltpu.VMEM) for arg in args]
    space = pl.BlockSpec(memory_space=pltpu.VMEM)
    return pl.pallas_call(
        kernel,
        out_shape=out_shape,
        in_specs=[space] * len(args),
        out_specs=jax.tree.map(lambda _: space, out_shape),
        input_output_aliases=aliases or {},
        compiler_params=pltpu.CompilerParams(vmem_limit_bytes=limit * 1024 * 1024),
    )(*args)


def per_device(diag_blocks, coupling, sources, requests):
    rows, size, cols = diag_blocks.shape[1], diag_blocks.shape[2], sources.shape[2]
    few = requests.shape[1]
    width = size + cols + (SENT_GROUPS + 1) * LANES
    far = pl.BlockSpec(memory_space=pltpu.HBM)
    operands = (requests, diag_blocks[0], coupling[0], sources[0])
    packed = pl.pallas_call(
        pack_kernel,
        out_shape=vmem((rows, width)),
        in_specs=[far] * 4,
        out_specs=pl.BlockSpec(memory_space=pltpu.VMEM),
        scratch_shapes=[pltpu.SMEM(requests.shape, jnp.int32), pltpu.SemaphoreType.DMA((3 + SENT_GROUPS,))],
        compiler_params=pltpu.CompilerParams(vmem_limit_bytes=8 * 1024 * 1024),
    )(*[pltpu.with_memory_space_constraint(x, pltpu.HBM) for x in operands])
    pieces = gathered(packed)

    vec = vmem((8, size))
    mat = vmem((size, size), BF16)
    filled = call(
        early_kernel,
        (mat, mat, mat, mat, vmem((size, cols + LANES))),
        *[pieces[number] for number in EARLY],
    )
    d_high, d_low, c_high, c_low, source, diag, wanted = call(
        late_kernel,
        (mat, mat, mat, mat, vec, vec, vmem((8, LANES))),
        *[pieces[number] for number in LATE],
        *filled,
        aliases={len(LATE) + number: number for number in range(4)},
    )
    mats = (d_high, d_low, c_high, c_low)

    last = 3
    lefts = []
    for k in range(last):
        carried = call(
            functools.partial(forward_kernel, k),
            vec, *mats, source, diag, *lefts[-1:],
        )
        lefts.append(hop(carried, k, k + 1))
    turned = call(functools.partial(transpose_kernel, last), (mat, mat), c_high, c_low)
    right_hand, panel = call(
        functools.partial(turn_kernel, last),
        (vec, vec), d_high, d_low, source, diag, *lefts,
    )
    aheads = []
    for k in range(last - 1, -1, -1):
        aheads.append(hop(panel, k + 1, k))
        if k > 0:
            panel = call(
                functools.partial(backward_kernel, k),
                vec, d_high, d_low, *turned, right_hand, diag, aheads[-1],
            )
    send = call(
        functools.partial(last_kernel, last),
        vmem((size // rows, 8, LANES)),
        d_high, d_low, *turned, right_hand, diag, wanted, *aheads,
    )
    got = lax.all_to_all(send, "panel", 0, 0, tiled=True).reshape(cols, LANES)
    panels, picked = call(
        unpack_kernel,
        (jax.ShapeDtypeStruct((rows, cols), F32), jax.ShapeDtypeStruct((few, cols), F32)),
        got,
    )
    return panels[None], picked[None]


def solution(mesh):
    placed = (
        P("depth", "panel", None),
        P("depth", "panel", None),
        P("depth", "panel", None),
        P("depth", "panel"),
    )
    return jax.shard_map(
        per_device,
        mesh=mesh,
        in_specs=placed,
        out_specs=(P("depth", "panel", None), P("depth", "panel", None)),
        check_vma=False,
    )
```

```python
import functools

import jax
import jax.numpy as jnp
from jax import lax
from jax.experimental import pallas as pl
from jax.experimental.pallas import tpu as pltpu
from jax.sharding import PartitionSpec as P


ITERS = 2
F32, BF16 = jnp.float32, jnp.bfloat16
LANES = 128
SENT_GROUPS = 5

AXES = ((1, 3, 2), (4, 12, 8))
SIBLINGS = [(p, p ^ 1) for p in range(32)]


def from_partner(block, phase, number):
    pairs = [
        (yz * 2 + core, (yz ^ AXES[core ^ phase][number]) * 2 + core)
        for yz in range(16)
        for core in range(2)
    ]
    return lax.ppermute(block, "panel", pairs)


def join_kernel(first, second, both):
    rows = first.shape[0]
    both[:rows] = first[...]
    both[rows:] = second[...]


def cut_kernel(part, both, one):
    rows = one.shape[0]
    one[...] = both[part * rows : (part + 1) * rows]


def cut(both, part):
    shape = (both.shape[0] // 2, both.shape[1])
    return call(functools.partial(cut_kernel, part), vmem(shape), both)


def joined(first, second):
    return call(join_kernel, vmem((first.shape[0] * 2, first.shape[1])), first, second)


PIECES = (
    (None, (0, 1)), (None, (2, 3)), (0, (0, 1)), (1, (0, 1)), (0, (2, 3)), (1, (2, 3)),
    (2, (0,)), (2, (1,)), (2, (2,)), (2, (3,)),
)


def offset_of(core, line, unit):
    offset = (0, *AXES[core])[unit]
    return offset ^ (0 if line is None else AXES[1 - core][line])


def gathered(own):
    near = from_partner(own, 0, 0)
    other = from_partner(own, 0, 1)
    far = from_partner(own, 0, 2)
    a = joined(own, near)
    a1, a0 = from_partner(a, 1, 1), from_partner(a, 1, 0)
    b = joined(other, far)
    b0, b1 = from_partner(b, 1, 0), from_partner(b, 1, 1)
    far_pieces = [
        from_partner(cut(a1, 0), 1, 0),
        from_partner(cut(a0, 1), 1, 1),
        from_partner(cut(b0, 0), 1, 1),
        from_partner(cut(b1, 1), 1, 0),
    ]
    pieces = [a, b, a0, a1, b0, b1, *far_pieces]
    return pieces + [lax.ppermute(piece, "panel", SIBLINGS) for piece in pieces]


def split(x):
    high = x.astype(BF16)
    return high, (x - high.astype(F32)).astype(BF16)


def product(x, high_ref, low_ref):
    rows = x.shape[0]
    both = jnp.concatenate(split(x), 0)
    dims = (((1,), (0,)), ((), ()))
    first = lax.dot_general(both, high_ref[...], dims, preferred_element_type=F32)
    second = lax.dot_general(both, low_ref[...], dims, preferred_element_type=F32)
    total = first + second
    return total[:rows] + total[rows:]


def jacobi(right_hand, diag, d_high, d_low):
    iterate = right_hand / diag
    for _ in range(ITERS):
        image = product(iterate, d_high, d_low)
        iterate = iterate + (right_hand - image) / diag
    return iterate


def pack_kernel(asked, diag_rows, coupling_rows, source_rows, packed, requests, sems):
    few = requests.shape[1]
    fetch = pltpu.make_async_copy(asked, requests, sems.at[2 + SENT_GROUPS])
    fetch.start()
    count, size = diag_rows.shape
    cols = source_rows.shape[1]
    sent = [(coupling_rows, size), (source_rows, cols)]
    group = lax.div(lax.axis_index("panel") * count, LANES)
    for k in range(SENT_GROUPS):
        start = lax.rem(group + k, size // LANES) * LANES
        sent.append((diag_rows.at[:, pl.ds(pl.multiple_of(start, LANES), LANES)], LANES))
    copies = []
    at = 0
    for number, (rows, width) in enumerate(sent):
        copies.append(
            pltpu.make_async_copy(rows, packed.at[:, at : at + width], sems.at[number])
        )
        copies[-1].start()
        at += width
    fetch.wait()
    row = lax.broadcasted_iota(jnp.int32, (count, LANES), 0)
    lane = lax.broadcasted_iota(jnp.int32, (count, LANES), 1)
    slots = jnp.zeros((count, LANES), F32)
    for k in range(few):
        here = (row == 0) & (lane == lax.axis_index("panel") * few + k)
        slots = jnp.where(here, requests[0, k].astype(F32), slots)
    packed[:, at:] = slots
    for copy in copies:
        copy.wait()


def move_pieces(numbers, pieces, d_high, d_low, c_high, c_low, side):
    size = d_high.shape[0]
    cols = side.shape[1] - LANES
    core = lax.rem(lax.axis_index("panel"), 2)
    place = lax.div(lax.axis_index("panel"), 2)
    unit_rows = size // 32
    step = 16
    groups = size // LANES

    def move(piece, start, to):
        def body(i, _):
            rows = pl.ds(pl.multiple_of(to + i * step, step), step)
            held = piece.at[pl.ds(pl.multiple_of(start + i * step, step), step)]
            c_high[rows, :], c_low[rows, :] = split(held[:, 0:size])
            side[rows, 0:cols] = held[:, size : size + cols]
            for k in range(SENT_GROUPS):
                at = lax.rem(lax.div(to, LANES) + k, groups) * LANES
                where = pl.ds(pl.multiple_of(at, LANES), LANES)
                own = size + cols + k * LANES
                d_high[rows, where], d_low[rows, where] = split(held[:, own : own + LANES])
            side[rows, cols:] = held[:, size + cols + SENT_GROUPS * LANES :]
            return 0

        lax.fori_loop(0, unit_rows // step, body, 0)

    for number, held in zip(numbers, pieces):
        sibling = number // len(PIECES)
        line, units = PIECES[number % len(PIECES)]
        for place_in, unit in enumerate(units):
            offset = jnp.where(
                core == sibling, offset_of(0, line, unit), offset_of(1, line, unit)
            )
            owner = lax.bitwise_xor(place, offset) * 2 + lax.bitwise_xor(core, sibling)
            move(held, place_in * unit_rows, owner * unit_rows)


EARLY = (0, 1, 2, 3, 10, 11, 12, 13)
LATE = tuple(number for number in range(2 * len(PIECES)) if number not in EARLY)


def early_kernel(*refs):
    count = len(EARLY)
    move_pieces(EARLY, refs[:count], *refs[count:])


def late_kernel(*refs):
    count = len(LATE)
    side = refs[count + 4]
    d_high, d_low, c_high, c_low, source, diag, wanted = refs[count + 5 :]
    size = d_high.shape[0]
    groups = size // LANES
    cols = side.shape[1] - LANES
    move_pieces(LATE, refs[:count], d_high, d_low, c_high, c_low, side)

    for group in range(groups):
        for k in range(1, groups - SENT_GROUPS + 1):
            rows = slice(group * LANES, (group + 1) * LANES)
            where = (group + k) % groups * LANES
            where = slice(where, where + LANES)
            block = d_high[rows, where].astype(F32) + d_low[rows, where].astype(F32)
            d_high[where, rows], d_low[where, rows] = split(block.T)

    pick = lax.broadcasted_iota(jnp.int32, (8, cols), 1) == (
        lax.broadcasted_iota(jnp.int32, (8, cols), 0) + lax.axis_index("panel") * 8
    )
    own = lax.dot_general(
        pick.astype(F32),
        side[:, 0:cols],
        (((1,), (1,)), ((), ())),
        precision=lax.Precision.HIGHEST,
        preferred_element_type=F32,
    )
    source[...] = own
    eye = lax.broadcasted_iota(jnp.int32, (LANES, LANES), 0) == lax.broadcasted_iota(
        jnp.int32, (LANES, LANES), 1
    )
    for start in range(0, size, LANES):
        tiles = slice(start, start + LANES)
        tile = d_high[tiles, tiles].astype(F32) + d_low[tiles, tiles].astype(F32)
        line = jnp.sum(jnp.where(eye, tile, 0.0), axis=0, keepdims=True)
        diag[:, start : start + LANES] = jnp.broadcast_to(line, (8, LANES))
    line = jnp.sum(side[:, cols : cols + LANES], axis=0, keepdims=True)
    wanted[...] = jnp.broadcast_to(line, (8, LANES))


def hop(block, here, there):
    other = [k for k in range(4) if k not in (here, there)]
    route = [(here, there), (there, here), tuple(other), tuple(other[::-1])]
    return lax.ppermute(block, "depth", route)


def taken(plane, planes, refs):
    total = jnp.zeros_like(refs[0])
    for meant, ref in zip(planes, refs):
        total = jnp.where(plane == meant, ref[...], total)
    return total


def forward_kernel(stage, d_high, d_low, c_high, c_low, source, diag, *refs):
    @pl.when(lax.axis_index("depth") == stage)
    def _():
        right_hand = source[...] - refs[0][...] if stage else source[...]
        forward = jacobi(right_hand, diag[...], d_high, d_low)
        refs[-1][...] = product(forward, c_high, c_low)


def transpose_kernel(last, high, low, high_turned, low_turned):
    @pl.when(lax.axis_index("depth") != last)
    def _():
        for ref, turned in ((high, high_turned), (low, low_turned)):
            for row in range(0, ref.shape[0], LANES):
                for col in range(0, ref.shape[1], LANES):
                    block = ref[row : row + LANES, col : col + LANES].astype(F32)
                    turned[col : col + LANES, row : row + LANES] = block.T.astype(BF16)


def turn_kernel(count, d_high, d_low, source, diag, *refs):
    right_hand = source[...] - taken(lax.axis_index("depth"), range(1, count + 1), refs[:count])
    refs[count][...] = right_hand

    @pl.when(lax.axis_index("depth") == count)
    def _():
        refs[count + 1][...] = jacobi(right_hand, diag[...], d_high, d_low)


def backward_kernel(plane, d_high, d_low, c_high, c_low, right_hand, diag, ahead, panel):
    @pl.when(lax.axis_index("depth") == plane)
    def _():
        rest = right_hand[...] - product(ahead[...], c_high, c_low)
        panel[...] = jacobi(rest, diag[...], d_high, d_low)


def last_kernel(count, d_high, d_low, c_high, c_low, right_hand, diag, wanted, *refs):
    ahead = taken(lax.axis_index("depth"), range(count - 1, -1, -1), refs[:count])
    coupled = jnp.where(lax.axis_index("depth") == count, 0.0, product(ahead, c_high, c_low))
    panel = jacobi(right_hand[...] - coupled, diag[...], d_high, d_low)
    size = panel.shape[1]
    high = panel.astype(BF16)
    rest = panel - high.astype(F32)
    middle = rest.astype(BF16)
    low = (rest - middle.astype(F32)).astype(BF16)
    line = wanted[0:1, :].astype(jnp.int32)
    chosen = (lax.broadcasted_iota(jnp.int32, (size, LANES), 0) == line).astype(BF16)
    parts = [jnp.dot(part, chosen, preferred_element_type=F32) for part in (high, middle, low)]
    picked = parts[0] + parts[1] + parts[2]
    send = refs[count]
    blocks = send.shape[0]
    own, few = size // blocks, LANES // blocks
    filler = jnp.zeros((8, LANES - own - few), F32)
    for block in range(blocks):
        send[block] = jnp.concatenate(
            [
                panel[:, block * own : (block + 1) * own],
                picked[:, block * few : (block + 1) * few],
                filler,
            ],
            1,
        )


def unpack_kernel(got, panels, picked):
    turned = got[...].T
    own = panels.shape[0]
    panels[...] = turned[:own]
    picked[...] = turned[own : own + picked.shape[0]]


def vmem(shape, dtype=F32):
    return pltpu.VMEM(shape, dtype)


def call(kernel, out_shape, *args, aliases=None, limit=8):
    args = [pltpu.with_memory_space_constraint(arg, pltpu.VMEM) for arg in args]
    space = pl.BlockSpec(memory_space=pltpu.VMEM)
    return pl.pallas_call(
        kernel,
        out_shape=out_shape,
        in_specs=[space] * len(args),
        out_specs=jax.tree.map(lambda _: space, out_shape),
        input_output_aliases=aliases or {},
        compiler_params=pltpu.CompilerParams(vmem_limit_bytes=limit * 1024 * 1024),
    )(*args)


def per_device(diag_blocks, coupling, sources, requests):
    rows, size, cols = diag_blocks.shape[1], diag_blocks.shape[2], sources.shape[2]
    few = requests.shape[1]
    width = size + cols + (SENT_GROUPS + 1) * LANES
    far = pl.BlockSpec(memory_space=pltpu.HBM)
    operands = (requests, diag_blocks[0], coupling[0], sources[0])
    packed = pl.pallas_call(
        pack_kernel,
        out_shape=vmem((rows, width)),
        in_specs=[far] * 4,
        out_specs=pl.BlockSpec(memory_space=pltpu.VMEM),
        scratch_shapes=[pltpu.SMEM(requests.shape, jnp.int32), pltpu.SemaphoreType.DMA((3 + SENT_GROUPS,))],
        compiler_params=pltpu.CompilerParams(vmem_limit_bytes=8 * 1024 * 1024),
    )(*[pltpu.with_memory_space_constraint(x, pltpu.HBM) for x in operands])
    pieces = gathered(packed)

    vec = vmem((8, size))
    mat = vmem((size, size), BF16)
    filled = call(
        early_kernel,
        (mat, mat, mat, mat, vmem((size, cols + LANES))),
        *[pieces[number] for number in EARLY],
    )
    d_high, d_low, c_high, c_low, source, diag, wanted = call(
        late_kernel,
        (mat, mat, mat, mat, vec, vec, vmem((8, LANES))),
        *[pieces[number] for number in LATE],
        *filled,
        aliases={len(LATE) + number: number for number in range(4)},
    )
    mats = (d_high, d_low, c_high, c_low)

    last = 3
    lefts = []
    for k in range(last):
        carried = call(
            functools.partial(forward_kernel, k),
            vec, *mats, source, diag, *lefts[-1:],
        )
        lefts.append(hop(carried, k, k + 1))
    turned = call(functools.partial(transpose_kernel, last), (mat, mat), c_high, c_low)
    right_hand, panel = call(
        functools.partial(turn_kernel, last),
        (vec, vec), d_high, d_low, source, diag, *lefts,
    )
    aheads = []
    for k in range(last - 1, -1, -1):
        aheads.append(hop(panel, k + 1, k))
        if k > 0:
            panel = call(
                functools.partial(backward_kernel, k),
                vec, d_high, d_low, *turned, right_hand, diag, aheads[-1],
            )
    send = call(
        functools.partial(last_kernel, last),
        vmem((size // rows, 8, LANES)),
        d_high, d_low, *turned, right_hand, diag, wanted, *aheads,
    )
    got = lax.all_to_all(send, "panel", 0, 0, tiled=True).reshape(cols, LANES)
    panels, picked = call(
        unpack_kernel,
        (jax.ShapeDtypeStruct((rows, cols), F32), jax.ShapeDtypeStruct((few, cols), F32)),
        got,
    )
    return panels[None], picked[None]


def solution(mesh):
    placed = (
        P("depth", "panel", None),
        P("depth", "panel", None),
        P("depth", "panel", None),
        P("depth", "panel"),
    )
    return jax.shard_map(
        per_device,
        mesh=mesh,
        in_specs=placed,
        out_specs=(P("depth", "panel", None), P("depth", "panel", None)),
        check_vma=False,
    )
```

```python
import functools

import jax
import jax.numpy as jnp
from jax import lax
from jax.experimental import pallas as pl
from jax.experimental.pallas import tpu as pltpu
from jax.sharding import PartitionSpec as P


ITERS = 2
F32, BF16 = jnp.float32, jnp.bfloat16
LANES = 128
SENT_GROUPS = 5

AXES = ((1, 3, 2), (4, 12, 8))
SIBLINGS = [(p, p ^ 1) for p in range(32)]


def from_partner(block, phase, number):
    pairs = [
        (yz * 2 + core, (yz ^ AXES[core ^ phase][number]) * 2 + core)
        for yz in range(16)
        for core in range(2)
    ]
    return lax.ppermute(block, "panel", pairs)


def join_kernel(first, second, both):
    rows = first.shape[0]
    both[:rows] = first[...]
    both[rows:] = second[...]


def cut_kernel(part, both, one):
    rows = one.shape[0]
    one[...] = both[part * rows : (part + 1) * rows]


def cut(both, part):
    shape = (both.shape[0] // 2, both.shape[1])
    return call(functools.partial(cut_kernel, part), vmem(shape), both)


def joined(first, second):
    return call(join_kernel, vmem((first.shape[0] * 2, first.shape[1])), first, second)


PIECES = (
    (None, (0, 1)), (None, (2, 3)), (0, (0, 1)), (1, (0, 1)), (0, (2, 3)), (1, (2, 3)),
    (2, (0,)), (2, (1,)), (2, (2,)), (2, (3,)),
)


def offset_of(core, line, unit):
    offset = (0, *AXES[core])[unit]
    return offset ^ (0 if line is None else AXES[1 - core][line])


def gathered(own):
    near = from_partner(own, 0, 0)
    other = from_partner(own, 0, 1)
    far = from_partner(own, 0, 2)
    a = joined(own, near)
    a1, a0 = from_partner(a, 1, 1), from_partner(a, 1, 0)
    b = joined(other, far)
    b0, b1 = from_partner(b, 1, 0), from_partner(b, 1, 1)
    far_pieces = [
        from_partner(cut(a1, 0), 1, 0),
        from_partner(cut(a0, 1), 1, 1),
        from_partner(cut(b0, 0), 1, 1),
        from_partner(cut(b1, 1), 1, 0),
    ]
    pieces = [a, b, a0, a1, b0, b1, *far_pieces]
    return pieces + [lax.ppermute(piece, "panel", SIBLINGS) for piece in pieces]


COLUMNS = 16


def sweeps():
    return lax.rem(lax.axis_index("panel"), 2) == 1


def split(x):
    high = x.astype(BF16)
    return high, (x - high.astype(F32)).astype(BF16)


def product(x, high_ref, low_ref):
    rows = x.shape[0]
    both = jnp.concatenate(split(x), 0)
    dims = (((1,), (0,)), ((), ()))
    first = lax.dot_general(both, high_ref[...], dims, preferred_element_type=F32)
    second = lax.dot_general(both, low_ref[...], dims, preferred_element_type=F32)
    total = first + second
    return total[:rows] + total[rows:]


def jacobi(right_hand, diag, d_high, d_low):
    iterate = right_hand / diag
    for _ in range(ITERS):
        image = product(iterate, d_high, d_low)
        iterate = iterate + (right_hand - image) / diag
    return iterate


def pack_kernel(asked, diag_rows, coupling_rows, source_rows, packed, requests, sems):
    few = requests.shape[1]
    fetch = pltpu.make_async_copy(asked, requests, sems.at[2 + SENT_GROUPS])
    fetch.start()
    count, size = diag_rows.shape
    cols = source_rows.shape[1]
    sent = [(coupling_rows, size), (source_rows, cols)]
    group = lax.div(lax.axis_index("panel") * count, LANES)
    for k in range(SENT_GROUPS):
        start = lax.rem(group + k, size // LANES) * LANES
        sent.append((diag_rows.at[:, pl.ds(pl.multiple_of(start, LANES), LANES)], LANES))
    copies = []
    at = 0
    for number, (rows, width) in enumerate(sent):
        copies.append(
            pltpu.make_async_copy(rows, packed.at[:, at : at + width], sems.at[number])
        )
        copies[-1].start()
        at += width
    fetch.wait()
    row = lax.broadcasted_iota(jnp.int32, (count, LANES), 0)
    lane = lax.broadcasted_iota(jnp.int32, (count, LANES), 1)
    slots = jnp.zeros((count, LANES), F32)
    for k in range(few):
        here = (row == 0) & (lane == lax.axis_index("panel") * few + k)
        slots = jnp.where(here, requests[0, k].astype(F32), slots)
    packed[:, at:] = slots
    for copy in copies:
        copy.wait()


def move_pieces(numbers, pieces, d_high, d_low, c_high, c_low, side):
    size = d_high.shape[0]
    cols = side.shape[1] - LANES
    core = lax.rem(lax.axis_index("panel"), 2)
    place = lax.div(lax.axis_index("panel"), 2)
    unit_rows = size // 32
    step = 16
    groups = size // LANES

    def move(piece, start, to):
        def body(i, _):
            rows = pl.ds(pl.multiple_of(to + i * step, step), step)
            held = piece.at[pl.ds(pl.multiple_of(start + i * step, step), step)]
            c_high[rows, :], c_low[rows, :] = split(held[:, 0:size])
            side[rows, 0:cols] = held[:, size : size + cols]
            for k in range(SENT_GROUPS):
                at = lax.rem(lax.div(to, LANES) + k, groups) * LANES
                where = pl.ds(pl.multiple_of(at, LANES), LANES)
                own = size + cols + k * LANES
                d_high[rows, where], d_low[rows, where] = split(held[:, own : own + LANES])
            side[rows, cols:] = held[:, size + cols + SENT_GROUPS * LANES :]
            return 0

        lax.fori_loop(0, unit_rows // step, body, 0)

    for number, held in zip(numbers, pieces):
        sibling = number // len(PIECES)
        line, units = PIECES[number % len(PIECES)]
        for place_in, unit in enumerate(units):
            offset = jnp.where(
                core == sibling, offset_of(0, line, unit), offset_of(1, line, unit)
            )
            owner = lax.bitwise_xor(place, offset) * 2 + lax.bitwise_xor(core, sibling)
            move(held, place_in * unit_rows, owner * unit_rows)


EARLY = (0, 1, 2, 3, 10, 11, 12, 13)
LATE = tuple(number for number in range(2 * len(PIECES)) if number not in EARLY)


def early_kernel(*refs):
    count = len(EARLY)
    move_pieces(EARLY, refs[:count], *refs[count:])


def late_kernel(*refs):
    count = len(LATE)
    side = refs[count + 4]
    d_high, d_low, c_high, c_low, source, diag, wanted = refs[count + 5 :]
    size = d_high.shape[0]
    groups = size // LANES
    cols = side.shape[1] - LANES
    move_pieces(LATE, refs[:count], d_high, d_low, c_high, c_low, side)

    for group in range(groups):
        for k in range(1, groups - SENT_GROUPS + 1):
            rows = slice(group * LANES, (group + 1) * LANES)
            where = (group + k) % groups * LANES
            where = slice(where, where + LANES)
            block = d_high[rows, where].astype(F32) + d_low[rows, where].astype(F32)
            d_high[where, rows], d_low[where, rows] = split(block.T)

    line = lax.broadcasted_iota(jnp.int32, (COLUMNS, cols), 0)
    few = COLUMNS // 2
    mine = line + lax.div(lax.axis_index("panel"), 2) * few
    mine = jnp.where(line < few, mine, mine + cols // 2 - few)
    pick = lax.broadcasted_iota(jnp.int32, (COLUMNS, cols), 1) == mine
    own = lax.dot_general(
        pick.astype(F32),
        side[:, 0:cols],
        (((1,), (1,)), ((), ())),
        precision=lax.Precision.HIGHEST,
        preferred_element_type=F32,
    )
    source[...] = own
    eye = lax.broadcasted_iota(jnp.int32, (LANES, LANES), 0) == lax.broadcasted_iota(
        jnp.int32, (LANES, LANES), 1
    )
    for start in range(0, size, LANES):
        tiles = slice(start, start + LANES)
        tile = d_high[tiles, tiles].astype(F32) + d_low[tiles, tiles].astype(F32)
        line = jnp.sum(jnp.where(eye, tile, 0.0), axis=0, keepdims=True)
        diag[:, start : start + LANES] = jnp.broadcast_to(line, (COLUMNS, LANES))
    line = jnp.sum(side[:, cols : cols + LANES], axis=0, keepdims=True)
    wanted[...] = jnp.broadcast_to(line, (8, LANES))


def hop(block, here, there):
    other = [k for k in range(4) if k not in (here, there)]
    route = [(here, there), (there, here), tuple(other), tuple(other[::-1])]
    return lax.ppermute(block, "depth", route)


def taken(plane, planes, refs):
    total = jnp.zeros_like(refs[0])
    for meant, ref in zip(planes, refs):
        total = jnp.where(plane == meant, ref[...], total)
    return total


def forward_kernel(stage, d_high, d_low, c_high, c_low, source, diag, *refs):
    @pl.when(sweeps() & (lax.axis_index("depth") == stage))
    def _():
        right_hand = source[...] - refs[0][...] if stage else source[...]
        forward = jacobi(right_hand, diag[...], d_high, d_low)
        refs[-1][...] = product(forward, c_high, c_low)


def transpose_kernel(last, high, low, high_turned, low_turned):
    @pl.when(sweeps() & (lax.axis_index("depth") != last))
    def _():
        for ref, turned in ((high, high_turned), (low, low_turned)):
            for row in range(0, ref.shape[0], LANES):
                for col in range(0, ref.shape[1], LANES):
                    block = ref[row : row + LANES, col : col + LANES].astype(F32)
                    turned[col : col + LANES, row : row + LANES] = block.T.astype(BF16)


def turn_kernel(count, d_high, d_low, source, diag, *refs):
    right_hand = source[...] - taken(lax.axis_index("depth"), range(1, count + 1), refs[:count])
    refs[count][...] = right_hand

    @pl.when(sweeps() & (lax.axis_index("depth") == count))
    def _():
        refs[count + 1][...] = jacobi(right_hand, diag[...], d_high, d_low)


def backward_kernel(plane, d_high, d_low, c_high, c_low, right_hand, diag, ahead, panel):
    @pl.when(sweeps() & (lax.axis_index("depth") == plane))
    def _():
        rest = right_hand[...] - product(ahead[...], c_high, c_low)
        panel[...] = jacobi(rest, diag[...], d_high, d_low)


def last_kernel(count, d_high, d_low, c_high, c_low, right_hand, diag, wanted, *refs):
    @pl.when(sweeps())
    def _():
        ahead = taken(lax.axis_index("depth"), range(count - 1, -1, -1), refs[:count])
        coupled = product(ahead, c_high, c_low)
        coupled = jnp.where(lax.axis_index("depth") == count, 0.0, coupled)
        panel = jacobi(right_hand[...] - coupled, diag[...], d_high, d_low)
        size = panel.shape[1]
        high = panel.astype(BF16)
        rest = panel - high.astype(F32)
        middle = rest.astype(BF16)
        low = (rest - middle.astype(F32)).astype(BF16)
        line = wanted[0:1, :].astype(jnp.int32)
        chosen = (lax.broadcasted_iota(jnp.int32, (size, LANES), 0) == line).astype(BF16)
        parts = [jnp.dot(x, chosen, preferred_element_type=F32) for x in (high, middle, low)]
        picked = parts[0] + parts[1] + parts[2]
        send = refs[count]
        blocks = send.shape[0]
        own, few = size // blocks, LANES // blocks
        lines = COLUMNS // 2
        filler = jnp.zeros((lines, LANES // 2 - own - few), F32)
        for block in range(blocks):
            tile = []
            for half in range(2):
                rows = slice(half * lines, (half + 1) * lines)
                tile.append(panel[rows, block * own : (block + 1) * own])
                tile.append(picked[rows, block * few : (block + 1) * few])
                tile.append(filler)
            send[block] = jnp.concatenate(tile, 1)


def unpack_kernel(got, panels, picked):
    turned = jnp.concatenate([got[k] for k in range(1, got.shape[0], 2)], 0).T
    own, few = panels.shape[0], picked.shape[0]
    width = turned.shape[1]
    for half in range(2):
        at = half * LANES // 2
        cols = slice(half * width, (half + 1) * width)
        panels[:, cols] = turned[at : at + own]
        picked[:, cols] = turned[at + own : at + own + few]


def vmem(shape, dtype=F32):
    return pltpu.VMEM(shape, dtype)


def call(kernel, out_shape, *args, aliases=None, limit=8):
    args = [pltpu.with_memory_space_constraint(arg, pltpu.VMEM) for arg in args]
    space = pl.BlockSpec(memory_space=pltpu.VMEM)
    return pl.pallas_call(
        kernel,
        out_shape=out_shape,
        in_specs=[space] * len(args),
        out_specs=jax.tree.map(lambda _: space, out_shape),
        input_output_aliases=aliases or {},
        compiler_params=pltpu.CompilerParams(vmem_limit_bytes=limit * 1024 * 1024),
    )(*args)


def per_device(diag_blocks, coupling, sources, requests):
    rows, size, cols = diag_blocks.shape[1], diag_blocks.shape[2], sources.shape[2]
    few = requests.shape[1]
    width = size + cols + (SENT_GROUPS + 1) * LANES
    far = pl.BlockSpec(memory_space=pltpu.HBM)
    operands = (requests, diag_blocks[0], coupling[0], sources[0])
    packed = pl.pallas_call(
        pack_kernel,
        out_shape=vmem((rows, width)),
        in_specs=[far] * 4,
        out_specs=pl.BlockSpec(memory_space=pltpu.VMEM),
        scratch_shapes=[pltpu.SMEM(requests.shape, jnp.int32), pltpu.SemaphoreType.DMA((3 + SENT_GROUPS,))],
        compiler_params=pltpu.CompilerParams(vmem_limit_bytes=8 * 1024 * 1024),
    )(*[pltpu.with_memory_space_constraint(x, pltpu.HBM) for x in operands])
    pieces = gathered(packed)

    vec = vmem((COLUMNS, size))
    mat = vmem((size, size), BF16)
    filled = call(
        early_kernel,
        (mat, mat, mat, mat, vmem((size, cols + LANES))),
        *[pieces[number] for number in EARLY],
    )
    d_high, d_low, c_high, c_low, source, diag, wanted = call(
        late_kernel,
        (mat, mat, mat, mat, vec, vec, vmem((8, LANES))),
        *[pieces[number] for number in LATE],
        *filled,
        aliases={len(LATE) + number: number for number in range(4)},
    )
    mats = (d_high, d_low, c_high, c_low)

    last = 3
    lefts = []
    for k in range(last):
        carried = call(
            functools.partial(forward_kernel, k),
            vec, *mats, source, diag, *lefts[-1:],
        )
        lefts.append(hop(carried, k, k + 1))
    turned = call(functools.partial(transpose_kernel, last), (mat, mat), c_high, c_low)
    right_hand, panel = call(
        functools.partial(turn_kernel, last),
        (vec, vec), d_high, d_low, source, diag, *lefts,
    )
    aheads = []
    for k in range(last - 1, -1, -1):
        aheads.append(hop(panel, k + 1, k))
        if k > 0:
            panel = call(
                functools.partial(backward_kernel, k),
                vec, d_high, d_low, *turned, right_hand, diag, aheads[-1],
            )
    send = call(
        functools.partial(last_kernel, last),
        vmem((size // rows, COLUMNS // 2, LANES)),
        d_high, d_low, *turned, right_hand, diag, wanted, *aheads,
    )
    got = lax.all_to_all(send, "panel", 0, 0, tiled=True)
    panels, picked = call(
        unpack_kernel,
        (jax.ShapeDtypeStruct((rows, cols), F32), jax.ShapeDtypeStruct((few, cols), F32)),
        got,
    )
    return panels[None], picked[None]


def solution(mesh):
    placed = (
        P("depth", "panel", None),
        P("depth", "panel", None),
        P("depth", "panel", None),
        P("depth", "panel"),
    )
    return jax.shard_map(
        per_device,
        mesh=mesh,
        in_specs=placed,
        out_specs=(P("depth", "panel", None), P("depth", "panel", None)),
        check_vma=False,
    )
```

```python
import functools

import jax
import jax.numpy as jnp
from jax import lax
from jax.experimental import pallas as pl
from jax.experimental.pallas import tpu as pltpu
from jax.sharding import PartitionSpec as P


ITERS = 2
F32, BF16 = jnp.float32, jnp.bfloat16
LANES = 128
SENT_GROUPS = 5

AXES = ((1, 3, 2), (4, 12, 8))
SIBLINGS = [(p, p ^ 1) for p in range(32)]


def from_partner(block, phase, number):
    pairs = [
        (yz * 2 + core, (yz ^ AXES[core ^ phase][number]) * 2 + core)
        for yz in range(16)
        for core in range(2)
    ]
    return lax.ppermute(block, "panel", pairs)


def join_kernel(first, second, both):
    rows = first.shape[0]
    both[:rows] = first[...]
    both[rows:] = second[...]


def cut_kernel(part, both, one):
    rows = one.shape[0]
    one[...] = both[part * rows : (part + 1) * rows]


def cut(both, part):
    shape = (both.shape[0] // 2, both.shape[1])
    return call(functools.partial(cut_kernel, part), vmem(shape), both)


def joined(first, second):
    return call(join_kernel, vmem((first.shape[0] * 2, first.shape[1])), first, second)


PIECES = (
    (None, (0, 1)), (None, (2, 3)), (0, (0, 1)), (1, (0, 1)), (0, (2, 3)), (1, (2, 3)),
    (2, (0,)), (2, (1,)), (2, (2,)), (2, (3,)),
)


def offset_of(core, line, unit):
    offset = (0, *AXES[core])[unit]
    return offset ^ (0 if line is None else AXES[1 - core][line])


def gathered(own):
    near = from_partner(own, 0, 0)
    other = from_partner(own, 0, 1)
    far = from_partner(own, 0, 2)
    a = joined(own, near)
    a1, a0 = from_partner(a, 1, 1), from_partner(a, 1, 0)
    b = joined(other, far)
    b0, b1 = from_partner(b, 1, 0), from_partner(b, 1, 1)
    far_pieces = [
        from_partner(cut(a1, 0), 1, 0),
        from_partner(cut(a0, 1), 1, 1),
        from_partner(cut(b0, 0), 1, 1),
        from_partner(cut(b1, 1), 1, 0),
    ]
    pieces = [a, b, a0, a1, b0, b1, *far_pieces]
    sibling = []
    for piece in pieces:
        sibling.append(lax.ppermute(piece, "panel", SIBLINGS))
    return pieces + sibling


def split(x):
    high = x.astype(BF16)
    return high, (x - high.astype(F32)).astype(BF16)


def product(x, high_ref, low_ref):
    rows = x.shape[0]
    both = jnp.concatenate(split(x), 0)
    dims = (((1,), (0,)), ((), ()))
    first = lax.dot_general(both, high_ref[...], dims, preferred_element_type=F32)
    second = lax.dot_general(both, low_ref[...], dims, preferred_element_type=F32)
    total = first + second
    return total[:rows] + total[rows:]


def jacobi(right_hand, diag, d_high, d_low):
    iterate = right_hand / diag
    for _ in range(ITERS):
        image = product(iterate, d_high, d_low)
        iterate = iterate + (right_hand - image) / diag
    return iterate


def pack_kernel(asked, diag_rows, coupling_rows, source_rows, packed, requests, sems):
    few = requests.shape[1]
    fetch = pltpu.make_async_copy(asked, requests, sems.at[2 + SENT_GROUPS])
    fetch.start()
    count, size = diag_rows.shape
    cols = source_rows.shape[1]
    sent = [(coupling_rows, size), (source_rows, cols)]
    group = lax.div(lax.axis_index("panel") * count, LANES)
    for k in range(SENT_GROUPS):
        start = lax.rem(group + k, size // LANES) * LANES
        sent.append((diag_rows.at[:, pl.ds(pl.multiple_of(start, LANES), LANES)], LANES))
    copies = []
    at = 0
    for number, (rows, width) in enumerate(sent):
        copies.append(
            pltpu.make_async_copy(rows, packed.at[:, at : at + width], sems.at[number])
        )
        copies[-1].start()
        at += width
    fetch.wait()
    row = lax.broadcasted_iota(jnp.int32, (count, LANES), 0)
    lane = lax.broadcasted_iota(jnp.int32, (count, LANES), 1)
    slots = jnp.zeros((count, LANES), F32)
    for k in range(few):
        here = (row == 0) & (lane == lax.axis_index("panel") * few + k)
        slots = jnp.where(here, requests[0, k].astype(F32), slots)
    packed[:, at:] = slots
    for copy in copies:
        copy.wait()


def move_pieces(numbers, pieces, d_high, d_low, c_high, c_low, side):
    size = d_high.shape[0]
    cols = side.shape[1] - LANES
    core = lax.rem(lax.axis_index("panel"), 2)
    place = lax.div(lax.axis_index("panel"), 2)
    unit_rows = size // 32
    step = 16
    groups = size // LANES

    def move(piece, start, to):
        def body(i, _):
            rows = pl.ds(pl.multiple_of(to + i * step, step), step)
            held = piece.at[pl.ds(pl.multiple_of(start + i * step, step), step)]
            c_high[rows, :], c_low[rows, :] = split(held[:, 0:size])
            side[rows, 0:cols] = held[:, size : size + cols]
            for k in range(SENT_GROUPS):
                at = lax.rem(lax.div(to, LANES) + k, groups) * LANES
                where = pl.ds(pl.multiple_of(at, LANES), LANES)
                own = size + cols + k * LANES
                d_high[rows, where], d_low[rows, where] = split(held[:, own : own + LANES])
            side[rows, cols:] = held[:, size + cols + SENT_GROUPS * LANES :]
            return 0

        lax.fori_loop(0, unit_rows // step, body, 0)

    for number, held in zip(numbers, pieces):
        sibling = number // len(PIECES)
        line, units = PIECES[number % len(PIECES)]
        for place_in, unit in enumerate(units):
            offset = jnp.where(
                core == sibling, offset_of(0, line, unit), offset_of(1, line, unit)
            )
            owner = lax.bitwise_xor(place, offset) * 2 + lax.bitwise_xor(core, sibling)
            move(held, place_in * unit_rows, owner * unit_rows)


EARLY = (0, 1, 2, 3, 4, 5, 10, 11, 12, 13, 14, 15)
LATE = tuple(number for number in range(2 * len(PIECES)) if number not in EARLY)


def early_kernel(*refs):
    count = len(EARLY)
    move_pieces(EARLY, refs[:count], *refs[count:])


def late_kernel(*refs):
    count = len(LATE)
    side = refs[count + 4]
    d_high, d_low, c_high, c_low, source, diag, wanted = refs[count + 5 :]
    size = d_high.shape[0]
    groups = size // LANES
    cols = side.shape[1] - LANES
    move_pieces(LATE, refs[:count], d_high, d_low, c_high, c_low, side)

    for group in range(groups):
        for k in range(1, groups - SENT_GROUPS + 1):
            rows = slice(group * LANES, (group + 1) * LANES)
            where = (group + k) % groups * LANES
            where = slice(where, where + LANES)
            block = d_high[rows, where].astype(F32) + d_low[rows, where].astype(F32)
            d_high[where, rows], d_low[where, rows] = split(block.T)

    pick = lax.broadcasted_iota(jnp.int32, (8, cols), 1) == (
        lax.broadcasted_iota(jnp.int32, (8, cols), 0) + lax.axis_index("panel") * 8
    )
    own = lax.dot_general(
        pick.astype(F32),
        side[:, 0:cols],
        (((1,), (1,)), ((), ())),
        precision=lax.Precision.HIGHEST,
        preferred_element_type=F32,
    )
    source[...] = own
    eye = lax.broadcasted_iota(jnp.int32, (LANES, LANES), 0) == lax.broadcasted_iota(
        jnp.int32, (LANES, LANES), 1
    )
    for start in range(0, size, LANES):
        tiles = slice(start, start + LANES)
        tile = d_high[tiles, tiles].astype(F32) + d_low[tiles, tiles].astype(F32)
        line = jnp.sum(jnp.where(eye, tile, 0.0), axis=0, keepdims=True)
        diag[:, start : start + LANES] = jnp.broadcast_to(line, (8, LANES))
    line = jnp.sum(side[:, cols : cols + LANES], axis=0, keepdims=True)
    wanted[...] = jnp.broadcast_to(line, (8, LANES))


def hop(block, here, there):
    other = [k for k in range(4) if k not in (here, there)]
    route = [(here, there), (there, here), tuple(other), tuple(other[::-1])]
    return lax.ppermute(block, "depth", route)


def taken(plane, planes, refs):
    total = jnp.zeros_like(refs[0])
    for meant, ref in zip(planes, refs):
        total = jnp.where(plane == meant, ref[...], total)
    return total


def forward_kernel(stage, d_high, d_low, c_high, c_low, source, diag, *refs):
    @pl.when(lax.axis_index("depth") == stage)
    def _():
        right_hand = source[...] - refs[0][...] if stage else source[...]
        forward = jacobi(right_hand, diag[...], d_high, d_low)
        refs[-1][...] = product(forward, c_high, c_low)


def transpose_kernel(last, high, low, high_turned, low_turned):
    @pl.when(lax.axis_index("depth") != last)
    def _():
        for ref, turned in ((high, high_turned), (low, low_turned)):
            for row in range(0, ref.shape[0], LANES):
                for col in range(0, ref.shape[1], LANES):
                    block = ref[row : row + LANES, col : col + LANES].astype(F32)
                    turned[col : col + LANES, row : row + LANES] = block.T.astype(BF16)


def turn_kernel(count, d_high, d_low, source, diag, *refs):
    right_hand = source[...] - taken(lax.axis_index("depth"), range(1, count + 1), refs[:count])
    refs[count][...] = right_hand

    @pl.when(lax.axis_index("depth") == count)
    def _():
        refs[count + 1][...] = jacobi(right_hand, diag[...], d_high, d_low)


def backward_kernel(plane, d_high, d_low, c_high, c_low, right_hand, diag, ahead, panel):
    @pl.when(lax.axis_index("depth") == plane)
    def _():
        rest = right_hand[...] - product(ahead[...], c_high, c_low)
        panel[...] = jacobi(rest, diag[...], d_high, d_low)


def last_kernel(count, d_high, d_low, c_high, c_low, right_hand, diag, wanted, *refs):
    ahead = taken(lax.axis_index("depth"), range(count - 1, -1, -1), refs[:count])
    coupled = jnp.where(lax.axis_index("depth") == count, 0.0, product(ahead, c_high, c_low))
    panel = jacobi(right_hand[...] - coupled, diag[...], d_high, d_low)
    size = panel.shape[1]
    high = panel.astype(BF16)
    rest = panel - high.astype(F32)
    middle = rest.astype(BF16)
    low = (rest - middle.astype(F32)).astype(BF16)
    line = wanted[0:1, :].astype(jnp.int32)
    chosen = (lax.broadcasted_iota(jnp.int32, (size, LANES), 0) == line).astype(BF16)
    parts = [jnp.dot(part, chosen, preferred_element_type=F32) for part in (high, middle, low)]
    picked = parts[0] + parts[1] + parts[2]
    send = refs[count]
    blocks = send.shape[0]
    own, few = size // blocks, LANES // blocks
    filler = jnp.zeros((8, LANES - own - few), F32)
    for block in range(blocks):
        send[block] = jnp.concatenate(
            [
                panel[:, block * own : (block + 1) * own],
                picked[:, block * few : (block + 1) * few],
                filler,
            ],
            1,
        )


def unpack_kernel(got, panels, picked):
    turned = got[...].T
    own = panels.shape[0]
    panels[...] = turned[:own]
    picked[...] = turned[own : own + picked.shape[0]]


def vmem(shape, dtype=F32):
    return pltpu.VMEM(shape, dtype)


def call(kernel, out_shape, *args, aliases=None, limit=8):
    args = [pltpu.with_memory_space_constraint(arg, pltpu.VMEM) for arg in args]
    space = pl.BlockSpec(memory_space=pltpu.VMEM)
    return pl.pallas_call(
        kernel,
        out_shape=out_shape,
        in_specs=[space] * len(args),
        out_specs=jax.tree.map(lambda _: space, out_shape),
        input_output_aliases=aliases or {},
        compiler_params=pltpu.CompilerParams(vmem_limit_bytes=limit * 1024 * 1024),
    )(*args)


def per_device(diag_blocks, coupling, sources, requests):
    rows, size, cols = diag_blocks.shape[1], diag_blocks.shape[2], sources.shape[2]
    few = requests.shape[1]
    width = size + cols + (SENT_GROUPS + 1) * LANES
    far = pl.BlockSpec(memory_space=pltpu.HBM)
    operands = (requests, diag_blocks[0], coupling[0], sources[0])
    packed = pl.pallas_call(
        pack_kernel,
        out_shape=vmem((rows, width)),
        in_specs=[far] * 4,
        out_specs=pl.BlockSpec(memory_space=pltpu.VMEM),
        scratch_shapes=[pltpu.SMEM(requests.shape, jnp.int32), pltpu.SemaphoreType.DMA((3 + SENT_GROUPS,))],
        compiler_params=pltpu.CompilerParams(vmem_limit_bytes=8 * 1024 * 1024),
    )(*[pltpu.with_memory_space_constraint(x, pltpu.HBM) for x in operands])
    pieces = gathered(packed)

    vec = vmem((8, size))
    mat = vmem((size, size), BF16)
    filled = call(
        early_kernel,
        (mat, mat, mat, mat, vmem((size, cols + LANES))),
        *[pieces[number] for number in EARLY],
    )
    d_high, d_low, c_high, c_low, source, diag, wanted = call(
        late_kernel,
        (mat, mat, mat, mat, vec, vec, vmem((8, LANES))),
        *[pieces[number] for number in LATE],
        *filled,
        aliases={len(LATE) + number: number for number in range(4)},
    )
    mats = (d_high, d_low, c_high, c_low)

    last = 3
    lefts = []
    for k in range(last):
        carried = call(
            functools.partial(forward_kernel, k),
            vec, *mats, source, diag, *lefts[-1:],
        )
        lefts.append(hop(carried, k, k + 1))
    turned = call(functools.partial(transpose_kernel, last), (mat, mat), c_high, c_low)
    right_hand, panel = call(
        functools.partial(turn_kernel, last),
        (vec, vec), d_high, d_low, source, diag, *lefts,
    )
    aheads = []
    for k in range(last - 1, -1, -1):
        aheads.append(hop(panel, k + 1, k))
        if k > 0:
            panel = call(
                functools.partial(backward_kernel, k),
                vec, d_high, d_low, *turned, right_hand, diag, aheads[-1],
            )
    send = call(
        functools.partial(last_kernel, last),
        vmem((size // rows, 8, LANES)),
        d_high, d_low, *turned, right_hand, diag, wanted, *aheads,
    )
    got = lax.all_to_all(send, "panel", 0, 0, tiled=True).reshape(cols, LANES)
    panels, picked = call(
        unpack_kernel,
        (jax.ShapeDtypeStruct((rows, cols), F32), jax.ShapeDtypeStruct((few, cols), F32)),
        got,
    )
    return panels[None], picked[None]


def solution(mesh):
    placed = (
        P("depth", "panel", None),
        P("depth", "panel", None),
        P("depth", "panel", None),
        P("depth", "panel"),
    )
    return jax.shard_map(
        per_device,
        mesh=mesh,
        in_specs=placed,
        out_specs=(P("depth", "panel", None), P("depth", "panel", None)),
        check_vma=False,
    )
```

```python
import functools

import jax
import jax.numpy as jnp
from jax import lax
from jax.experimental import pallas as pl
from jax.experimental.pallas import tpu as pltpu
from jax.sharding import PartitionSpec as P


ITERS = 2
F32, BF16 = jnp.float32, jnp.bfloat16
LANES = 128
SENT_GROUPS = 5

AXES = ((1, 3, 2), (4, 12, 8))
SIBLINGS = [(p, p ^ 1) for p in range(32)]


def from_partner(block, phase, number):
    pairs = [
        (yz * 2 + core, (yz ^ AXES[core ^ phase][number]) * 2 + core)
        for yz in range(16)
        for core in range(2)
    ]
    return lax.ppermute(block, "panel", pairs)


def join_kernel(first, second, both):
    rows = first.shape[0]
    both[:rows] = first[...]
    both[rows:] = second[...]


def cut_kernel(part, both, one):
    rows = one.shape[0]
    one[...] = both[part * rows : (part + 1) * rows]


def cut(both, part):
    shape = (both.shape[0] // 2, both.shape[1])
    return call(functools.partial(cut_kernel, part), vmem(shape), both)


def joined(first, second):
    return call(join_kernel, vmem((first.shape[0] * 2, first.shape[1])), first, second)


PIECES = (
    (None, (0, 1)), (None, (2, 3)), (0, (0, 1)), (1, (0, 1)), (0, (2, 3)), (1, (2, 3)),
    (2, (0,)), (2, (1,)), (2, (2,)), (2, (3,)),
)


def offset_of(core, line, unit):
    offset = (0, *AXES[core])[unit]
    return offset ^ (0 if line is None else AXES[1 - core][line])


def gathered(own):
    near = from_partner(own, 0, 0)
    other = from_partner(own, 0, 1)
    far = from_partner(own, 0, 2)
    a = joined(own, near)
    a1, a0 = from_partner(a, 1, 1), from_partner(a, 1, 0)
    b = joined(other, far)
    b0, b1 = from_partner(b, 1, 0), from_partner(b, 1, 1)
    far_pieces = [
        from_partner(cut(a1, 0), 1, 0),
        from_partner(cut(a0, 1), 1, 1),
        from_partner(cut(b0, 0), 1, 1),
        from_partner(cut(b1, 1), 1, 0),
    ]
    pieces = [a, b, a0, a1, b0, b1, *far_pieces]
    sibling = []
    for piece in pieces:
        sibling.append(lax.ppermute(piece, "panel", SIBLINGS))
    return pieces + sibling


def split(x):
    high = x.astype(BF16)
    return high, (x - high.astype(F32)).astype(BF16)


def product(x, high_ref, low_ref):
    rows = x.shape[0]
    both = jnp.concatenate(split(x), 0)
    dims = (((1,), (0,)), ((), ()))
    first = lax.dot_general(both, high_ref[...], dims, preferred_element_type=F32)
    second = lax.dot_general(both, low_ref[...], dims, preferred_element_type=F32)
    total = first + second
    return total[:rows] + total[rows:]


def jacobi(right_hand, diag, d_high, d_low):
    iterate = right_hand / diag
    for _ in range(ITERS):
        image = product(iterate, d_high, d_low)
        iterate = iterate + (right_hand - image) / diag
    return iterate


def pack_kernel(asked, diag_rows, coupling_rows, source_rows, packed, requests, sems):
    few = requests.shape[1]
    fetch = pltpu.make_async_copy(asked, requests, sems.at[2 + SENT_GROUPS])
    fetch.start()
    count, size = diag_rows.shape
    cols = source_rows.shape[1]
    sent = [(coupling_rows, size), (source_rows, cols)]
    group = lax.div(lax.axis_index("panel") * count, LANES)
    for k in range(SENT_GROUPS):
        start = lax.rem(group + k, size // LANES) * LANES
        sent.append((diag_rows.at[:, pl.ds(pl.multiple_of(start, LANES), LANES)], LANES))
    copies = []
    at = 0
    for number, (rows, width) in enumerate(sent):
        copies.append(
            pltpu.make_async_copy(rows, packed.at[:, at : at + width], sems.at[number])
        )
        copies[-1].start()
        at += width
    fetch.wait()
    row = lax.broadcasted_iota(jnp.int32, (count, LANES), 0)
    lane = lax.broadcasted_iota(jnp.int32, (count, LANES), 1)
    slots = jnp.zeros((count, LANES), F32)
    for k in range(few):
        here = (row == 0) & (lane == lax.axis_index("panel") * few + k)
        slots = jnp.where(here, requests[0, k].astype(F32), slots)
    packed[:, at:] = slots
    for copy in copies:
        copy.wait()


def move_pieces(numbers, pieces, d_high, d_low, c_high, c_low, side):
    size = d_high.shape[0]
    cols = side.shape[1] - LANES
    core = lax.rem(lax.axis_index("panel"), 2)
    place = lax.div(lax.axis_index("panel"), 2)
    unit_rows = size // 32
    step = 16
    groups = size // LANES

    def move(piece, start, to):
        def body(i, _):
            rows = pl.ds(pl.multiple_of(to + i * step, step), step)
            held = piece.at[pl.ds(pl.multiple_of(start + i * step, step), step)]
            c_high[rows, :], c_low[rows, :] = split(held[:, 0:size])
            side[rows, 0:cols] = held[:, size : size + cols]
            for k in range(SENT_GROUPS):
                at = lax.rem(lax.div(to, LANES) + k, groups) * LANES
                where = pl.ds(pl.multiple_of(at, LANES), LANES)
                own = size + cols + k * LANES
                d_high[rows, where], d_low[rows, where] = split(held[:, own : own + LANES])
            side[rows, cols:] = held[:, size + cols + SENT_GROUPS * LANES :]
            return 0

        lax.fori_loop(0, unit_rows // step, body, 0)

    for number, held in zip(numbers, pieces):
        sibling = number // len(PIECES)
        line, units = PIECES[number % len(PIECES)]
        for place_in, unit in enumerate(units):
            offset = jnp.where(
                core == sibling, offset_of(0, line, unit), offset_of(1, line, unit)
            )
            owner = lax.bitwise_xor(place, offset) * 2 + lax.bitwise_xor(core, sibling)
            move(held, place_in * unit_rows, owner * unit_rows)


EARLY = (0, 1, 2, 3, 4, 5, 10, 11, 12, 13, 14, 15)
LATE = tuple(number for number in range(2 * len(PIECES)) if number not in EARLY)


def early_kernel(*refs):
    count = len(EARLY)
    move_pieces(EARLY, refs[:count], *refs[count:])


def late_kernel(*refs):
    count = len(LATE)
    side = refs[count + 4]
    d_high, d_low, c_high, c_low, source, diag, wanted, flipped = refs[count + 5 :]
    size = d_high.shape[0]
    groups = size // LANES
    cols = side.shape[1] - LANES
    move_pieces(LATE, refs[:count], d_high, d_low, c_high, c_low, side)

    for group in range(groups):
        for k in range(1, groups - SENT_GROUPS + 1):
            rows = slice(group * LANES, (group + 1) * LANES)
            where = (group + k) % groups * LANES
            where = slice(where, where + LANES)
            block = d_high[rows, where].astype(F32) + d_low[rows, where].astype(F32)
            d_high[where, rows], d_low[where, rows] = split(block.T)

    first = lax.axis_index("panel") * 8
    group = pl.ds(pl.multiple_of(lax.div(first, LANES) * LANES, LANES), LANES)
    for start in range(0, size, LANES):
        flipped[:, start : start + LANES] = side[start : start + LANES, group].T
    source[...] = flipped[pl.ds(pl.multiple_of(lax.rem(first, LANES), 8), 8), :]
    eye = lax.broadcasted_iota(jnp.int32, (LANES, LANES), 0) == lax.broadcasted_iota(
        jnp.int32, (LANES, LANES), 1
    )
    for start in range(0, size, LANES):
        tiles = slice(start, start + LANES)
        tile = d_high[tiles, tiles].astype(F32) + d_low[tiles, tiles].astype(F32)
        line = jnp.sum(jnp.where(eye, tile, 0.0), axis=0, keepdims=True)
        diag[:, start : start + LANES] = jnp.broadcast_to(line, (8, LANES))
    line = jnp.sum(side[:, cols : cols + LANES], axis=0, keepdims=True)
    wanted[...] = jnp.broadcast_to(line, (8, LANES))


def hop(block, here, there):
    other = [k for k in range(4) if k not in (here, there)]
    route = [(here, there), (there, here), tuple(other), tuple(other[::-1])]
    return lax.ppermute(block, "depth", route)


def taken(plane, planes, refs):
    total = jnp.zeros_like(refs[0])
    for meant, ref in zip(planes, refs):
        total = jnp.where(plane == meant, ref[...], total)
    return total


def forward_kernel(stage, d_high, d_low, c_high, c_low, source, diag, *refs):
    @pl.when(lax.axis_index("depth") == stage)
    def _():
        right_hand = source[...] - refs[0][...] if stage else source[...]
        forward = jacobi(right_hand, diag[...], d_high, d_low)
        refs[-1][...] = product(forward, c_high, c_low)


def transpose_kernel(last, high, low, high_turned, low_turned):
    @pl.when(lax.axis_index("depth") != last)
    def _():
        for ref, turned in ((high, high_turned), (low, low_turned)):
            for row in range(0, ref.shape[0], LANES):
                for col in range(0, ref.shape[1], LANES):
                    block = ref[row : row + LANES, col : col + LANES].astype(F32)
                    turned[col : col + LANES, row : row + LANES] = block.T.astype(BF16)


def turn_kernel(count, d_high, d_low, source, diag, *refs):
    right_hand = source[...] - taken(lax.axis_index("depth"), range(1, count + 1), refs[:count])
    refs[count][...] = right_hand

    @pl.when(lax.axis_index("depth") == count)
    def _():
        refs[count + 1][...] = jacobi(right_hand, diag[...], d_high, d_low)


def backward_kernel(plane, d_high, d_low, c_high, c_low, right_hand, diag, ahead, panel):
    @pl.when(lax.axis_index("depth") == plane)
    def _():
        rest = right_hand[...] - product(ahead[...], c_high, c_low)
        panel[...] = jacobi(rest, diag[...], d_high, d_low)


def last_kernel(count, d_high, d_low, c_high, c_low, right_hand, diag, wanted, *refs):
    ahead = taken(lax.axis_index("depth"), range(count - 1, -1, -1), refs[:count])
    coupled = jnp.where(lax.axis_index("depth") == count, 0.0, product(ahead, c_high, c_low))
    panel = jacobi(right_hand[...] - coupled, diag[...], d_high, d_low)
    size = panel.shape[1]
    high = panel.astype(BF16)
    rest = panel - high.astype(F32)
    middle = rest.astype(BF16)
    low = (rest - middle.astype(F32)).astype(BF16)
    line = wanted[0:1, :].astype(jnp.int32)
    chosen = (lax.broadcasted_iota(jnp.int32, (size, LANES), 0) == line).astype(BF16)
    parts = [jnp.dot(part, chosen, preferred_element_type=F32) for part in (high, middle, low)]
    picked = parts[0] + parts[1] + parts[2]
    send = refs[count]
    blocks = send.shape[0]
    own, few = size // blocks, LANES // blocks
    filler = jnp.zeros((8, LANES - own - few), F32)
    for block in range(blocks):
        send[block] = jnp.concatenate(
            [
                panel[:, block * own : (block + 1) * own],
                picked[:, block * few : (block + 1) * few],
                filler,
            ],
            1,
        )


def unpack_kernel(got, panels, picked):
    turned = got[...].T
    own = panels.shape[0]
    panels[...] = turned[:own]
    picked[...] = turned[own : own + picked.shape[0]]


def vmem(shape, dtype=F32):
    return pltpu.VMEM(shape, dtype)


def call(kernel, out_shape, *args, aliases=None, scratch=(), limit=8):
    args = [pltpu.with_memory_space_constraint(arg, pltpu.VMEM) for arg in args]
    space = pl.BlockSpec(memory_space=pltpu.VMEM)
    return pl.pallas_call(
        kernel,
        out_shape=out_shape,
        in_specs=[space] * len(args),
        out_specs=jax.tree.map(lambda _: space, out_shape),
        input_output_aliases=aliases or {},
        scratch_shapes=scratch,
        compiler_params=pltpu.CompilerParams(vmem_limit_bytes=limit * 1024 * 1024),
    )(*args)


def per_device(diag_blocks, coupling, sources, requests):
    rows, size, cols = diag_blocks.shape[1], diag_blocks.shape[2], sources.shape[2]
    few = requests.shape[1]
    width = size + cols + (SENT_GROUPS + 1) * LANES
    far = pl.BlockSpec(memory_space=pltpu.HBM)
    operands = (requests, diag_blocks[0], coupling[0], sources[0])
    packed = pl.pallas_call(
        pack_kernel,
        out_shape=vmem((rows, width)),
        in_specs=[far] * 4,
        out_specs=pl.BlockSpec(memory_space=pltpu.VMEM),
        scratch_shapes=[pltpu.SMEM(requests.shape, jnp.int32), pltpu.SemaphoreType.DMA((3 + SENT_GROUPS,))],
        compiler_params=pltpu.CompilerParams(vmem_limit_bytes=8 * 1024 * 1024),
    )(*[pltpu.with_memory_space_constraint(x, pltpu.HBM) for x in operands])
    pieces = gathered(packed)

    vec = vmem((8, size))
    mat = vmem((size, size), BF16)
    filled = call(
        early_kernel,
        (mat, mat, mat, mat, vmem((size, cols + LANES))),
        *[pieces[number] for number in EARLY],
    )
    d_high, d_low, c_high, c_low, source, diag, wanted = call(
        late_kernel,
        (mat, mat, mat, mat, vec, vec, vmem((8, LANES))),
        *[pieces[number] for number in LATE],
        *filled,
        aliases={len(LATE) + number: number for number in range(4)},
        scratch=[pltpu.VMEM((LANES, size), F32)],
    )
    mats = (d_high, d_low, c_high, c_low)

    last = 3
    lefts = []
    for k in range(last):
        carried = call(
            functools.partial(forward_kernel, k),
            vec, *mats, source, diag, *lefts[-1:],
        )
        lefts.append(hop(carried, k, k + 1))
    turned = call(functools.partial(transpose_kernel, last), (mat, mat), c_high, c_low)
    right_hand, panel = call(
        functools.partial(turn_kernel, last),
        (vec, vec), d_high, d_low, source, diag, *lefts,
    )
    aheads = []
    for k in range(last - 1, -1, -1):
        aheads.append(hop(panel, k + 1, k))
        if k > 0:
            panel = call(
                functools.partial(backward_kernel, k),
                vec, d_high, d_low, *turned, right_hand, diag, aheads[-1],
            )
    send = call(
        functools.partial(last_kernel, last),
        vmem((size // rows, 8, LANES)),
        d_high, d_low, *turned, right_hand, diag, wanted, *aheads,
    )
    got = lax.all_to_all(send, "panel", 0, 0, tiled=True).reshape(cols, LANES)
    panels, picked = call(
        unpack_kernel,
        (jax.ShapeDtypeStruct((rows, cols), F32), jax.ShapeDtypeStruct((few, cols), F32)),
        got,
    )
    return panels[None], picked[None]


def solution(mesh):
    placed = (
        P("depth", "panel", None),
        P("depth", "panel", None),
        P("depth", "panel", None),
        P("depth", "panel"),
    )
    return jax.shard_map(
        per_device,
        mesh=mesh,
        in_specs=placed,
        out_specs=(P("depth", "panel", None), P("depth", "panel", None)),
        check_vma=False,
    )
```

```python
import functools

import jax
import jax.numpy as jnp
from jax import lax
from jax.experimental import pallas as pl
from jax.experimental.pallas import tpu as pltpu
from jax.sharding import PartitionSpec as P


ITERS = 2
F32, BF16 = jnp.float32, jnp.bfloat16
LANES = 128
SENT_GROUPS = 5

AXES = ((1, 3, 2), (4, 12, 8))
SIBLINGS = [(p, p ^ 1) for p in range(32)]


def from_partner(block, phase, number):
    pairs = [
        (yz * 2 + core, (yz ^ AXES[core ^ phase][number]) * 2 + core)
        for yz in range(16)
        for core in range(2)
    ]
    return lax.ppermute(block, "panel", pairs)


def join_kernel(first, second, both):
    rows = first.shape[0]
    both[:rows] = first[...]
    both[rows:] = second[...]


def cut_kernel(part, both, one):
    rows = one.shape[0]
    one[...] = both[part * rows : (part + 1) * rows]


def cut(both, part):
    shape = (both.shape[0] // 2, both.shape[1])
    return call(functools.partial(cut_kernel, part), vmem(shape), both)


def joined(first, second):
    return call(join_kernel, vmem((first.shape[0] * 2, first.shape[1])), first, second)


PIECES = (
    (None, (0, 1)), (None, (2, 3)), (0, (0, 1)), (1, (0, 1)), (0, (2, 3)), (1, (2, 3)),
    (2, (0,)), (2, (1,)), (2, (2,)), (2, (3,)),
)


def offset_of(core, line, unit):
    offset = (0, *AXES[core])[unit]
    return offset ^ (0 if line is None else AXES[1 - core][line])


def gathered(own):
    near = from_partner(own, 0, 0)
    other = from_partner(own, 0, 1)
    far = from_partner(own, 0, 2)
    a = joined(own, near)
    a1, a0 = from_partner(a, 1, 1), from_partner(a, 1, 0)
    b = joined(other, far)
    b0, b1 = from_partner(b, 1, 0), from_partner(b, 1, 1)
    far_pieces = [
        from_partner(cut(a1, 0), 1, 0),
        from_partner(cut(a0, 1), 1, 1),
        from_partner(cut(b0, 0), 1, 1),
        from_partner(cut(b1, 1), 1, 0),
    ]
    pieces = [a, b, a0, a1, b0, b1, *far_pieces]
    sibling = []
    for piece in pieces:
        sibling.append(lax.ppermute(piece, "panel", SIBLINGS))
    return pieces + sibling


def split(x):
    high = x.astype(BF16)
    return high, (x - high.astype(F32)).astype(BF16)


def product(x, high_ref, low_ref):
    rows = x.shape[0]
    both = jnp.concatenate(split(x), 0)
    dims = (((1,), (0,)), ((), ()))
    first = lax.dot_general(both, high_ref[...], dims, preferred_element_type=F32)
    second = lax.dot_general(both, low_ref[...], dims, preferred_element_type=F32)
    total = first + second
    return total[:rows] + total[rows:]


def jacobi(right_hand, diag, d_high, d_low):
    iterate = right_hand / diag
    for _ in range(ITERS):
        image = product(iterate, d_high, d_low)
        iterate = iterate + (right_hand - image) / diag
    return iterate


def pack_kernel(asked, diag_rows, coupling_rows, source_rows, packed, requests, sems):
    few = requests.shape[1]
    fetch = pltpu.make_async_copy(asked, requests, sems.at[2 + SENT_GROUPS])
    fetch.start()
    count, size = diag_rows.shape
    cols = source_rows.shape[1]
    sent = [(coupling_rows, size), (source_rows, cols)]
    group = lax.div(lax.axis_index("panel") * count, LANES)
    for k in range(SENT_GROUPS):
        start = lax.rem(group + k, size // LANES) * LANES
        sent.append((diag_rows.at[:, pl.ds(pl.multiple_of(start, LANES), LANES)], LANES))
    copies = []
    at = 0
    for number, (rows, width) in enumerate(sent):
        copies.append(
            pltpu.make_async_copy(rows, packed.at[:, at : at + width], sems.at[number])
        )
        copies[-1].start()
        at += width
    fetch.wait()
    row = lax.broadcasted_iota(jnp.int32, (count, LANES), 0)
    lane = lax.broadcasted_iota(jnp.int32, (count, LANES), 1)
    slots = jnp.zeros((count, LANES), F32)
    for k in range(few):
        here = (row == 0) & (lane == lax.axis_index("panel") * few + k)
        slots = jnp.where(here, requests[0, k].astype(F32), slots)
    packed[:, at:] = slots
    for copy in copies:
        copy.wait()


def move_pieces(numbers, pieces, d_high, d_low, c_high, c_low, side):
    size = d_high.shape[0]
    cols = side.shape[1] - LANES
    core = lax.rem(lax.axis_index("panel"), 2)
    place = lax.div(lax.axis_index("panel"), 2)
    unit_rows = size // 32
    step = 16
    groups = size // LANES

    def move(piece, start, to):
        def body(i, _):
            rows = pl.ds(pl.multiple_of(to + i * step, step), step)
            held = piece.at[pl.ds(pl.multiple_of(start + i * step, step), step)]
            c_high[rows, :], c_low[rows, :] = split(held[:, 0:size])
            side[rows, 0:cols] = held[:, size : size + cols]
            for k in range(SENT_GROUPS):
                at = lax.rem(lax.div(to, LANES) + k, groups) * LANES
                where = pl.ds(pl.multiple_of(at, LANES), LANES)
                own = size + cols + k * LANES
                d_high[rows, where], d_low[rows, where] = split(held[:, own : own + LANES])
            side[rows, cols:] = held[:, size + cols + SENT_GROUPS * LANES :]
            return 0

        lax.fori_loop(0, unit_rows // step, body, 0)

    for number, held in zip(numbers, pieces):
        sibling = number // len(PIECES)
        line, units = PIECES[number % len(PIECES)]
        for place_in, unit in enumerate(units):
            offset = jnp.where(
                core == sibling, offset_of(0, line, unit), offset_of(1, line, unit)
            )
            owner = lax.bitwise_xor(place, offset) * 2 + lax.bitwise_xor(core, sibling)
            move(held, place_in * unit_rows, owner * unit_rows)


EARLY = (0, 1, 2, 3, 4, 5, 10, 11, 12, 13, 14, 15)
LATE = tuple(number for number in range(2 * len(PIECES)) if number not in EARLY)


def early_kernel(*refs):
    count = len(EARLY)
    move_pieces(EARLY, refs[:count], *refs[count:])


def late_kernel(*refs):
    count = len(LATE)
    d_high, d_low, c_high, c_low, side, source, diag, flipped = refs[count + 5 :]
    size = d_high.shape[0]
    groups = size // LANES
    move_pieces(LATE, refs[:count], d_high, d_low, c_high, c_low, side)

    for group in range(groups):
        for k in range(1, groups - SENT_GROUPS + 1):
            rows = slice(group * LANES, (group + 1) * LANES)
            where = (group + k) % groups * LANES
            where = slice(where, where + LANES)
            block = d_high[rows, where].astype(F32) + d_low[rows, where].astype(F32)
            d_high[where, rows], d_low[where, rows] = split(block.T)

    first = lax.axis_index("panel") * 8
    group = pl.ds(pl.multiple_of(lax.div(first, LANES) * LANES, LANES), LANES)
    for start in range(0, size, LANES):
        flipped[:, start : start + LANES] = side[start : start + LANES, group].T
    source[...] = flipped[pl.ds(pl.multiple_of(lax.rem(first, LANES), 8), 8), :]
    eye = lax.broadcasted_iota(jnp.int32, (LANES, LANES), 0) == lax.broadcasted_iota(
        jnp.int32, (LANES, LANES), 1
    )
    for start in range(0, size, LANES):
        tiles = slice(start, start + LANES)
        tile = d_high[tiles, tiles].astype(F32) + d_low[tiles, tiles].astype(F32)
        line = jnp.sum(jnp.where(eye, tile, 0.0), axis=0, keepdims=True)
        diag[:, start : start + LANES] = jnp.broadcast_to(line, (8, LANES))


def hop(block, here, there):
    other = [k for k in range(4) if k not in (here, there)]
    route = [(here, there), (there, here), tuple(other), tuple(other[::-1])]
    return lax.ppermute(block, "depth", route)


def taken(plane, planes, refs):
    total = jnp.zeros_like(refs[0])
    for meant, ref in zip(planes, refs):
        total = jnp.where(plane == meant, ref[...], total)
    return total


def forward_kernel(stage, d_high, d_low, c_high, c_low, source, diag, *refs):
    @pl.when(lax.axis_index("depth") == stage)
    def _():
        right_hand = source[...] - refs[0][...] if stage else source[...]
        forward = jacobi(right_hand, diag[...], d_high, d_low)
        refs[-1][...] = product(forward, c_high, c_low)


def transpose_kernel(last, high, low, side, high_turned, low_turned, chosen):
    line = jnp.sum(side[:, side.shape[1] - LANES :], axis=0, keepdims=True).astype(jnp.int32)
    row = lax.broadcasted_iota(jnp.int32, chosen.shape, 0)
    chosen[...] = (row == line).astype(BF16)

    @pl.when(lax.axis_index("depth") != last)
    def _():
        for ref, turned in ((high, high_turned), (low, low_turned)):
            for row in range(0, ref.shape[0], LANES):
                for col in range(0, ref.shape[1], LANES):
                    block = ref[row : row + LANES, col : col + LANES].astype(F32)
                    turned[col : col + LANES, row : row + LANES] = block.T.astype(BF16)


def turn_kernel(count, d_high, d_low, source, diag, *refs):
    right_hand = source[...] - taken(lax.axis_index("depth"), range(1, count + 1), refs[:count])
    refs[count][...] = right_hand

    @pl.when(lax.axis_index("depth") == count)
    def _():
        refs[count + 1][...] = jacobi(right_hand, diag[...], d_high, d_low)


def backward_kernel(plane, d_high, d_low, c_high, c_low, right_hand, diag, ahead, panel):
    @pl.when(lax.axis_index("depth") == plane)
    def _():
        rest = right_hand[...] - product(ahead[...], c_high, c_low)
        panel[...] = jacobi(rest, diag[...], d_high, d_low)


def last_kernel(count, d_high, d_low, c_high, c_low, right_hand, diag, chosen, *refs):
    ahead = taken(lax.axis_index("depth"), range(count - 1, -1, -1), refs[:count])
    coupled = jnp.where(lax.axis_index("depth") == count, 0.0, product(ahead, c_high, c_low))
    panel = jacobi(right_hand[...] - coupled, diag[...], d_high, d_low)
    size = panel.shape[1]
    high = panel.astype(BF16)
    rest = panel - high.astype(F32)
    middle = rest.astype(BF16)
    low = (rest - middle.astype(F32)).astype(BF16)
    parts = [jnp.dot(part, chosen[...], preferred_element_type=F32) for part in (high, middle, low)]
    picked = parts[0] + parts[1] + parts[2]
    send = refs[count]
    blocks = send.shape[0]
    own, few = size // blocks, LANES // blocks
    filler = jnp.zeros((8, LANES - own - few), F32)
    for block in range(blocks):
        send[block] = jnp.concatenate(
            [
                panel[:, block * own : (block + 1) * own],
                picked[:, block * few : (block + 1) * few],
                filler,
            ],
            1,
        )


def unpack_kernel(got, panels, picked):
    turned = got[...].T
    own = panels.shape[0]
    panels[...] = turned[:own]
    picked[...] = turned[own : own + picked.shape[0]]


def vmem(shape, dtype=F32):
    return pltpu.VMEM(shape, dtype)


def call(kernel, out_shape, *args, aliases=None, scratch=(), limit=8):
    args = [pltpu.with_memory_space_constraint(arg, pltpu.VMEM) for arg in args]
    space = pl.BlockSpec(memory_space=pltpu.VMEM)
    return pl.pallas_call(
        kernel,
        out_shape=out_shape,
        in_specs=[space] * len(args),
        out_specs=jax.tree.map(lambda _: space, out_shape),
        input_output_aliases=aliases or {},
        scratch_shapes=scratch,
        compiler_params=pltpu.CompilerParams(vmem_limit_bytes=limit * 1024 * 1024),
    )(*args)


def per_device(diag_blocks, coupling, sources, requests):
    rows, size, cols = diag_blocks.shape[1], diag_blocks.shape[2], sources.shape[2]
    few = requests.shape[1]
    width = size + cols + (SENT_GROUPS + 1) * LANES
    far = pl.BlockSpec(memory_space=pltpu.HBM)
    operands = (requests, diag_blocks[0], coupling[0], sources[0])
    packed = pl.pallas_call(
        pack_kernel,
        out_shape=vmem((rows, width)),
        in_specs=[far] * 4,
        out_specs=pl.BlockSpec(memory_space=pltpu.VMEM),
        scratch_shapes=[pltpu.SMEM(requests.shape, jnp.int32), pltpu.SemaphoreType.DMA((3 + SENT_GROUPS,))],
        compiler_params=pltpu.CompilerParams(vmem_limit_bytes=8 * 1024 * 1024),
    )(*[pltpu.with_memory_space_constraint(x, pltpu.HBM) for x in operands])
    pieces = gathered(packed)

    vec = vmem((8, size))
    mat = vmem((size, size), BF16)
    filled = call(
        early_kernel,
        (mat, mat, mat, mat, vmem((size, cols + LANES))),
        *[pieces[number] for number in EARLY],
    )
    d_high, d_low, c_high, c_low, side, source, diag = call(
        late_kernel,
        (mat, mat, mat, mat, vmem((size, cols + LANES)), vec, vec),
        *[pieces[number] for number in LATE],
        *filled,
        aliases={len(LATE) + number: number for number in range(5)},
        scratch=[pltpu.VMEM((LANES, size), F32)],
    )
    mats = (d_high, d_low, c_high, c_low)

    last = 3
    lefts = []
    for k in range(last):
        carried = call(
            functools.partial(forward_kernel, k),
            vec, *mats, source, diag, *lefts[-1:],
        )
        lefts.append(hop(carried, k, k + 1))
    *turned, chosen = call(
        functools.partial(transpose_kernel, last),
        (mat, mat, vmem((size, LANES), BF16)),
        c_high, c_low, side,
    )
    right_hand, panel = call(
        functools.partial(turn_kernel, last),
        (vec, vec), d_high, d_low, source, diag, *lefts,
    )
    aheads = []
    for k in range(last - 1, -1, -1):
        aheads.append(hop(panel, k + 1, k))
        if k > 0:
            panel = call(
                functools.partial(backward_kernel, k),
                vec, d_high, d_low, *turned, right_hand, diag, aheads[-1],
            )
    send = call(
        functools.partial(last_kernel, last),
        vmem((size // rows, 8, LANES)),
        d_high, d_low, *turned, right_hand, diag, chosen, *aheads,
    )
    got = lax.all_to_all(send, "panel", 0, 0, tiled=True).reshape(cols, LANES)
    panels, picked = call(
        unpack_kernel,
        (jax.ShapeDtypeStruct((rows, cols), F32), jax.ShapeDtypeStruct((few, cols), F32)),
        got,
    )
    return panels[None], picked[None]


def solution(mesh):
    placed = (
        P("depth", "panel", None),
        P("depth", "panel", None),
        P("depth", "panel", None),
        P("depth", "panel"),
    )
    return jax.shard_map(
        per_device,
        mesh=mesh,
        in_specs=placed,
        out_specs=(P("depth", "panel", None), P("depth", "panel", None)),
        check_vma=False,
    )
```

```python
import functools

import jax
import jax.numpy as jnp
from jax import lax
from jax.experimental import pallas as pl
from jax.experimental.pallas import tpu as pltpu
from jax.sharding import PartitionSpec as P


ITERS = 2
F32, BF16 = jnp.float32, jnp.bfloat16
LANES = 128
SENT_GROUPS = 5

AXES = ((1, 3, 2), (4, 12, 8))
SIBLINGS = [(p, p ^ 1) for p in range(32)]


def from_partner(block, phase, number):
    pairs = [
        (yz * 2 + core, (yz ^ AXES[core ^ phase][number]) * 2 + core)
        for yz in range(16)
        for core in range(2)
    ]
    return lax.ppermute(block, "panel", pairs)


def join_kernel(first, second, both):
    rows = first.shape[0]
    both[:rows] = first[...]
    both[rows:] = second[...]


def cut_kernel(part, both, one):
    rows = one.shape[0]
    one[...] = both[part * rows : (part + 1) * rows]


def cut(both, part):
    shape = (both.shape[0] // 2, both.shape[1])
    return call(functools.partial(cut_kernel, part), vmem(shape), both)


def joined(first, second):
    return call(join_kernel, vmem((first.shape[0] * 2, first.shape[1])), first, second)


PIECES = (
    (None, (0, 1)), (None, (2, 3)), (0, (0, 1)), (1, (0, 1)), (0, (2, 3)), (1, (2, 3)),
    (2, (0,)), (2, (1,)), (2, (2,)), (2, (3,)),
)


def offset_of(core, line, unit):
    offset = (0, *AXES[core])[unit]
    return offset ^ (0 if line is None else AXES[1 - core][line])


def gathered(own):
    near = from_partner(own, 0, 0)
    other = from_partner(own, 0, 1)
    far = from_partner(own, 0, 2)
    a = joined(own, near)
    a1, a0 = from_partner(a, 1, 1), from_partner(a, 1, 0)
    b = joined(other, far)
    b0, b1 = from_partner(b, 1, 0), from_partner(b, 1, 1)
    far_pieces = [
        from_partner(cut(a1, 0), 1, 0),
        from_partner(cut(a0, 1), 1, 1),
        from_partner(cut(b0, 0), 1, 1),
        from_partner(cut(b1, 1), 1, 0),
    ]
    pieces = [a, b, a0, a1, b0, b1, *far_pieces]
    sibling = []
    for piece in pieces:
        sibling.append(lax.ppermute(piece, "panel", SIBLINGS))
    return pieces + sibling


def split(x):
    high = x.astype(BF16)
    return high, (x - high.astype(F32)).astype(BF16)


def product(x, high_ref, low_ref):
    rows = x.shape[0]
    both = jnp.concatenate(split(x), 0)
    dims = (((1,), (0,)), ((), ()))
    first = lax.dot_general(both, high_ref[...], dims, preferred_element_type=F32)
    second = lax.dot_general(both, low_ref[...], dims, preferred_element_type=F32)
    total = first + second
    return total[:rows] + total[rows:]


def jacobi(right_hand, diag, d_high, d_low):
    iterate = right_hand / diag
    for _ in range(ITERS):
        image = product(iterate, d_high, d_low)
        iterate = iterate + (right_hand - image) / diag
    return iterate


def pack_kernel(asked, diag_rows, coupling_rows, source_rows, packed, requests, sems):
    few = requests.shape[1]
    fetch = pltpu.make_async_copy(asked, requests, sems.at[2 + SENT_GROUPS])
    fetch.start()
    count, size = diag_rows.shape
    cols = source_rows.shape[1]
    sent = [(coupling_rows, size), (source_rows, cols)]
    group = lax.div(lax.axis_index("panel") * count, LANES)
    for k in range(SENT_GROUPS):
        start = lax.rem(group + k, size // LANES) * LANES
        sent.append((diag_rows.at[:, pl.ds(pl.multiple_of(start, LANES), LANES)], LANES))
    copies = []
    at = 0
    for number, (rows, width) in enumerate(sent):
        copies.append(
            pltpu.make_async_copy(rows, packed.at[:, at : at + width], sems.at[number])
        )
        copies[-1].start()
        at += width
    fetch.wait()
    row = lax.broadcasted_iota(jnp.int32, (count, LANES), 0)
    lane = lax.broadcasted_iota(jnp.int32, (count, LANES), 1)
    slots = jnp.zeros((count, LANES), F32)
    for k in range(few):
        here = (row == 0) & (lane == lax.axis_index("panel") * few + k)
        slots = jnp.where(here, requests[0, k].astype(F32), slots)
    packed[:, at:] = slots
    for copy in copies:
        copy.wait()


def move_pieces(numbers, pieces, d_high, d_low, c_high, c_low, side):
    size = d_high.shape[0]
    cols = side.shape[1] - LANES
    core = lax.rem(lax.axis_index("panel"), 2)
    place = lax.div(lax.axis_index("panel"), 2)
    unit_rows = size // 32
    step = 16
    groups = size // LANES

    def move(piece, start, to):
        def body(i, _):
            rows = pl.ds(pl.multiple_of(to + i * step, step), step)
            held = piece.at[pl.ds(pl.multiple_of(start + i * step, step), step)]
            c_high[rows, :], c_low[rows, :] = split(held[:, 0:size])
            side[rows, 0:cols] = held[:, size : size + cols]
            for k in range(SENT_GROUPS):
                at = lax.rem(lax.div(to, LANES) + k, groups) * LANES
                where = pl.ds(pl.multiple_of(at, LANES), LANES)
                own = size + cols + k * LANES
                d_high[rows, where], d_low[rows, where] = split(held[:, own : own + LANES])
            side[rows, cols:] = held[:, size + cols + SENT_GROUPS * LANES :]
            return 0

        lax.fori_loop(0, unit_rows // step, body, 0)

    for number, held in zip(numbers, pieces):
        sibling = number // len(PIECES)
        line, units = PIECES[number % len(PIECES)]
        for place_in, unit in enumerate(units):
            offset = jnp.where(
                core == sibling, offset_of(0, line, unit), offset_of(1, line, unit)
            )
            owner = lax.bitwise_xor(place, offset) * 2 + lax.bitwise_xor(core, sibling)
            move(held, place_in * unit_rows, owner * unit_rows)


EARLY = (0, 1, 2, 3, 4, 5, 10, 11, 12, 13, 14, 15)
LATE = tuple(number for number in range(2 * len(PIECES)) if number not in EARLY)


def early_kernel(*refs):
    count = len(EARLY)
    move_pieces(EARLY, refs[:count], *refs[count:])


def late_kernel(*refs):
    count = len(LATE)
    d_high, d_low, c_high, c_low, side, source, diag, wanted, flipped = refs[count + 5 :]
    size = d_high.shape[0]
    groups = size // LANES
    cols = side.shape[1] - LANES
    move_pieces(LATE, refs[:count], d_high, d_low, c_high, c_low, side)

    for group in range(groups):
        for k in range(1, groups - SENT_GROUPS + 1):
            rows = slice(group * LANES, (group + 1) * LANES)
            where = (group + k) % groups * LANES
            where = slice(where, where + LANES)
            block = d_high[rows, where].astype(F32) + d_low[rows, where].astype(F32)
            d_high[where, rows], d_low[where, rows] = split(block.T)

    first = lax.axis_index("panel") * 8
    group = pl.ds(pl.multiple_of(lax.div(first, LANES) * LANES, LANES), LANES)
    for start in range(0, size, LANES):
        flipped[:, start : start + LANES] = side[start : start + LANES, group].T
    source[...] = flipped[pl.ds(pl.multiple_of(lax.rem(first, LANES), 8), 8), :]
    eye = lax.broadcasted_iota(jnp.int32, (LANES, LANES), 0) == lax.broadcasted_iota(
        jnp.int32, (LANES, LANES), 1
    )
    for start in range(0, size, LANES):
        tiles = slice(start, start + LANES)
        tile = d_high[tiles, tiles].astype(F32) + d_low[tiles, tiles].astype(F32)
        line = jnp.sum(jnp.where(eye, tile, 0.0), axis=0, keepdims=True)
        diag[:, start : start + LANES] = jnp.broadcast_to(line, (8, LANES))
    line = jnp.sum(side[:, cols : cols + LANES], axis=0, keepdims=True)
    wanted[...] = jnp.broadcast_to(line, (8, LANES))


def hop(block, here, there):
    other = [k for k in range(4) if k not in (here, there)]
    route = [(here, there), (there, here), tuple(other), tuple(other[::-1])]
    return lax.ppermute(block, "depth", route)


def taken(plane, planes, refs):
    total = jnp.zeros_like(refs[0])
    for meant, ref in zip(planes, refs):
        total = jnp.where(plane == meant, ref[...], total)
    return total


def forward_kernel(stage, d_high, d_low, c_high, c_low, source, diag, *refs):
    @pl.when(lax.axis_index("depth") == stage)
    def _():
        right_hand = source[...] - refs[0][...] if stage else source[...]
        forward = jacobi(right_hand, diag[...], d_high, d_low)
        refs[-1][...] = product(forward, c_high, c_low)


def transpose_kernel(last, high, low, high_turned, low_turned):
    @pl.when(lax.axis_index("depth") != last)
    def _():
        for ref, turned in ((high, high_turned), (low, low_turned)):
            for row in range(0, ref.shape[0], LANES):
                for col in range(0, ref.shape[1], LANES):
                    block = ref[row : row + LANES, col : col + LANES].astype(F32)
                    turned[col : col + LANES, row : row + LANES] = block.T.astype(BF16)


def turn_kernel(count, d_high, d_low, source, diag, *refs):
    right_hand = source[...] - taken(lax.axis_index("depth"), range(1, count + 1), refs[:count])
    refs[count][...] = right_hand

    @pl.when(lax.axis_index("depth") == count)
    def _():
        refs[count + 1][...] = jacobi(right_hand, diag[...], d_high, d_low)


def backward_kernel(plane, d_high, d_low, c_high, c_low, right_hand, diag, ahead, panel):
    @pl.when(lax.axis_index("depth") == plane)
    def _():
        rest = right_hand[...] - product(ahead[...], c_high, c_low)
        panel[...] = jacobi(rest, diag[...], d_high, d_low)


def last_kernel(count, d_high, d_low, c_high, c_low, right_hand, diag, wanted, *refs):
    ahead = taken(lax.axis_index("depth"), range(count - 1, -1, -1), refs[:count])
    coupled = jnp.where(lax.axis_index("depth") == count, 0.0, product(ahead, c_high, c_low))
    panel = jacobi(right_hand[...] - coupled, diag[...], d_high, d_low)
    size = panel.shape[1]
    high = panel.astype(BF16)
    rest = panel - high.astype(F32)
    middle = rest.astype(BF16)
    low = (rest - middle.astype(F32)).astype(BF16)
    line = wanted[0:1, :].astype(jnp.int32)
    chosen = (lax.broadcasted_iota(jnp.int32, (size, LANES), 0) == line).astype(BF16)
    parts = [jnp.dot(part, chosen, preferred_element_type=F32) for part in (high, middle, low)]
    picked = parts[0] + parts[1] + parts[2]
    send = refs[count]
    blocks = send.shape[0]
    own, few = size // blocks, LANES // blocks
    filler = jnp.zeros((8, LANES - own - few), F32)
    for block in range(blocks):
        send[block] = jnp.concatenate(
            [
                panel[:, block * own : (block + 1) * own],
                picked[:, block * few : (block + 1) * few],
                filler,
            ],
            1,
        )


def unpack_kernel(got, panels, picked):
    turned = got[...].T
    own = panels.shape[0]
    panels[...] = turned[:own]
    picked[...] = turned[own : own + picked.shape[0]]


def vmem(shape, dtype=F32):
    return pltpu.VMEM(shape, dtype)


def call(kernel, out_shape, *args, aliases=None, scratch=(), limit=8):
    args = [pltpu.with_memory_space_constraint(arg, pltpu.VMEM) for arg in args]
    space = pl.BlockSpec(memory_space=pltpu.VMEM)
    return pl.pallas_call(
        kernel,
        out_shape=out_shape,
        in_specs=[space] * len(args),
        out_specs=jax.tree.map(lambda _: space, out_shape),
        input_output_aliases=aliases or {},
        scratch_shapes=scratch,
        compiler_params=pltpu.CompilerParams(vmem_limit_bytes=limit * 1024 * 1024),
    )(*args)


def per_device(diag_blocks, coupling, sources, requests):
    rows, size, cols = diag_blocks.shape[1], diag_blocks.shape[2], sources.shape[2]
    few = requests.shape[1]
    width = size + cols + (SENT_GROUPS + 1) * LANES
    far = pl.BlockSpec(memory_space=pltpu.HBM)
    operands = (requests, diag_blocks[0], coupling[0], sources[0])
    packed = pl.pallas_call(
        pack_kernel,
        out_shape=vmem((rows, width)),
        in_specs=[far] * 4,
        out_specs=pl.BlockSpec(memory_space=pltpu.VMEM),
        scratch_shapes=[pltpu.SMEM(requests.shape, jnp.int32), pltpu.SemaphoreType.DMA((3 + SENT_GROUPS,))],
        compiler_params=pltpu.CompilerParams(vmem_limit_bytes=8 * 1024 * 1024),
    )(*[pltpu.with_memory_space_constraint(x, pltpu.HBM) for x in operands])
    pieces = gathered(packed)

    vec = vmem((8, size))
    mat = vmem((size, size), BF16)
    filled = call(
        early_kernel,
        (mat, mat, mat, mat, vmem((size, cols + LANES))),
        *[pieces[number] for number in EARLY],
    )
    d_high, d_low, c_high, c_low, _, source, diag, wanted = call(
        late_kernel,
        (mat, mat, mat, mat, vmem((size, cols + LANES)), vec, vec, vmem((8, LANES))),
        *[pieces[number] for number in LATE],
        *filled,
        aliases={len(LATE) + number: number for number in range(5)},
        scratch=[pltpu.VMEM((LANES, size), F32)],
    )
    mats = (d_high, d_low, c_high, c_low)

    last = 3
    lefts = []
    for k in range(last):
        carried = call(
            functools.partial(forward_kernel, k),
            vec, *mats, source, diag, *lefts[-1:],
        )
        lefts.append(hop(carried, k, k + 1))
    turned = call(functools.partial(transpose_kernel, last), (mat, mat), c_high, c_low)
    right_hand, panel = call(
        functools.partial(turn_kernel, last),
        (vec, vec), d_high, d_low, source, diag, *lefts,
    )
    aheads = []
    for k in range(last - 1, -1, -1):
        aheads.append(hop(panel, k + 1, k))
        if k > 0:
            panel = call(
                functools.partial(backward_kernel, k),
                vec, d_high, d_low, *turned, right_hand, diag, aheads[-1],
            )
    send = call(
        functools.partial(last_kernel, last),
        vmem((size // rows, 8, LANES)),
        d_high, d_low, *turned, right_hand, diag, wanted, *aheads,
    )
    got = lax.all_to_all(send, "panel", 0, 0, tiled=True).reshape(cols, LANES)
    panels, picked = call(
        unpack_kernel,
        (jax.ShapeDtypeStruct((rows, cols), F32), jax.ShapeDtypeStruct((few, cols), F32)),
        got,
    )
    return panels[None], picked[None]


def solution(mesh):
    placed = (
        P("depth", "panel", None),
        P("depth", "panel", None),
        P("depth", "panel", None),
        P("depth", "panel"),
    )
    return jax.shard_map(
        per_device,
        mesh=mesh,
        in_specs=placed,
        out_specs=(P("depth", "panel", None), P("depth", "panel", None)),
        check_vma=False,
    )
```
